32 devices in a mesh: seq: 8 (over y, x, core), heads: 4 (over z).
Axes of the slice: x: 2, y: 2, z: 4, core: 2. Of those that a mesh axis runs over, the one named last changes fastest.
Arguments:
- tokens: bfloat16 [8192, 768], P('seq'), may hold values from -6 to 6
- docs: int32 [8192], replicated, may hold values from 0 to 2, never falling along the last dimension, each value on 1 to 6144 neighbouring positions
- ln_gain: float32 [1, 2, 768], replicated, may hold values from 0.25 to 1.75
- ln_bias: float32 [1, 2, 768], replicated, may hold values from -1.75 to 1.75
- w_qkv: bfloat16 [1, 768, 3, 768], P(None, None, None, 'heads'), may hold values from -0.3125 to 0.3125
- b_qv: float32 [1, 2, 768], P(None, None, 'heads'), may hold values from -3 to 3
- w_out: bfloat16 [1, 768, 768], P(None, 'heads'), may hold values from -0.625 to 0.625
- b_out: float32 [1, 768], replicated, may hold values from -3 to 3
- w_up: bfloat16 [1, 768, 3072], P(None, None, 'heads'), may hold values from -0.21875 to 0.21875
- b_up: float32 [1, 3072], P(None, 'heads'), may hold values from -3 to 3
- w_down: bfloat16 [1, 3072, 768], P(None, 'heads'), may hold values from -0.15625 to 0.15625
- b_down: float32 [1, 768], replicated, may hold values from -3 to 3
- cotangent: bfloat16 [8192, 768], P('seq'), may hold values from -6 to 6
Outputs:
- output: bfloat16 [8192, 768], P('seq')
- grad_tokens: float32 [8192, 768], P('seq')
- grad_ln_gain: float32 [1, 2, 768], replicated
- grad_ln_bias: float32 [1, 2, 768], replicated
- grad_w_qkv: float32 [1, 768, 3, 768], P(None, None, None, 'heads')
- grad_b_qv: float32 [1, 2, 768], P(None, None, 'heads')
- grad_w_out: float32 [1, 768, 768], P(None, 'heads')
- grad_b_out: float32 [1, 768], replicated
- grad_w_up: float32 [1, 768, 3072], P(None, None, 'heads')
- grad_b_up: float32 [1, 3072], P(None, 'heads')
- grad_w_down: float32 [1, 3072, 768], P(None, 'heads')
- grad_b_down: float32 [1, 768], replicated
The draws below stay inside these ranges and needn't reach their ends.
Inputs may be any that keep to these rules, and one draw needn't show every extreme that they name: `docs`: slide ids never fall along the sequence; each of the 3 slides holds 1 to 6144 tiles, and one holds exactly 6144.
All inputs are finite; a program needn't handle non-finite values.
Results may differ from the reference program's by a relative error of at most 0.025.
Values may be sent and summed in bfloat16 or wider, within the bound.
No kernel may reach another device: no remote copies, remote signals or barrier semaphores. Data moves between devices by JAX's collectives and lax.ppermute only.
A program may use at most 192 MiB of HBM per device.

```python
import math
import jax
import jax.numpy as jnp
import numpy as np
from jax import lax

D = 768
HEADS = 16
HEAD_DIM = 48
FF = 3072
LAYERS = 1
BRANCHES = 5
DOCS = 3
TOK_DEV = 1024
TOKENS = 8192
MOST_DOC = 6144


def block_levels(rng, dims, cuts, smallest, largest):
    level = 1.0
    for dim, blocks in cuts:
        steps = jax.random.uniform(jax.random.fold_in(jax.random.fold_in(rng, 6), dim), (blocks,), jnp.float32, smallest / len(cuts), largest / len(cuts))
        level = level * jnp.repeat(jnp.exp(steps), dims[dim] // blocks).reshape((-1,) + (1,) * (len(dims) - 1 - dim))
    return level


def profile(number_of, total, most, lean):
    loads = [(1 << 20) // math.isqrt(standing ** lean) + 1 for standing in range(2, number_of + 1)]
    rest, holding = total - most - (number_of - 1), [1] * (number_of - 1)
    while rest > 0:
        candidates = [i for i in range(number_of - 1) if holding[i] < most]
        mass, left = sum([loads[i] for i in candidates]), rest
        for i in candidates:
            extra = min(most - holding[i], max(1, left * loads[i] // mass), rest)
            holding[i] = holding[i] + extra
            rest = rest - extra
    return np.array([most] + holding)


def uneven_parts(rng, amount, total, reach, skew):
    if amount == 2:
        one = jax.random.randint(rng, (), max(1, total - reach), min(reach, total - 1) + 1)
        return jnp.stack([one, total - one])
    tallies = jnp.asarray(profile(amount, total, reach, skew), jnp.int32)
    couples = (amount - 1) // 2
    source_of, sink = tallies[1:1 + 2 * couples:2], tallies[2:2 + 2 * couples:2]
    margin = jnp.minimum(source_of - 1, reach - sink)
    shifted = jax.random.randint(jax.random.fold_in(rng, 1), (couples,), 0, 1 << 20) % (margin + 1)
    tallies = tallies.at[1:1 + 2 * couples:2].set(source_of - shifted).at[2:2 + 2 * couples:2].set(sink + shifted)
    return tallies[jax.random.permutation(jax.random.fold_in(rng, 2), amount)]


def bell_draw(rng, shape, scale, reach, shards=(), kind=jnp.bfloat16):
    values = jax.random.normal(rng, shape, jnp.float32) * scale
    if len(shards) > 0:
        values = block_levels(rng, shape, shards, -0.22, 0.18) * values
    return jnp.clip(values, min=-reach, max=reach).astype(kind)


def setup_inputs(seed: int = 0) -> dict:
    seeds = jax.random.split(jax.random.key(seed), 14)
    tokens = bell_draw(seeds[0], (TOKENS, D), 1.0, 6.0, ((0, 8),))
    docs = jnp.searchsorted(jnp.cumsum(uneven_parts(seeds[1], DOCS, TOKENS, MOST_DOC, 2)), jnp.arange(TOKENS), side="right").astype(jnp.int32)
    ln_gain = jnp.clip(1.0 + 0.15 * jax.random.normal(seeds[2], (LAYERS, 2, D), jnp.float32), 0.25, 1.75)
    ln_bias = bell_draw(seeds[3], (LAYERS, 2, D), 0.3, 1.75, (), jnp.float32)
    w_qkv = bell_draw(seeds[4], (LAYERS, D, 3, D), (D // 2) ** -0.5, 0.3125, ((3, 4),))
    b_qv = bell_draw(seeds[5], (LAYERS, 2, D), 0.5, 3.0, ((2, 4),), jnp.float32)
    w_out = bell_draw(seeds[6], (LAYERS, D, D), (D // 8) ** -0.5, 0.625, ((1, 4),))
    b_out = bell_draw(seeds[7], (LAYERS, D), 0.5, 3.0, (), jnp.float32)
    w_up = bell_draw(seeds[8], (LAYERS, D, FF), D ** -0.5, 0.21875, ((2, 4),))
    b_up = bell_draw(seeds[9], (LAYERS, FF), 0.5, 3.0, ((1, 4),), jnp.float32)
    w_down = bell_draw(seeds[10], (LAYERS, FF, D), (FF // 2) ** -0.5, 0.15625, ((1, 4),))
    b_down = bell_draw(seeds[11], (LAYERS, D), 0.5, 3.0, (), jnp.float32)
    cotangent = bell_draw(seeds[12], (TOKENS, D), 1.0, 6.0, ((0, 8),))
    return {"tokens": tokens, "docs": docs, "ln_gain": ln_gain, "ln_bias": ln_bias, "w_qkv": w_qkv, "b_qv": b_qv, "w_out": w_out, "b_out": b_out, "w_up": w_up, "b_up": b_up, "w_down": w_down, "b_down": b_down, "cotangent": cotangent}


@jax.custom_vjp
def low(v):
    return lax.optimization_barrier(v.astype(jnp.bfloat16)).astype(jnp.float32)

@jax.custom_vjp
def low_back(v):
    return v

def low_keep(v):
    return (low(v), None)

def low_pass(kept, grad):
    return (grad,)

def back_keep(v):
    return (v, None)

def back_low(kept, grad):
    return (low(grad),)
low.defvjp(low_keep, low_pass)
low_back.defvjp(back_keep, back_low)
NEGATIVE = -1e+30
epsilon = 1e-05

def norm_rows(values, gain_row, shift_row):
    center = values - lax.optimization_barrier(jnp.mean(values, axis=-1, keepdims=True))
    spread = lax.optimization_barrier(jnp.mean(center * center, axis=-1, keepdims=True))
    return center * lax.rsqrt(spread + epsilon) * gain_row + shift_row

def attend_block(operands):
    queries, key_rows, value_rows, doc_rows = operands
    scores = jnp.einsum('qhe,khe->hqk', queries, key_rows, precision=lax.Precision.HIGHEST)
    scores = low_back(scores * HEAD_DIM ** (-0.5))
    allowed = doc_rows.T[:, :, None] == doc_rows.T[:, None, :]
    row_peak = lax.optimization_barrier(jnp.max(jnp.where(allowed, scores, NEGATIVE), axis=-1))
    prob_rows = jnp.where(allowed, jnp.exp(scores - row_peak[..., None]), 0.0)
    row_total = lax.optimization_barrier(jnp.sum(prob_rows, axis=-1))
    summed = low_back(jnp.einsum('hqk,khe->qhe', low(prob_rows), value_rows, precision=lax.Precision.HIGHEST))
    return (summed, row_peak.T, row_total.T)

def branch_terms(queries, key_rows, value_rows, doc_ids, segment, dilation):
    row_count, heads_all, head_width = queries.shape
    blocks = row_count // segment
    rows_block = segment // dilation
    pick_int = (jnp.arange(dilation)[:, None] == jnp.arange(heads_all)[None, :] % dilation).astype(jnp.int32)
    pick_float = pick_int.astype(jnp.float32)

    def gather_rows(values):
        shaped = values.reshape(blocks, rows_block, dilation, heads_all, head_width)
        return jnp.einsum('snrhe,rh->snhe', shaped, pick_float, precision=lax.Precision.HIGHEST)
    doc_pick = lax.optimization_barrier(jnp.sum(doc_ids.reshape(blocks, rows_block, dilation)[..., None] * pick_int[None, None], axis=2))
    summed, row_peak, row_total = lax.map(jax.checkpoint(attend_block), (gather_rows(queries), gather_rows(key_rows), gather_rows(value_rows), doc_pick))
    chosen = pick_int[None, None] > 0
    summed_full = (summed[:, :, None] * pick_float[None, None, :, :, None]).reshape(row_count, heads_all, head_width)
    peak_full = jnp.where(chosen, row_peak[:, :, None], NEGATIVE).reshape(row_count, heads_all)
    total_full = (row_total[:, :, None] * pick_float[None, None]).reshape(row_count, heads_all)
    return (summed_full, peak_full, total_full)

def layer_apply(hidden_in, doc_ids, gain_rows, shift_rows, qkv_weight, qv_bias, out_weight, out_bias, up_weight, up_bias, down_weight, down_bias):
    row_count = hidden_in.shape[0]
    normed = low(norm_rows(hidden_in, gain_rows[0], shift_rows[0]))
    projected = jnp.einsum('td,dcf->tcf', normed, qkv_weight, precision=lax.Precision.HIGHEST)
    head_shape = (row_count, HEADS, HEAD_DIM)
    queries = low(low_back(projected[:, 0] + qv_bias[0])).reshape(head_shape)
    key_rows = low(low_back(projected[:, 1])).reshape(head_shape)
    value_rows = low(low_back(projected[:, 2] + qv_bias[1])).reshape(head_shape)
    branch_parts = []
    for branch_index in range(BRANCHES):
        dilation = 2 ** branch_index
        segment = min(TOK_DEV * dilation, row_count)
        branch_parts.append(branch_terms(queries, key_rows, value_rows, doc_ids, segment, dilation))
    row_top = branch_parts[0][1]
    for part_item in branch_parts[1:]:
        row_top = jnp.maximum(row_top, part_item[1])
    factors = [jnp.exp(part_item[1] - row_top) for part_item in branch_parts]
    denominator = jnp.zeros_like(row_top)
    numerator = jnp.zeros_like(queries)
    for factor_row, part_item in zip(factors, branch_parts):
        denominator = denominator + factor_row * part_item[2]
        numerator = numerator + factor_row[..., None] * part_item[0]
    merged = numerator / denominator[..., None]
    attn_rows = low(merged.reshape(row_count, D))
    residual = hidden_in + low_back(jnp.dot(attn_rows, out_weight, precision=lax.Precision.HIGHEST)) + out_bias
    normed_two = low(norm_rows(residual, gain_rows[1], shift_rows[1]))
    pre_act = low_back(jnp.dot(normed_two, up_weight, precision=lax.Precision.HIGHEST) + up_bias)
    activated = low(jax.nn.gelu(pre_act, approximate=False))
    return residual + low_back(jnp.dot(activated, down_weight, precision=lax.Precision.HIGHEST)) + down_bias

def reference(tokens, docs, ln_gain, ln_bias, w_qkv, b_qv, w_out, b_out, w_up, b_up, w_down, b_down, cotangent):

    def stacked_model(start, gains, shifts, qkv_all, qv_all, out_all, outb_all, up_all, upb_all, down_all, downb_all):
        running = start
        for layer_index in range(LAYERS):
            running = layer_apply(running, docs, gains[layer_index], shifts[layer_index], qkv_all[layer_index], qv_all[layer_index], out_all[layer_index], outb_all[layer_index], up_all[layer_index], upb_all[layer_index], down_all[layer_index], downb_all[layer_index])
        return running
    final, pullback = jax.vjp(stacked_model, tokens.astype(jnp.float32), ln_gain.astype(jnp.float32), ln_bias.astype(jnp.float32), w_qkv.astype(jnp.float32), b_qv.astype(jnp.float32), w_out.astype(jnp.float32), b_out.astype(jnp.float32), w_up.astype(jnp.float32), b_up.astype(jnp.float32), w_down.astype(jnp.float32), b_down.astype(jnp.float32))
    grads = pullback(cotangent.astype(jnp.float32))
    return (final.astype(jnp.bfloat16), grads[0], grads[1], grads[2], grads[3], grads[4], grads[5], grads[6], grads[7], grads[8], grads[9], grads[10])
```

```python
import functools
import math

import jax
import jax.numpy as jnp
import ml_dtypes
import numpy as np
from jax import lax
from jax.experimental import pallas as pl
from jax.experimental.pallas import tpu as pltpu
from jax.sharding import PartitionSpec as P

HEAD_DIM = 48
BRANCHES = 5
DOCS = 3
TOP = BRANCHES - 1
STRIDE = 2**TOP
LANES = 128
EPSILON = 1e-05
BIG = 2.0**100
SCALE = HEAD_DIM**-0.5
LOG2E = math.log2(math.e)
LN2 = math.log(2.0)
DOC_LANE = HEAD_DIM
MULT_LANE = DOC_LANE + DOCS
LSE_LANE = MULT_LANE + 2 * TOP
VALUE_LANE = LANES // 2
ONE_LANE = VALUE_LANE + HEAD_DIM
F32 = jnp.float32
BF16 = jnp.bfloat16
VMEM_LIMIT = 48 * 1024 * 1024


def bit_reversed(block):
    return sum(((block >> bit) & 1) << (TOP - 1 - bit) for bit in range(TOP))


def level_columns(rows):
    table = np.zeros((rows, LANES), np.float32)
    for level in range(1, TOP + 1):
        table[: rows >> level, MULT_LANE + level - 1] = 1.0
        table[: rows >> level, MULT_LANE + TOP + level - 1] = 1.0
    return table.astype(ml_dtypes.bfloat16)


def count_columns(rows, groups):
    table = np.zeros((groups, rows, LANES), np.float32)
    for group in range(groups):
        for level in range(group + 1, TOP + 1):
            step = math.log2((level - group + 1) / (level - group))
            high = float(np.float32(step).astype(ml_dtypes.bfloat16))
            table[group, : rows >> level, MULT_LANE + level - 1] = high
            table[group, : rows >> level, MULT_LANE + TOP + level - 1] = step - high
    return table.astype(ml_dtypes.bfloat16)


def spread_table(heads, first_lane):
    table = np.zeros((heads * HEAD_DIM, heads * LANES), np.float32)
    for head in range(heads):
        for item in range(HEAD_DIM):
            table[head * HEAD_DIM + item, head * LANES + first_lane + item] = 1.0
    return table.astype(ml_dtypes.bfloat16)


def dot_nn(left, right):
    return jnp.dot(left, right, preferred_element_type=F32)


def dot_nt(left, right):
    return lax.dot_general(left, right, (((1,), (1,)), ((), ())), preferred_element_type=F32)


def dot_tn(left, right):
    return lax.dot_general(left, right, (((0,), (0,)), ((), ())), preferred_element_type=F32)


def norm_rows(values, gain_row, shift_row):
    center = values - jnp.mean(values, axis=-1, keepdims=True)
    spread = jnp.mean(center * center, axis=-1, keepdims=True)
    return center * lax.rsqrt(spread + EPSILON) * gain_row + shift_row


def norm_back(values, gain_row, grad_rows):
    center = values - jnp.mean(values, axis=-1, keepdims=True)
    spread = jnp.mean(center * center, axis=-1, keepdims=True)
    inverse = lax.rsqrt(spread + EPSILON)
    unit = center * inverse
    scaled = grad_rows * gain_row
    grad_in = inverse * (
        scaled
        - jnp.mean(scaled, axis=-1, keepdims=True)
        - unit * jnp.mean(scaled * unit, axis=-1, keepdims=True)
    )
    return grad_in, jnp.sum(grad_rows * unit, axis=0), jnp.sum(grad_rows, axis=0)


def full_spec(shape):
    return pl.BlockSpec(shape, lambda *_: (0,) * len(shape))


def head_spec(rows):
    return pl.BlockSpec((1, rows, LANES), lambda head, *_: (head, 0, 0))


SMALL_SPEC = pl.BlockSpec(memory_space=pltpu.SMEM)


def project_kernel(
    first_ref, x_ref, gain_ref, shift_ref, w_ref, bias_ref, fq_ref, fkv_ref, level_ref, spread_k_ref, spread_v_ref,
    normed_ref, q_ref, kv_ref, q_rows, kv_rows,
):
    step = pl.program_id(0)
    tile = x_ref.shape[0]
    heads, rows = q_ref.shape[0], q_ref.shape[1]
    block = rows // STRIDE
    normed = norm_rows(x_ref[...].astype(F32), gain_ref[...], shift_ref[...]).astype(BF16)
    normed_ref[...] = normed
    query = ((dot_nn(normed, w_ref[0]) + bias_ref[0:1]) * (SCALE * LOG2E)).astype(BF16)
    key = dot_nn(normed, w_ref[1]).astype(BF16)
    value = (dot_nn(normed, w_ref[2]) + bias_ref[1:2]).astype(BF16)
    query_wide = dot_nn(query, spread_k_ref[...])
    pair_wide = dot_nn(key, spread_k_ref[...]) + dot_nn(value, spread_v_ref[...])
    here = pl.ds(pl.multiple_of(step * tile, tile), tile)
    for head in range(heads):
        lanes = slice(head * LANES, (head + 1) * LANES)
        q_rows[head, here, :] = query_wide[:, lanes] + fq_ref[...]
        kv_rows[head, here, :] = pair_wide[:, lanes] + fkv_ref[...]

    @pl.when(step == pl.num_programs(0) - 1)
    def _():
        for head in range(heads):
            turn = (first_ref[0] + head) & (STRIDE - 1)
            for item in range(STRIDE):
                start = bit_reversed(item) ^ turn
                there = slice(item * block, (item + 1) * block)
                q_ref[head, there, :] = q_rows[head, pl.ds(start, block, stride=STRIDE), :].astype(BF16)
                kv_ref[head, there, :] = (
                    kv_rows[head, pl.ds(start, block, stride=STRIDE), :] + level_ref[there, :].astype(F32)
                ).astype(BF16)


def project(first, tokens, gain, shift, weights, bias, fq, fkv):
    rows, width = tokens.shape
    feats = weights.shape[2]
    heads = feats // HEAD_DIM
    tile = min(rows, 256)
    row_spec = pl.BlockSpec((tile, width), lambda i: (i, 0))
    lane_spec = pl.BlockSpec((tile, LANES), lambda i: (i, 0))
    shape = (heads, rows, LANES)
    return pl.pallas_call(
        project_kernel,
        grid=(rows // tile,),
        in_specs=[
            SMALL_SPEC, row_spec, full_spec((1, width)), full_spec((1, width)), full_spec(weights.shape),
            full_spec(bias.shape), lane_spec, lane_spec, full_spec((rows, LANES)),
            full_spec((feats, heads * LANES)), full_spec((feats, heads * LANES)),
        ],
        out_specs=[row_spec, full_spec(shape), full_spec(shape)],
        out_shape=[
            jax.ShapeDtypeStruct((rows, width), BF16),
            jax.ShapeDtypeStruct(shape, BF16),
            jax.ShapeDtypeStruct(shape, BF16),
        ],
        scratch_shapes=[pltpu.VMEM(shape, F32), pltpu.VMEM(shape, F32)],
        compiler_params=pltpu.CompilerParams(vmem_limit_bytes=VMEM_LIMIT),
        name="project",
    )(
        first, tokens, gain, shift, weights, bias, fq, fkv, level_columns(rows),
        spread_table(heads, 0), spread_table(heads, VALUE_LANE),
    )


def group_of(distance):
    return distance.bit_length()


def row_tiles(rows, smallest):
    edges = [0, smallest] if smallest < 128 else [0]
    while edges[-1] < rows:
        edges.append(min(rows, edges[-1] - edges[-1] % 128 + 128))
    return list(zip(edges[:-1], edges[1:]))


def attend_kernel(distances, first_ref, q_ref, kv_ref, count_ref, gather_ref, *refs):
    far_refs = refs[: len(distances)]
    out_ref, joined_ref, placed = refs[len(distances) :]
    head = pl.program_id(0)
    rows = q_ref.shape[1]
    block = rows // STRIDE
    turn = (first_ref[0] + head) & (STRIDE - 1)
    smallest = min([rows] + [ref.shape[1] for ref in far_refs])
    for low, high in row_tiles(rows, smallest):
        query = q_ref[0, low:high, :]
        pieces = [(kv_ref, 0)] + [
            (ref, group_of(distance)) for distance, ref in zip(distances, far_refs) if low < ref.shape[1]
        ]
        scores = [dot_nt(query + count_ref[group, low:high, :], ref[0]) for ref, group in pieces]
        peak = functools.reduce(jnp.maximum, [jnp.max(item, axis=-1, keepdims=True) for item in scores])
        total = functools.reduce(
            jnp.add,
            [dot_nn(jnp.exp2(item - peak).astype(BF16), ref[0]) for item, (ref, _) in zip(scores, pieces)],
        )
        mass = total[:, ONE_LANE : ONE_LANE + 1]
        result = total * (1.0 / mass)
        lane = lax.broadcasted_iota(jnp.int32, result.shape, 1)
        out_ref[0, low:high, :] = jnp.where(lane == 0, peak + jnp.log2(mass), result)
        for offset in range(low, high, block):
            start = bit_reversed(offset // block) ^ turn
            placed[head, pl.ds(start, block, stride=STRIDE), :] = result[offset - low : offset - low + block]

    @pl.when(head == pl.num_programs(0) - 1)
    def _():
        joined_ref[...] = functools.reduce(
            jnp.add,
            [
                dot_nn(placed[item].astype(BF16), gather_ref[item * LANES : (item + 1) * LANES])
                for item in range(placed.shape[0])
            ],
        ).astype(BF16)


def attend(first, queries, pairs, far, distances, counts):
    heads, rows, _ = queries.shape
    feats = heads * HEAD_DIM
    gather = spread_table(heads, VALUE_LANE).T.copy()
    return pl.pallas_call(
        functools.partial(attend_kernel, distances),
        grid=(heads,),
        in_specs=[SMALL_SPEC, head_spec(rows), head_spec(rows), full_spec(counts.shape), full_spec(gather.shape)]
        + [head_spec(item.shape[1]) for item in far],
        out_specs=[head_spec(rows), full_spec((rows, feats))],
        out_shape=[
            jax.ShapeDtypeStruct((heads, rows, LANES), F32),
            jax.ShapeDtypeStruct((rows, feats), BF16),
        ],
        scratch_shapes=[pltpu.VMEM((heads, rows, LANES), F32)],
        compiler_params=pltpu.CompilerParams(vmem_limit_bytes=VMEM_LIMIT),
        name="attend",
    )(first, queries, pairs, counts, gather, *far)


def three_parts(values):
    high = values.astype(BF16).astype(F32)
    middle = (values - high).astype(BF16).astype(F32)
    return high, middle, values - high - middle


def attend_back_kernel(distances, first_ref, grad_ref, spread_ref, q_ref, kv_ref, out_ref, count_ref, *refs):
    far_refs = refs[: len(distances)]
    dq_ref, dkv_ref = refs[len(distances) : len(distances) + 2]
    dfar_refs = refs[len(distances) + 2 : 2 * len(distances) + 2]
    wide, query, grad = refs[2 * len(distances) + 2 :]
    head = pl.program_id(0)
    rows = q_ref.shape[1]
    block = rows // STRIDE
    turn = (first_ref[0] + head) & (STRIDE - 1)

    @pl.when(head == 0)
    def _():
        for item in range(wide.shape[0]):
            wide[item] = dot_nn(grad_ref[...], spread_ref[:, item * LANES : (item + 1) * LANES])

    for item in range(STRIDE):
        there = slice(item * block, (item + 1) * block)
        start = bit_reversed(item) ^ turn
        rows_grad = wide[head, pl.ds(start, block, stride=STRIDE), :]
        rows_out = out_ref[0, there, :]
        lane = lax.broadcasted_iota(jnp.int32, rows_grad.shape, 1)
        rows_query = q_ref[0, there, :].astype(F32)
        parts = three_parts(jnp.sum(rows_grad * rows_out, axis=-1, keepdims=True))
        for index, part in enumerate(parts):
            rows_grad = jnp.where(lane == ONE_LANE + index, -part, rows_grad)
        for index, part in enumerate(three_parts(rows_out[:, 0:1])):
            rows_query = jnp.where(lane == LSE_LANE + index, -part, rows_query)
        grad[there, :] = rows_grad.astype(BF16)
        query[there, :] = rows_query.astype(BF16)

    def one(keys, last, group, dq_first):
        counted = query[:last, :] + count_ref[group, :last, :]
        prob = jnp.exp2(dot_nt(keys, counted))
        slope = (prob * dot_nt(keys, grad[:last, :])).astype(BF16)
        dkv = dot_nn(prob.astype(BF16), grad[:last, :]) + dot_nn(slope, query[:last, :])
        dq = dot_tn(slope, keys)
        if dq_first:
            dq_ref[0, :last, :] = dq
        else:
            dq_ref[0, :last, :] += dq
        return dkv

    tile = min(rows, 256)
    for low in range(0, rows, tile):
        dkv_ref[0, low : low + tile, :] = one(kv_ref[0, low : low + tile, :], rows, 0, low == 0)
    for distance, ref, dref in zip(distances, far_refs, dfar_refs):
        count = ref.shape[1]
        step = min(count, tile)
        for low in range(0, count, step):
            dref[0, low : low + step, :] = one(
                ref[0, low : low + step, :], count, group_of(distance), False
            ).astype(BF16)


def attend_back(first, grads, queries, pairs, outs, far, distances, counts):
    heads, rows, _ = queries.shape
    feats = heads * HEAD_DIM
    spread = spread_table(heads, VALUE_LANE)
    return pl.pallas_call(
        functools.partial(attend_back_kernel, distances),
        grid=(heads,),
        in_specs=[
            SMALL_SPEC, full_spec((rows, feats)), full_spec(spread.shape), head_spec(rows), head_spec(rows),
            head_spec(rows), full_spec(counts.shape),
        ]
        + [head_spec(item.shape[1]) for item in far],
        out_specs=[head_spec(rows), head_spec(rows)] + [head_spec(item.shape[1]) for item in far],
        out_shape=[
            jax.ShapeDtypeStruct((heads, rows, LANES), F32),
            jax.ShapeDtypeStruct((heads, rows, LANES), F32),
        ]
        + [jax.ShapeDtypeStruct(item.shape, BF16) for item in far],
        scratch_shapes=[
            pltpu.VMEM((heads, rows, LANES), F32),
            pltpu.VMEM((rows, LANES), BF16),
            pltpu.VMEM((rows, LANES), BF16),
        ],
        compiler_params=pltpu.CompilerParams(vmem_limit_bytes=VMEM_LIMIT),
        name="attend_back",
    )(first, grads, spread, queries, pairs, outs, counts, *far)


def collect_kernel(count, first_ref, dq_ref, dkv_ref, gather_k_ref, gather_v_ref, *refs):
    far_refs = refs[:count]
    outs = refs[count : count + 3]
    q_rows, kv_rows = refs[count + 3 :]
    head = pl.program_id(0)
    rows = dq_ref.shape[1]
    block = rows // STRIDE
    turn = (first_ref[0] + head) & (STRIDE - 1)
    for item in range(STRIDE):
        there = slice(item * block, (item + 1) * block)
        start = bit_reversed(item) ^ turn
        pair = dkv_ref[0, there, :]
        for ref in far_refs:
            if item * block < ref.shape[1]:
                pair = pair + ref[0, there, :].astype(F32)
        lane = lax.broadcasted_iota(jnp.int32, pair.shape, 1)
        q_rows[head, pl.ds(start, block, stride=STRIDE), :] = dq_ref[0, there, :] * SCALE
        kv_rows[head, pl.ds(start, block, stride=STRIDE), :] = jnp.where(lane < VALUE_LANE, pair * LN2, pair)

    @pl.when(head == pl.num_programs(0) - 1)
    def _():
        total = [None] * 3
        for item in range(q_rows.shape[0]):
            lanes = slice(item * LANES, (item + 1) * LANES)
            query = q_rows[item].astype(BF16)
            pair = kv_rows[item].astype(BF16)
            terms = (
                dot_nn(query, gather_k_ref[lanes]),
                dot_nn(pair, gather_k_ref[lanes]),
                dot_nn(pair, gather_v_ref[lanes]),
            )
            total = [term if old is None else old + term for old, term in zip(total, terms)]
        for ref, value in zip(outs, total):
            ref[...] = value.astype(BF16)


def collect(first, dq, dkv, far):
    heads, rows, _ = dq.shape
    feats = heads * HEAD_DIM
    gather_k = spread_table(heads, 0).T.copy()
    gather_v = spread_table(heads, VALUE_LANE).T.copy()
    return pl.pallas_call(
        functools.partial(collect_kernel, len(far)),
        grid=(heads,),
        in_specs=[SMALL_SPEC, head_spec(rows), head_spec(rows), full_spec(gather_k.shape), full_spec(gather_v.shape)]
        + [head_spec(item.shape[1]) for item in far],
        out_specs=[full_spec((rows, feats))] * 3,
        out_shape=[jax.ShapeDtypeStruct((rows, feats), BF16)] * 3,
        scratch_shapes=[pltpu.VMEM((heads, rows, LANES), F32), pltpu.VMEM((heads, rows, LANES), F32)],
        compiler_params=pltpu.CompilerParams(vmem_limit_bytes=VMEM_LIMIT),
        name="collect",
    )(first, dq, dkv, gather_k, gather_v, *far)


def flipped(array, distance):
    return lax.ppermute(array, "seq", [(i, i ^ distance) for i in range(lax.axis_size("seq"))])


def shards(tokens, docs, ln_gain, ln_bias, w_qkv, b_qv, w_out, b_out, w_up, b_up, w_down, b_down, cotangent):
    rows, width = tokens.shape
    feats = w_qkv.shape[3]
    heads = feats // HEAD_DIM
    seq_count = lax.axis_size("seq")
    head_count = lax.axis_size("heads")
    seq_pos = lax.axis_index("seq")
    head_pos = lax.axis_index("heads")
    first = (head_pos * heads).astype(jnp.int32).reshape(1)
    gains, shifts = ln_gain[0], ln_bias[0]
    part = rows // head_count

    own_docs = lax.dynamic_slice_in_dim(docs, seq_pos * rows, rows)
    lane = jnp.arange(LANES)[None, :]
    same = own_docs[:, None] == lane - DOC_LANE
    doc_lanes = (lane >= DOC_LANE) & (lane < DOC_LANE + DOCS)
    one_lanes = ((lane >= LSE_LANE) & (lane < LSE_LANE + 3)) | ((lane >= ONE_LANE) & (lane < ONE_LANE + 3))
    query_extra = (same & doc_lanes).astype(F32)
    pair_extra = jnp.where(doc_lanes & ~same, -BIG, one_lanes.astype(F32))

    w_three = jnp.transpose(w_qkv[0], (1, 0, 2))
    normed, queries, pairs = project(
        first, tokens, gains[0:1], shifts[0:1], w_three, b_qv[0], query_extra, pair_extra
    )
    distances = tuple(range(1, min(seq_count, STRIDE)))
    counts = jnp.asarray(count_columns(rows, max([0] + [group_of(item) for item in distances]) + 1))
    far = [flipped(pairs[:, : rows >> group_of(item)], item) for item in distances]
    outs, attn_part = attend(first, queries, pairs, far, distances, counts)

    w_out_all = lax.all_gather(w_out[0], "heads", axis=0, tiled=True)
    attn_all = lax.all_gather(attn_part, "heads", axis=1, tiled=True)
    current = tokens.astype(F32)
    resid = current + dot_nn(attn_all, w_out_all) + b_out[0]
    normed_two = norm_rows(resid, gains[1], shifts[1]).astype(BF16)
    pre = dot_nn(normed_two, w_up[0]) + b_up[0]
    share = 0.5 * (1.0 + lax.erf(pre * math.sqrt(0.5)))
    hidden = (pre * share).astype(BF16)
    slope = share + pre * jnp.exp(-0.5 * pre * pre) * (1.0 / math.sqrt(2.0 * math.pi))
    grad_pre = (dot_nt(cotangent, w_down[0]) * slope).astype(BF16)

    grad_two_part = lax.psum_scatter(
        dot_nt(grad_pre, w_up[0]).astype(BF16), "heads", scatter_dimension=0, tiled=True
    ).astype(F32)
    here = head_pos * part
    resid_part = lax.dynamic_slice_in_dim(resid, here, part)
    grad_out_part = lax.dynamic_slice_in_dim(cotangent, here, part).astype(F32)
    tokens_part = lax.dynamic_slice_in_dim(tokens, here, part).astype(F32)
    grad_resid_n, gain_two, shift_two = norm_back(resid_part, gains[1], grad_two_part)
    grad_resid = grad_out_part + grad_resid_n
    grad_resid_b = grad_resid.astype(BF16)
    grad_attn_part = dot_nt(grad_resid_b, w_out_all).astype(BF16)
    grad_attn = lax.all_to_all(
        grad_attn_part.reshape(part, head_count, feats), "heads", split_axis=1, concat_axis=0, tiled=True
    ).reshape(rows, feats)
    returned = attend_back(first, grad_attn, queries, pairs, outs, far, distances, counts)
    back = [flipped(item, distance) for item, distance in zip(returned[2:], distances)]
    grads_three = collect(first, returned[0], returned[1], back)

    out_sum = lax.psum_scatter(
        dot_nn(hidden, w_down[0]).astype(BF16), "heads", scatter_dimension=0, tiled=True
    ).astype(F32)
    out_part = (resid_part + out_sum + b_down[0]).astype(BF16)
    output = lax.all_gather(out_part, "heads", axis=0, tiled=True)

    grad_resid_all = lax.all_gather(grad_resid_b, "heads", axis=0, tiled=True)
    grad_w_out = dot_tn(attn_part, grad_resid_all)
    grad_w_up = dot_tn(normed_two, grad_pre)
    grad_w_down = dot_tn(hidden, cotangent)
    grad_w_qkv = jnp.stack([dot_tn(normed, item) for item in grads_three], axis=1)

    grad_one = functools.reduce(jnp.add, [dot_nt(item, w_three[index]) for index, item in enumerate(grads_three)])
    grad_one_part = lax.psum_scatter(grad_one.astype(BF16), "heads", scatter_dimension=0, tiled=True).astype(F32)
    grad_in_n, gain_one, shift_one = norm_back(tokens_part, gains[0], grad_one_part)
    grad_tokens = lax.all_gather((grad_resid + grad_in_n).astype(BF16), "heads", axis=0, tiled=True).astype(F32)

    wide_sums = lax.psum(
        jnp.stack(
            [gain_one, gain_two, shift_one, shift_two, jnp.sum(grad_resid, axis=0), jnp.sum(grad_out_part, axis=0)]
        ),
        ("seq", "heads"),
    )
    bias_sums = lax.psum(
        (
            jnp.stack([jnp.sum(item.astype(F32), axis=0) for item in (grads_three[0], grads_three[2])]),
            jnp.sum(grad_pre.astype(F32), axis=0),
        ),
        "seq",
    )
    weight_sums = lax.psum(
        tuple(item.astype(BF16) for item in (grad_w_up, grad_w_down, grad_w_out, grad_w_qkv)), "seq"
    )
    grad_w_up, grad_w_down, grad_w_out, grad_w_qkv = (item.astype(F32)[None] for item in weight_sums)
    return (
        output, grad_tokens, wide_sums[None, 0:2], wide_sums[None, 2:4], grad_w_qkv, bias_sums[0][None],
        grad_w_out, wide_sums[4:5], grad_w_up, bias_sums[1][None], grad_w_down, wide_sums[5:6],
    )


def solution(mesh):
    in_specs = (
        P("seq", None), P(), P(), P(), P(None, None, None, "heads"), P(None, None, "heads"),
        P(None, "heads", None), P(), P(None, None, "heads"), P(None, "heads"), P(None, "heads", None), P(),
        P("seq", None),
    )
    out_specs = (
        P("seq", None), P("seq", None), P(), P(), P(None, None, None, "heads"), P(None, None, "heads"),
        P(None, "heads", None), P(), P(None, None, "heads"), P(None, "heads"), P(None, "heads", None), P(),
    )
    return jax.shard_map(shards, mesh=mesh, in_specs=in_specs, out_specs=out_specs, check_vma=False)
```

```python
import functools
import math

import jax
import jax.numpy as jnp
import ml_dtypes
import numpy as np
from jax import lax
from jax.experimental import pallas as pl
from jax.experimental.pallas import tpu as pltpu
from jax.sharding import PartitionSpec as P

HEAD_DIM = 48
BRANCHES = 5
DOCS = 3
TOP = BRANCHES - 1
STRIDE = 2**TOP
LANES = 128
EPSILON = 1e-05
BIG = 2.0**100
SCALE = HEAD_DIM**-0.5
LOG2E = math.log2(math.e)
LN2 = math.log(2.0)
DOC_LANE = HEAD_DIM
MULT_LANE = DOC_LANE + DOCS
LSE_LANE = MULT_LANE + 2 * TOP
VALUE_LANE = LANES // 2
ONE_LANE = VALUE_LANE + HEAD_DIM
F32 = jnp.float32
BF16 = jnp.bfloat16
VMEM_LIMIT = 32 * 1024 * 1024
HEADS_PLACE = DOCS
SEQ_PLACE = DOCS + 1
PART_PLACE = DOCS + 2


def call(kernel, out_shape, **options):
    inner = pl.pallas_call(
        kernel,
        out_shape=jax.tree.map(lambda item: pltpu.HBM(item.shape, item.dtype), out_shape),
        compiler_params=pltpu.CompilerParams(vmem_limit_bytes=VMEM_LIMIT),
        **options,
    )

    def run(*arrays, loose=()):
        return inner(
            *[
                item if item.ndim == 1 else pltpu.with_memory_space_constraint(jnp.asarray(item), pltpu.HBM)
                for item in arrays
            ],
            *loose,
        )

    return run


def bit_reversed(block):
    return sum(((block >> bit) & 1) << (TOP - 1 - bit) for bit in range(TOP))


def level_columns(rows):
    table = np.zeros((rows, LANES), np.float32)
    for level in range(1, TOP + 1):
        table[: rows >> level, MULT_LANE + level - 1] = 1.0
        table[: rows >> level, MULT_LANE + TOP + level - 1] = 1.0
    return table.astype(ml_dtypes.bfloat16)


def count_columns(rows, groups):
    table = np.zeros((groups, rows, LANES), np.float32)
    for group in range(groups):
        for level in range(group + 1, TOP + 1):
            step = math.log2((level - group + 1) / (level - group))
            high = float(np.float32(step).astype(ml_dtypes.bfloat16))
            table[group, : rows >> level, MULT_LANE + level - 1] = high
            table[group, : rows >> level, MULT_LANE + TOP + level - 1] = step - high
    return table.astype(ml_dtypes.bfloat16)


def spread_table(heads, first_lane):
    table = np.zeros((heads * HEAD_DIM, heads * LANES), np.float32)
    for head in range(heads):
        for item in range(HEAD_DIM):
            table[head * HEAD_DIM + item, head * LANES + first_lane + item] = 1.0
    return table.astype(ml_dtypes.bfloat16)


def dot_nn(left, right):
    return jnp.dot(left, right, preferred_element_type=F32)


def dot_nt(left, right):
    return lax.dot_general(left, right, (((1,), (1,)), ((), ())), preferred_element_type=F32)


def dot_tn(left, right):
    return lax.dot_general(left, right, (((0,), (0,)), ((), ())), preferred_element_type=F32)


def norm_rows(values, gain_row, shift_row):
    center = values - jnp.mean(values, axis=-1, keepdims=True)
    spread = jnp.mean(center * center, axis=-1, keepdims=True)
    return center * lax.rsqrt(spread + EPSILON) * gain_row + shift_row


def norm_back(values, gain_row, grad_rows):
    center = values - jnp.mean(values, axis=-1, keepdims=True)
    spread = jnp.mean(center * center, axis=-1, keepdims=True)
    inverse = lax.rsqrt(spread + EPSILON)
    unit = center * inverse
    scaled = grad_rows * gain_row
    grad_in = inverse * (
        scaled
        - jnp.mean(scaled, axis=-1, keepdims=True)
        - unit * jnp.mean(scaled * unit, axis=-1, keepdims=True)
    )
    return grad_in, jnp.sum(grad_rows * unit, axis=0, keepdims=True), jnp.sum(grad_rows, axis=0, keepdims=True)


def full_spec(shape):
    return pl.BlockSpec(shape, lambda *_: (0,) * len(shape))


def head_spec(rows):
    return pl.BlockSpec((1, rows, LANES), lambda head, *_: (head, 0, 0))


SMALL_SPEC = pl.BlockSpec(memory_space=pltpu.SMEM)


def project_kernel(
    first_ref, x_ref, gain_ref, shift_ref, w_ref, bias_ref, level_ref, spread_k_ref, spread_v_ref,
    normed_ref, q_ref, kv_ref, *refs,
):
    *message_refs, q_rows, kv_rows = refs
    step = pl.program_id(0)
    tile = x_ref.shape[0]
    heads, rows = q_ref.shape[0], q_ref.shape[1]
    block = rows // STRIDE
    normed = norm_rows(x_ref[...].astype(F32), gain_ref[...], shift_ref[...]).astype(BF16)
    normed_ref[...] = normed
    query = ((dot_nn(normed, w_ref[0]) + bias_ref[0:1]) * (SCALE * LOG2E)).astype(BF16)
    key = dot_nn(normed, w_ref[1]).astype(BF16)
    value = (dot_nn(normed, w_ref[2]) + bias_ref[1:2]).astype(BF16)
    query_wide = dot_nn(query, spread_k_ref[...])
    pair_wide = dot_nn(key, spread_k_ref[...]) + dot_nn(value, spread_v_ref[...])
    here = pl.ds(pl.multiple_of(step * tile, tile), tile)
    row = lax.broadcasted_iota(jnp.int32, (tile, LANES), 0) + step * tile
    lane = lax.broadcasted_iota(jnp.int32, (tile, LANES), 1)
    doc_lane = functools.reduce(
        jnp.add, [(row >= first_ref[1 + item]).astype(jnp.int32) for item in range(DOCS - 1)], DOC_LANE
    )
    query_extra = (lane == doc_lane).astype(F32)
    other = (lane >= DOC_LANE) & (lane < DOC_LANE + DOCS) & (lane != doc_lane)
    ones = ((lane >= LSE_LANE) & (lane < LSE_LANE + 3)) | ((lane >= ONE_LANE) & (lane < ONE_LANE + 3))
    pair_extra = jnp.where(other, -BIG, ones.astype(F32))
    for head in range(heads):
        lanes = slice(head * LANES, (head + 1) * LANES)
        q_rows[head, here, :] = query_wide[:, lanes] + query_extra
        kv_rows[head, here, :] = pair_wide[:, lanes] + pair_extra

    @pl.when(step == pl.num_programs(0) - 1)
    def _():
        for head in range(heads):
            turn = (first_ref[0] + head) & (STRIDE - 1)
            for item in range(STRIDE):
                start = bit_reversed(item) ^ turn
                there = slice(item * block, (item + 1) * block)
                q_ref[head, there, :] = q_rows[head, pl.ds(start, block, stride=STRIDE), :].astype(BF16)
                pair = (kv_rows[head, pl.ds(start, block, stride=STRIDE), :] + level_ref[there, :].astype(F32)).astype(BF16)
                kv_ref[head, there, :] = pair
                for ref in message_refs:
                    if item * block < ref.shape[1]:
                        ref[head, there, :] = pair


def project(first, tokens, gain, shift, weights, bias, bits):
    rows, width = tokens.shape
    feats = weights.shape[2]
    heads = feats // HEAD_DIM
    tile = min(rows, 256)
    row_spec = pl.BlockSpec((tile, width), lambda i: (i, 0))
    shape = (heads, rows, LANES)
    messages = [(heads, rows >> (bit + 1), LANES) for bit in range(bits)]
    return call(
        project_kernel,
        grid=(rows // tile,),
        in_specs=[
            SMALL_SPEC, row_spec, full_spec((1, width)), full_spec((1, width)), full_spec(weights.shape),
            full_spec(bias.shape), full_spec((rows, LANES)),
            full_spec((feats, heads * LANES)), full_spec((feats, heads * LANES)),
        ],
        out_specs=[row_spec] + [full_spec(item) for item in (shape, shape, *messages)],
        out_shape=[
            jax.ShapeDtypeStruct((rows, width), BF16),
        ]
        + [jax.ShapeDtypeStruct(item, BF16) for item in (shape, shape, *messages)],
        scratch_shapes=[pltpu.VMEM(shape, F32), pltpu.VMEM(shape, F32)],
        name="project",
    )(
        first, tokens, gain, shift, weights, bias, level_columns(rows),
        spread_table(heads, 0), spread_table(heads, VALUE_LANE),
    )


def group_of(distance):
    return distance.bit_length()


def message_layout(rows, bits):
    direct = [1] + list(range(2, 1 << bits, 2)) if bits else []
    layout = [((item, 0, rows >> group_of(item)),) for item in direct]
    passed, offset = [], 0
    for item in direct[1:]:
        passed.append((item + 1, offset, rows >> group_of(item)))
        offset += rows >> group_of(item)
    return tuple(layout + [tuple(passed)]) if passed else tuple(layout)


def far_pieces(layout, refs):
    return [(ref, *entry) for ref, entries in zip(refs, layout) for entry in entries]


def row_tiles(rows, smallest):
    edges = [0, smallest] if smallest < 128 else [0]
    while edges[-1] < rows:
        edges.append(min(rows, edges[-1] - edges[-1] % 128 + 128))
    return list(zip(edges[:-1], edges[1:]))


def attend_own_kernel(q_ref, kv_ref, count_ref, out_ref):
    rows = q_ref.shape[1]
    tile = min(rows, 128)
    for low in range(0, rows, tile):
        there = slice(low, low + tile)
        scores = dot_nt(q_ref[0, there, :] + count_ref[0, there, :], kv_ref[0])
        peak = jnp.max(scores, axis=-1, keepdims=True)
        total = dot_nn(jnp.exp2(scores - peak).astype(BF16), kv_ref[0])
        lane = lax.broadcasted_iota(jnp.int32, total.shape, 1)
        out_ref[0, there, :] = jnp.where(lane == 0, peak, total)


def attend_own(queries, pairs, counts):
    heads, rows, _ = queries.shape
    return call(
        attend_own_kernel,
        grid=(heads,),
        in_specs=[head_spec(rows), head_spec(rows), full_spec(counts.shape)],
        out_specs=head_spec(rows),
        out_shape=jax.ShapeDtypeStruct((heads, rows, LANES), F32),
        name="attend_own",
    )(queries, pairs, counts)


def attend_far_kernel(layout, first_ref, q_ref, own_ref, count_ref, gather_ref, *refs):
    pieces_all = far_pieces(layout, refs[: len(layout)])
    out_ref, mine_ref, theirs_ref, placed = refs[len(layout) :]
    head = pl.program_id(0)
    rows = q_ref.shape[1]
    block = rows // STRIDE
    turn = (first_ref[0] + head) & (STRIDE - 1)
    smallest = min([rows] + [item[3] for item in pieces_all])
    for low, high in row_tiles(rows, smallest):
        query = q_ref[0, low:high, :]
        total = own_ref[0, low:high, :]
        peak = total[:, 0:1]
        keys = []
        scores = []
        for ref, distance, offset, count in pieces_all:
            if low < count:
                keys.append(ref[0, offset : offset + count, :])
                scores.append(dot_nt(query + count_ref[group_of(distance), low:high, :], keys[-1]))
        if scores:
            own_peak = peak
            peak = functools.reduce(
                jnp.maximum, [own_peak] + [jnp.max(item, axis=-1, keepdims=True) for item in scores]
            )
            total = functools.reduce(
                jnp.add,
                [total * jnp.exp2(own_peak - peak)]
                + [dot_nn(jnp.exp2(item - peak).astype(BF16), key) for item, key in zip(scores, keys)],
            )
        mass = total[:, ONE_LANE : ONE_LANE + 1]
        result = total * (1.0 / mass)
        lane = lax.broadcasted_iota(jnp.int32, result.shape, 1)
        out_ref[0, low:high, :] = jnp.where(lane == 0, peak + jnp.log2(mass), result)
        for offset in range(low, high, block):
            start = bit_reversed(offset // block) ^ turn
            placed[head, pl.ds(start, block, stride=STRIDE), :] = result[offset - low : offset - low + block]

    @pl.when(head == pl.num_programs(0) - 1)
    def _():
        half = rows // 2
        for side, ref in enumerate((mine_ref, theirs_ref)):
            here = pl.ds(pl.multiple_of(((first_ref[HEADS_PLACE] & 1) ^ side) * half, half), half)
            ref[...] = functools.reduce(
                jnp.add,
                [
                    dot_nn(placed[item, here, :].astype(BF16), gather_ref[item * LANES : (item + 1) * LANES])
                    for item in range(placed.shape[0])
                ],
            ).astype(BF16)


def attend_far(first, queries, own, far, layout, counts):
    heads, rows, _ = queries.shape
    feats = heads * HEAD_DIM
    gather = spread_table(heads, VALUE_LANE).T.copy()
    return call(
        functools.partial(attend_far_kernel, layout),
        grid=(heads,),
        in_specs=[SMALL_SPEC, head_spec(rows), head_spec(rows), full_spec(counts.shape), full_spec(gather.shape)]
        + [head_spec(item.shape[1]) for item in far],
        out_specs=[head_spec(rows), full_spec((rows // 2, feats)), full_spec((rows // 2, feats))],
        out_shape=[
            jax.ShapeDtypeStruct((heads, rows, LANES), F32),
            jax.ShapeDtypeStruct((rows // 2, feats), BF16),
            jax.ShapeDtypeStruct((rows // 2, feats), BF16),
        ],
        scratch_shapes=[pltpu.VMEM((heads, rows, LANES), F32)],
        name="attend_far",
    )(first, queries, own, counts, gather, loose=far)


def three_parts(values):
    high = values.astype(BF16).astype(F32)
    middle = (values - high).astype(BF16).astype(F32)
    return high, middle, values - high - middle


def pair_grads(keys, query, counted, grad):
    prob = jnp.exp2(dot_nt(keys, counted))
    slope = (prob * dot_nt(keys, grad)).astype(BF16)
    return dot_nn(prob.astype(BF16), grad) + dot_nn(slope, query), dot_tn(slope, keys)


def back_far_kernel(layout, pieces, place_ref, q_ref, out_ref, count_ref, spread_ref, *refs):
    grad_refs = refs[:pieces]
    far = far_pieces(layout, refs[pieces : pieces + len(layout)])
    query, grad, dq_ref = refs[pieces + len(layout) : pieces + len(layout) + 3]
    rows_half = q_ref.shape[1] // 2
    *message_refs, wide = refs[pieces + len(layout) + 3 :]
    targets = []
    for index, entries in enumerate(layout):
        passed = index == len(message_refs)
        for _, offset, _ in entries:
            targets.append((message_refs[0], rows_half + offset) if passed else (message_refs[index], 0))
    head = pl.program_id(0)
    rows = q_ref.shape[1]
    block = rows // STRIDE
    part = grad_refs[0].shape[0]
    turn = (place_ref[0] + head) & (STRIDE - 1)

    @pl.when(head == 0)
    def _():
        for index, ref in enumerate(grad_refs):
            start = pl.multiple_of(place_ref[PART_PLACE + index], part)
            for item in range(wide.shape[0]):
                wide[item, pl.ds(start, part), :] = dot_nn(ref[...], spread_ref[:, item * LANES : (item + 1) * LANES])

    for item in range(STRIDE):
        there = slice(item * block, (item + 1) * block)
        start = bit_reversed(item) ^ turn
        rows_grad = wide[head, pl.ds(start, block, stride=STRIDE), :]
        rows_out = out_ref[0, there, :]
        lane = lax.broadcasted_iota(jnp.int32, rows_grad.shape, 1)
        rows_query = q_ref[0, there, :].astype(F32)
        parts = three_parts(jnp.sum(rows_grad * rows_out, axis=-1, keepdims=True))
        for index, value in enumerate(parts):
            rows_grad = jnp.where(lane == ONE_LANE + index, -value, rows_grad)
        for index, value in enumerate(three_parts(rows_out[:, 0:1])):
            rows_query = jnp.where(lane == LSE_LANE + index, -value, rows_query)
        grad[0, there, :] = rows_grad.astype(BF16)
        query[0, there, :] = rows_query.astype(BF16)

    dq_ref[...] = jnp.zeros_like(dq_ref)
    for (ref, distance, offset, count), (dref, doffset) in zip(far, targets):
        counted = query[0, :count, :] + count_ref[group_of(distance), :count, :]
        step = min(count, 256)
        for low in range(offset, offset + count, step):
            dkv, dq = pair_grads(ref[0, low : low + step, :], query[0, :count, :], counted, grad[0, :count, :])
            there = slice(doffset + low - offset, doffset + low - offset + step)
            dref[0, there, :] = dkv.astype(BF16)
            dq_ref[0, :count, :] += dq


def back_far(places, grads, queries, outs, far, layout, counts):
    heads, rows, _ = queries.shape
    spread = spread_table(heads, VALUE_LANE)
    limit = rows // 2 if layout else rows // STRIDE
    messages = [sum(item[2] for item in entries) for entries in layout]
    if len(messages) > 1:
        messages = [messages[0] + messages[-1]] + messages[1:-1]
    messages = [(heads, count, LANES) for count in messages]
    return call(
        functools.partial(back_far_kernel, layout, len(grads)),
        grid=(heads,),
        in_specs=[SMALL_SPEC, head_spec(rows), head_spec(rows), full_spec(counts.shape), full_spec(spread.shape)]
        + [full_spec(item.shape) for item in grads]
        + [head_spec(item.shape[1]) for item in far],
        out_specs=[head_spec(rows), head_spec(rows), head_spec(limit)] + [head_spec(item[1]) for item in messages],
        out_shape=[
            jax.ShapeDtypeStruct((heads, rows, LANES), BF16),
            jax.ShapeDtypeStruct((heads, rows, LANES), BF16),
            jax.ShapeDtypeStruct((heads, limit, LANES), F32),
        ]
        + [jax.ShapeDtypeStruct(item, BF16) for item in messages],
        scratch_shapes=[pltpu.VMEM((heads, rows, LANES), F32)],
        name="back_far",
    )(places, queries, outs, counts, spread, loose=(*grads, *far))


def back_own_kernel(query, grad, kv_ref, count_ref, dq_far_ref, dq_ref, dkv_ref):
    rows = kv_ref.shape[1]
    limit = dq_far_ref.shape[1]
    counted = query[0] + count_ref[0]
    tile = min(rows, 256)
    for low in range(0, rows, tile):
        there = slice(low, low + tile)
        dkv, dq = pair_grads(kv_ref[0, there, :], query[0], counted, grad[0])
        dkv_ref[0, there, :] = dkv
        if low == 0:
            dq_ref[0] = dq
        else:
            dq_ref[0] += dq
    dq_ref[0, :limit, :] += dq_far_ref[0]


def back_own(queries, grads, pairs, counts, dq_far):
    heads, rows, _ = queries.shape
    return call(
        back_own_kernel,
        grid=(heads,),
        in_specs=[head_spec(rows)] * 3 + [full_spec(counts.shape), head_spec(dq_far.shape[1])],
        out_specs=[head_spec(rows)] * 2,
        out_shape=[jax.ShapeDtypeStruct((heads, rows, LANES), F32)] * 2,
        name="back_own",
    )(queries, grads, pairs, counts, dq_far)


def collect_kernel(count, peers, first_ref, dq_ref, dkv_ref, gather_k_ref, gather_v_ref, w_ref, *refs):
    far_refs = refs[:count]
    three_refs = refs[count : count + 3]
    term_ref = refs[count + 3]
    q_rows, kv_rows = refs[-2:]
    head = pl.program_id(0)
    rows = dq_ref.shape[1]
    part = rows // peers
    block = rows // STRIDE
    turn = (first_ref[0] + head) & (STRIDE - 1)
    for item in range(STRIDE):
        there = slice(item * block, (item + 1) * block)
        start = bit_reversed(item) ^ turn
        pair = dkv_ref[0, there, :]
        for ref in far_refs:
            if item * block < ref.shape[1]:
                pair = pair + ref[0, there, :].astype(F32)
        lane = lax.broadcasted_iota(jnp.int32, pair.shape, 1)
        q_rows[head, pl.ds(start, block, stride=STRIDE), :] = dq_ref[0, there, :] * SCALE
        kv_rows[head, pl.ds(start, block, stride=STRIDE), :] = jnp.where(lane < VALUE_LANE, pair * LN2, pair)

    @pl.when(head == pl.num_programs(0) - 1)
    def _():
        total = [None] * 3
        for item in range(q_rows.shape[0]):
            lanes = slice(item * LANES, (item + 1) * LANES)
            query = q_rows[item].astype(BF16)
            pair = kv_rows[item].astype(BF16)
            terms = (
                dot_nn(query, gather_k_ref[lanes]),
                dot_nn(pair, gather_k_ref[lanes]),
                dot_nn(pair, gather_v_ref[lanes]),
            )
            total = [term if old is None else old + term for old, term in zip(total, terms)]
        for ref, value in zip(three_refs, total):
            ref[...] = value.astype(BF16)
        for peer in range(peers):
            start = (peer & 1) * (rows // 2) + (peer >> 1) * part
            here = slice(start, start + part)
            term_ref[peer * part : (peer + 1) * part, :] = functools.reduce(
                jnp.add, [dot_nt(ref[here, :], w_ref[item]) for item, ref in enumerate(three_refs)]
            ).astype(BF16)


def collect(places, dq, dkv, far, weights, peers):
    heads, rows, _ = dq.shape
    width, feats = weights.shape[1:]
    gather_k = spread_table(heads, 0).T.copy()
    gather_v = spread_table(heads, VALUE_LANE).T.copy()
    return call(
        functools.partial(collect_kernel, len(far), peers),
        grid=(heads,),
        in_specs=[
            SMALL_SPEC, head_spec(rows), head_spec(rows), full_spec(gather_k.shape), full_spec(gather_v.shape),
            full_spec(weights.shape),
        ]
        + [head_spec(item.shape[1]) for item in far],
        out_specs=[full_spec((rows, feats))] * 3 + [full_spec((rows, width))],
        out_shape=[jax.ShapeDtypeStruct((rows, feats), BF16)] * 3
        + [jax.ShapeDtypeStruct((rows, width), BF16)],
        scratch_shapes=[pltpu.VMEM((heads, rows, LANES), F32), pltpu.VMEM((heads, rows, LANES), F32)],
        name="collect",
    )(places, dq, dkv, gather_k, gather_v, weights, loose=far)


def pick(core, low, high):
    return jnp.where(core == 0, low, high), jnp.where(core == 0, high, low)


def halves(array):
    half = array.shape[-1] // 2
    return array[:, :half], array[:, half:]


FETCHED = 2
BIAS_ROWS = 16


def fetched_weights(refs, up_shape, down_shape):
    sides = []
    for ref in refs:
        count = up_shape[0] // 2
        down = ref[count : 2 * count].reshape(down_shape[0] // 2, down_shape[1])
        bias = ref[2 * count : 2 * count + 1].astype(F32)
        for index in (1, 2):
            bias = bias + ref[2 * count + index : 2 * count + index + 1].astype(F32)
        sides.append((ref.at[:count], down, bias))
    return sides


def feed_kernel(
    place_ref, tok_ref, cot_ref, w_out_ref, b_out_ref, gain_ref, shift_ref, up_ref, down_ref, bias_ref, *refs,
):
    fetched, refs = refs[:FETCHED], refs[FETCHED:]
    (up_one, down_one, bias_other), (up_two, down_two, _) = fetched_weights(fetched, up_ref.shape, down_ref.shape)
    attn_refs = refs[:-10]
    resid_ref, normed_ref, cot_out_ref, h0_ref, h1_ref, p0_ref, p1_ref, da_ref, out_ref, sums_ref = refs[-10:]
    feats = attn_refs[0].shape[1]
    core = place_ref[SEQ_PLACE] & 1
    resid = tok_ref[...].astype(F32) + b_out_ref[...]
    for index, ref in enumerate(attn_refs):
        here = pl.ds(pl.multiple_of((place_ref[HEADS_PLACE] ^ index) * feats, feats), feats)
        resid = resid + dot_nn(ref[...], w_out_ref[here, :])
    resid_ref[0] = resid
    normed = norm_rows(resid, gain_ref[...], shift_ref[...]).astype(BF16)
    normed_ref[0] = normed
    cot = cot_ref[...]
    cot_out_ref[0] = cot
    normed_pair = pick(core, *halves(normed))
    pres = (
        dot_nn(normed, up_ref[...]) + bias_ref[...],
        dot_nn(normed_pair[0], up_one[...]) + dot_nn(normed_pair[1], up_two[...]) + bias_other,
    )
    acts = (
        dot_nt(cot, down_ref[...]),
        jnp.concatenate(pick(core, dot_nt(cot, down_one[...]), dot_nt(cot, down_two[...])), axis=1),
    )
    grads = []
    for pre, act, h_ref, p_ref in zip(pres, acts, (h0_ref, h1_ref), (p0_ref, p1_ref)):
        share = 0.5 * (1.0 + lax.erf(pre * math.sqrt(0.5)))
        h_ref[0] = (pre * share).astype(BF16)
        slope = share + pre * jnp.exp(-0.5 * pre * pre) * (1.0 / math.sqrt(2.0 * math.pi))
        grads.append((act * slope).astype(BF16))
        p_ref[0] = grads[-1]
    other = pick(core, dot_nt(grads[1], up_one[...]), dot_nt(grads[1], up_two[...]))
    da_ref[0] = (dot_nt(grads[0], up_ref[...]) + jnp.concatenate(other, axis=1)).astype(da_ref.dtype)
    hidden_pair = pick(core, *halves(h1_ref[0]))
    out_ref[0] = (
        dot_nn(h0_ref[0], down_ref[...])
        + dot_nn(hidden_pair[0], down_one[...])
        + dot_nn(hidden_pair[1], down_two[...])
    ).astype(out_ref.dtype)
    ones = jnp.ones((8, cot.shape[0]), BF16)
    sums_ref[0, 0] = dot_nn(ones, grads[0])
    sums_ref[0, 1] = dot_nn(ones, grads[1])


def feed(places, part, steps, kind, tokens, cotangent, w_out, b_out, gain, shift, up, down, bias, fetched, attns):
    rows, width = tokens.shape
    hidden = up.shape[1]
    feats = attns[0].shape[1]
    inner = attns[0].shape[0] // part
    first = steps[0]

    def piece(i, place):
        return (place[HEADS_PLACE] >> 1) ^ (i + first)

    def row_block(i, place):
        return ((place[HEADS_PLACE] & 1) * inner + piece(i, place), 0)

    def whole(array):
        return pl.BlockSpec(array.shape, lambda i, place: (0,) * array.ndim, pipeline_mode=pl.Buffered(1))

    def stacked(columns):
        return pl.BlockSpec((1, part, columns), lambda i, place: (i, 0, 0))

    constants = (w_out, b_out, gain, shift, up, down, bias)
    outs = [(width, F32), (width, BF16), (width, BF16)] + [(hidden, BF16)] * 4 + [(width, kind)] * 2
    count = len(steps)
    return call(
        feed_kernel,
        grid_spec=pltpu.PrefetchScalarGridSpec(
            num_scalar_prefetch=1,
            grid=(count,),
            in_specs=[pl.BlockSpec((part, width), row_block)] * 2
            + [whole(item) for item in (*constants, *fetched)]
            + [pl.BlockSpec((part, feats), lambda i, place: (piece(i, place), 0))] * len(attns),
            out_specs=[stacked(columns) for columns, _ in outs]
            + [pl.BlockSpec((1, 2, 8, hidden), lambda i, place: (i, 0, 0, 0))],
        ),
        out_shape=[jax.ShapeDtypeStruct((count, part, columns), dtype) for columns, dtype in outs]
        + [jax.ShapeDtypeStruct((count, 2, 8, hidden), F32)],
        name="feed",
    )(places, tokens, cotangent, *constants, loose=(*fetched, *attns))


def outer_kernel(pairs, place_ref, *refs):
    ins, (keep_ref, give_ref) = refs[:-2], refs[-2:]
    step = pl.program_id(0)
    core = place_ref[SEQ_PLACE] & 1
    for index in range(pairs):

        @pl.when(step == index)
        def _():
            total = None
            for left_ref, right_ref in zip(ins[4 * index : 4 * index + 2], ins[4 * index + 2 : 4 * index + 4]):
                for item in range(left_ref.shape[0]):
                    left = pick(core, *halves(left_ref[item]))
                    terms = [dot_tn(side, right_ref[item]) for side in left]
                    total = terms if total is None else [old + term for old, term in zip(total, terms)]
            keep_ref[0] = total[0].astype(BF16)
            give_ref[0] = total[1].astype(BF16)


def outer_sums(places, pairs):
    lefts = pairs[0][0][0].shape[2] // 2
    rights = pairs[0][1][0].shape[2]
    arrays = [item for pair in pairs for side in pair for item in side]
    spec = pl.BlockSpec((1, lefts, rights), lambda i: (i, 0, 0))
    shape = jax.ShapeDtypeStruct((len(pairs), lefts, rights), BF16)
    return call(
        functools.partial(outer_kernel, len(pairs)),
        grid=(len(pairs),),
        in_specs=[SMALL_SPEC] + [full_spec(item.shape) for item in arrays],
        out_specs=[spec, spec],
        out_shape=[shape, shape],
        name="outer_sums",
    )(places, *arrays)


def out_grads_kernel(place_ref, low_ref, *refs):
    *attn_refs, keep_ref, give_ref = refs
    half = attn_refs[0].shape[1] // 2
    core = place_ref[SEQ_PLACE] & 1
    for index, ref in enumerate(attn_refs):
        product = dot_tn(ref[...], low_ref[...])
        keep, give = pick(core, product[:half], product[half:])
        keep_ref[index] = keep.astype(BF16)
        give_ref[index] = give.astype(BF16)


def out_grads(places, low, attns):
    part, width = low.shape
    feats = attns[0].shape[1]
    shape = (len(attns), feats // 2, width)
    return call(
        out_grads_kernel,
        grid_spec=pltpu.PrefetchScalarGridSpec(
            num_scalar_prefetch=1,
            grid=(1,),
            in_specs=[full_spec((part, width))]
            + [pl.BlockSpec((part, feats), lambda i, place: (place[HEADS_PLACE] >> 1, 0))] * len(attns),
            out_specs=[full_spec(shape)] * 2,
        ),
        out_shape=[jax.ShapeDtypeStruct(shape, BF16)] * 2,
        name="out_grads",
    )(places, low, loose=attns)


def tail_kernel(normed_ref, tok_ref, w_ref, _, stats_ref, up_ref, *refs):
    *three_refs, out_ref, sums_ref = refs
    rows, width = normed_ref.shape
    feats = three_refs[0].shape[1]
    hidden = up_ref.shape[1]
    for index, ref in enumerate(three_refs):
        out_ref[index * feats : (index + 1) * feats, :] = dot_tn(ref[...], normed_ref[...]).astype(BF16)
    gain = jnp.zeros((1, width), F32)
    shift = jnp.zeros((1, width), F32)
    tile = min(rows, 256)
    for low in range(0, rows, tile):
        here = slice(low, low + tile)
        term = functools.reduce(
            jnp.add, [dot_nt(ref[here, :], w_ref[index]) for index, ref in enumerate(three_refs)]
        )
        center = tok_ref[here, :].astype(F32)
        center = center - jnp.mean(center, axis=-1, keepdims=True)
        unit = center * lax.rsqrt(jnp.mean(center * center, axis=-1, keepdims=True) + EPSILON)
        gain = gain + column_sums(term * unit)
        shift = shift + column_sums(term)
    row = lax.broadcasted_iota(jnp.int32, (SUM_ROWS, width), 0)
    other = up_ref[1:2, :]
    if hidden < width:
        other = jnp.concatenate([other, jnp.zeros((1, width - hidden), F32)], axis=1)
    lines = (gain, stats_ref[0:1], shift, stats_ref[1:2], stats_ref[2:3], stats_ref[3:4], other)
    block = jnp.zeros((SUM_ROWS, width), F32)
    for index, line in enumerate(lines):
        block = jnp.where(row == index, line, block)
    sums_ref[:SUM_ROWS, :] = block.astype(BF16)
    sums_ref[SUM_ROWS:, :] = jnp.zeros((3 * SUM_ROWS, width), BF16)
    ones = jnp.ones((SUM_ROWS, rows), BF16)
    own = jnp.broadcast_to(up_ref[0:1, :], (SUM_ROWS, hidden))
    for index, value in enumerate((own, dot_nn(ones, three_refs[0][...]), dot_nn(ones, three_refs[2][...]))):
        here = (index + 1) * SUM_ROWS
        sums_ref[here : here + SUM_ROWS, : value.shape[1]] = value.astype(BF16)


SUM_ROWS = 16


def tail_grads(normed, tokens, weights, earlier, stats, ups, three):
    rows, width = normed.shape
    feats = three[0].shape[1]
    ins = (normed, tokens, weights, stats, ups, *three)
    specs = [full_spec(item.shape) for item in ins]
    ins = (*ins[:3], earlier, *ins[3:])
    return call(
        tail_kernel,
        grid=(1,),
        in_specs=[*specs[:3], pl.BlockSpec(memory_space=pl.ANY), *specs[3:]],
        out_specs=[full_spec((3 * feats, width)), full_spec((4 * SUM_ROWS, width))],
        out_shape=[jax.ShapeDtypeStruct((count, width), BF16) for count in (3 * feats, 4 * SUM_ROWS)],
        name="tail_grads",
    )(*ins)


def pack_kernel(core_ref, up_ref, down_ref, bias_ref, out_ref):
    count = up_ref.shape[0] // 2
    here = pl.ds(pl.multiple_of(core_ref[0] * count, count), count)
    out_ref[:count, :] = up_ref[here, :]
    out_ref[count : 2 * count, :] = down_ref[here, :]
    row = lax.broadcasted_iota(jnp.int32, (BIAS_ROWS, bias_ref.shape[1]), 0)
    block = jnp.zeros(row.shape, F32)
    for index, line in enumerate(three_parts(bias_ref[...])):
        block = jnp.where(row == index, line, block)
    out_ref[2 * count :, :] = block.astype(BF16)


def pack_weights(core, up, down, bias):
    hidden = up.shape[1]
    shape = (up.shape[0] + BIAS_ROWS, hidden)
    if up.shape != down.shape:
        cuts = [
            lax.dynamic_slice_in_dim(item, core * (item.shape[0] // 2), item.shape[0] // 2).reshape(-1, hidden)
            for item in (up, down)
        ]
        zeros = jnp.zeros((BIAS_ROWS - 3, hidden), F32)
        return jnp.concatenate([*cuts, jnp.concatenate([*three_parts(bias), zeros]).astype(BF16)])
    return call(
        pack_kernel,
        grid=(1,),
        in_specs=[SMALL_SPEC] + [full_spec(item.shape) for item in (up, down, bias)],
        out_specs=full_spec(shape),
        out_shape=jax.ShapeDtypeStruct(shape, BF16),
        name="pack_weights",
    )(core.reshape(1), up, down, bias)


def column_sums(array):
    return jnp.sum(array, axis=0, keepdims=True)


def turn_kernel(received, place_ref, resid_ref, cot_ref, gain_ref, da_ref, w_out_ref, *refs):
    more_refs = refs[:received]
    dres_ref, low_ref, stats_ref, *grad_refs = refs[received:]
    feats = grad_refs[0].shape[1]
    total = da_ref[0]
    for ref in more_refs:
        total = total + ref[...].reshape(total.shape).astype(F32)
    cot = cot_ref[0].astype(F32)
    grad_n, gain_sum, shift_sum = norm_back(resid_ref[0], gain_ref[...], total)
    dres = cot + grad_n
    dres_ref[...] = dres
    low = dres.astype(BF16)
    low_ref[...] = low
    for index, ref in enumerate(grad_refs):
        here = pl.ds(pl.multiple_of((place_ref[HEADS_PLACE] ^ index) * feats, feats), feats)
        ref[...] = dot_nt(low, w_out_ref[here, :]).astype(BF16)
    stats_ref[0:1] = gain_sum
    stats_ref[1:2] = shift_sum
    stats_ref[2:3] = column_sums(dres)
    stats_ref[3:4] = column_sums(cot)
    stats_ref[4:8] = jnp.zeros_like(stats_ref[4:8])


def turn_back(places, resid, cot, gain, da, more, w_out, peers):
    _, part, width = resid.shape
    feats = width // peers
    ins = (resid, cot, gain, da, w_out)
    return call(
        functools.partial(turn_kernel, len(more)),
        grid=(1,),
        in_specs=[SMALL_SPEC] + [full_spec(item.shape) for item in (*ins, *more)],
        out_specs=[full_spec((part, width)), full_spec((part, width)), full_spec((8, width))]
        + [full_spec((part, feats))] * peers,
        out_shape=[
            jax.ShapeDtypeStruct((part, width), F32),
            jax.ShapeDtypeStruct((part, width), BF16),
            jax.ShapeDtypeStruct((8, width), F32),
        ]
        + [jax.ShapeDtypeStruct((part, feats), BF16)] * peers,
        name="turn_back",
    )(places, *ins, loose=more)


def finish_kernel(place_ref, tok_ref, gain_ref, term_ref, dres_ref, grad_ref):
    grad_n, _, _ = norm_back(tok_ref[...].astype(F32), gain_ref[...], term_ref[...].astype(F32))
    grad_ref[...] = (dres_ref[...] + grad_n).astype(BF16)


def finish(places, tokens, gain, term, dres):
    part, width = term.shape
    return call(
        finish_kernel,
        grid_spec=pltpu.PrefetchScalarGridSpec(
            num_scalar_prefetch=1,
            grid=(1,),
            in_specs=[pl.BlockSpec((part, width), lambda i, place: (place[PART_PLACE] // part, 0))]
            + [full_spec(item.shape) for item in (gain, term, dres)],
            out_specs=full_spec((part, width)),
        ),
        out_shape=jax.ShapeDtypeStruct((part, width), BF16),
        name="finish",
    )(places, tokens, gain, term, dres)


def flipped(array, distance):
    return lax.ppermute(array, "seq", [(i, i ^ distance) for i in range(lax.axis_size("seq"))])


def crossed(array, distance):
    if distance == 0:
        return array
    return lax.ppermute(array, "heads", [(i, i ^ distance) for i in range(lax.axis_size("heads"))])


def added(left, right):
    return (left.astype(F32) + right.astype(F32)).astype(BF16)


def halved(array, axis, bit, earlier=None):
    side = (lax.axis_index("seq") >> bit) & 1
    count = array.shape[axis] // 2
    keep = lax.dynamic_slice_in_dim(array, side * count, count, axis)
    give = lax.dynamic_slice_in_dim(array, (1 - side) * count, count, axis)
    if earlier is not None:
        give, earlier = lax.optimization_barrier((give, earlier))
    other = flipped(give, 1 << bit)
    return added(keep, other), other, earlier


def doubled(array, axis, bit):
    side = (lax.axis_index("seq") >> bit) & 1
    other = flipped(array, 1 << bit)
    whole = jnp.where(side == 0, jnp.concatenate([array, other], axis), jnp.concatenate([other, array], axis))
    return whole, other


def after(value, earlier):
    return lax.optimization_barrier((value, earlier))[0]


def shards(tokens, docs, ln_gain, ln_bias, w_qkv, b_qv, w_out, b_out, w_up, b_up, w_down, b_down, cotangent):
    rows, width = tokens.shape
    feats = w_qkv.shape[3]
    heads = feats // HEAD_DIM
    seq_count = lax.axis_size("seq")
    head_count = lax.axis_size("heads")
    seq_pos = lax.axis_index("seq")
    head_pos = lax.axis_index("heads")
    seq_bits = seq_count.bit_length() - 1
    gains, shifts = ln_gain[0], ln_bias[0]
    half = rows // 2
    part = rows // head_count
    peers = [head_pos ^ distance for distance in range(head_count)]
    part_starts = [(peer & 1) * half + (peer >> 1) * part for peer in peers]
    edges = [jnp.sum((docs <= item).astype(jnp.int32)) - seq_pos * rows for item in range(DOCS - 1)]
    places = jnp.stack(
        [item.astype(jnp.int32) for item in (head_pos * heads, *edges, head_pos, seq_pos, *part_starts)]
    )

    core = seq_pos & 1
    hidden = w_up.shape[2]
    w_out_all = lax.all_gather(w_out[0], "heads", axis=0, tiled=True)
    fetched_one = crossed(pack_weights(core.astype(jnp.int32), w_up[0], w_down[0], b_up), 1)

    w_three = jnp.transpose(w_qkv[0], (1, 0, 2))
    bits = min(seq_bits, TOP)
    normed, queries, pairs, *messages = project(places, tokens, gains[0:1], shifts[0:1], w_three, b_qv[0], bits)
    layout = message_layout(rows, bits)
    counts = jnp.asarray(count_columns(rows, bits + 1))
    direct = layout[:-1] if bits > 1 else layout
    far = [flipped(messages[group_of(entries[0][0]) - 1], entries[0][0]) for entries in direct]
    own_outs = attend_own(queries, pairs, counts)
    if bits > 1:
        far.append(flipped(after(jnp.concatenate(far[1:], axis=1), own_outs), 1))
    outs, attn_mine, attn_theirs = attend_far(places, queries, own_outs, far, layout, counts)
    fetched = [fetched_one, flipped(after(fetched_one, outs), 1)]
    attns = [attn_mine] + [
        crossed(attn_theirs if distance & 1 else attn_mine, distance) for distance in range(1, head_count)
    ]

    def in_rows(array):
        return jnp.transpose(array.reshape(steps, 2, part, width), (1, 0, 2, 3)).reshape(rows, width)

    steps = head_count // 2
    shared = (
        tokens, cotangent, w_out_all, b_out, gains[1:2], shifts[1:2], w_up[0], w_down[0], b_up, fetched, attns,
    )
    sent = feed(places, part, range(1, steps), BF16, *shared) if steps > 1 else None
    da_more = [crossed(sent[7][step - 1], 2 * step) for step in range(1, steps)]
    own = feed(places, part, range(0, 1), F32, *shared)
    if sent is None:
        sent = [item[:0] for item in own]
    resid, normed_two, cots, h0, h1, p0, p1, da_two, out_term, up_sums = zip(own, sent)

    dres, dres_low, stats_two, *grad_attns = turn_back(
        places, resid[0], cots[0], gains[1:2], da_two[0], da_more, w_out_all, head_count
    )
    grad_attns = [crossed(item, distance) for distance, item in enumerate(grad_attns)]
    later = after(places, dres)
    out_keep, out_give = out_grads(later, dres_low, attns)
    later = after(later, out_keep)
    out_other = flipped(out_give, 1)
    out_grad = added(out_keep, out_other)
    products = [(normed_two, p0), (h0, cots), (normed_two, p1), (h1, cots)]
    if hidden == width:
        packs = [outer_sums(later, products)]
    else:
        packs = [outer_sums(later, products[0::2]), outer_sums(later, products[1::2])]
    packs = after(packs, grad_attns)
    arrived = [flipped(give, 1) for _, give in packs]
    packs = [added(keep, item) for (keep, _), item in zip(packs, arrived)]

    out_terms = after(out_term[1], grad_attns)
    out_more = [crossed(out_terms[step - 1], 2 * step) for step in range(1, steps)]
    queries_b, grads_b, dq_far, *dfar = back_far(
        after(places, (*arrived, out_other)), grad_attns, queries, outs, far, layout, counts
    )
    back, arrived = [], dq_far
    if bits:
        arrived = flipped(after(dfar[0], out_more), 1)
        offset = rows // 2
        onward = []
        for item in dfar[1:]:
            count = item.shape[1]
            onward.append(added(item, arrived[:, offset : offset + count]))
            offset += count
        queries_b = after(queries_b, onward)
        back = [arrived[:, : rows // 2]] + [
            flipped(item, entries[0][0]) for entries, item in zip(direct[1:], onward)
        ]
    out_sum = functools.reduce(jnp.add, [item.astype(F32) for item in after(out_more, arrived)], out_term[0][0])
    out_part = (resid[0][0] + out_sum + b_down[0]).astype(BF16)
    distance = head_count // 2
    out_far = crossed(after(out_grad, out_part)[distance:], distance)
    queries_b, out_part = lax.optimization_barrier((queries_b, out_part))
    gathered = lax.all_gather(out_part, "heads", axis=0)
    output = in_rows(gathered)
    arrived = places
    if seq_bits > 1:
        packs, arrived, _ = zip(*[halved(item, 1, 1) for item in packs])
    dq, dkv = back_own(queries_b, grads_b, pairs, counts, dq_far)
    ups = (up_sums[0][:, :, 0], up_sums[1][:, :, 0])
    ups = jnp.sum(ups[0], axis=0) + jnp.sum(ups[1], axis=0)
    later = after(places, (*arrived, ups, out_far))
    others = ()
    for bit in range(2, seq_bits):
        cuts = []
        for item in packs:
            item, other, later = halved(item, 1, bit, later)
            cuts.append(item)
            others += (other,)
        packs = cuts
    *grads_three, terms = collect(later, dq, dkv, back, w_three, head_count)
    term = lax.psum_scatter(terms, "heads", scatter_dimension=0, tiled=True)
    arrived = (terms, *others)
    out_grad = added(out_grad[:distance], after(out_far, arrived))
    while distance > 1:
        distance = distance // 2
        out_grad = added(out_grad[:distance], crossed(out_grad[distance:], distance))
    grad_w_out = out_grad[0]

    rest, sums = tail_grads(after(normed, arrived), tokens, w_three, gathered, stats_two, ups, grads_three)
    packs = [
        added(item[: item.shape[0] // 2], crossed(item[item.shape[0] // 2 :], 1)) for item in packs
    ]
    count = rest.shape[0] // 2
    keep, give = (lax.dynamic_slice_in_dim(rest, side * count, count) for side in (core, 1 - core))
    rest = added(jnp.concatenate([keep, sums]), flipped(jnp.concatenate([give, sums]), 1))
    rest = jnp.concatenate([rest, grad_w_out])
    arrived = ()
    for bit in range(1, min(seq_bits, 2)):
        arrived += (flipped(rest, 1 << bit),)
        rest = added(rest, arrived[-1])
    for bit in reversed(range(2, seq_bits)):
        packs, others = zip(*[doubled(item, 1, bit) for item in packs])
        arrived += others
    grad_part = finish(after(places, arrived), tokens, gains[0:1], term, dres)
    grad_tokens = in_rows(lax.all_gather(grad_part, "heads", axis=0)).astype(F32)
    packs, rest = after((packs, rest), grad_part)
    for bit in range(2, seq_bits):
        rest = added(rest, flipped(rest, 1 << bit))
    for bit in reversed(range(min(seq_bits, 2))):
        packs, _ = zip(*[doubled(item, 1, bit) for item in packs])
    sums = rest[count : count + 4 * SUM_ROWS]
    rest = jnp.concatenate([rest[:count], rest[count + 4 * SUM_ROWS :]])
    rest = doubled(rest, 0, 0)[0].astype(F32).reshape(2, -1, width)
    grad_w_out = rest[:, count:].reshape(feats, width)
    rest = rest[:, :count]
    more = [crossed(sums[:SUM_ROWS], distance).astype(F32) for distance in range(1, head_count)]
    sums = sums.astype(F32)
    wide = functools.reduce(jnp.add, more, sums[:SUM_ROWS])[:6]
    grad_b_up = sums[SUM_ROWS, :hidden] + more[0][6, :hidden]
    grad_b_qv = jnp.stack([sums[(index + 2) * SUM_ROWS, :feats] for index in range(2)])
    packs = [packs[0][0], packs[0][1]] if hidden == width else [packs[0][0], packs[1][0]]
    grad_w_up, grad_w_down = (item.astype(F32) for item in packs)
    grad_w_qkv = jnp.transpose(rest.reshape(3, feats, width), (2, 0, 1))
    return (
        output, grad_tokens, wide[None, 0:2], wide[None, 2:4], grad_w_qkv[None], grad_b_qv[None],
        grad_w_out[None], wide[4:5], grad_w_up[None], grad_b_up[None], grad_w_down[None], wide[5:6],
    )


def solution(mesh):
    in_specs = (
        P("seq", None), P(), P(), P(), P(None, None, None, "heads"), P(None, None, "heads"),
        P(None, "heads", None), P(), P(None, None, "heads"), P(None, "heads"), P(None, "heads", None), P(),
        P("seq", None),
    )
    out_specs = (
        P("seq", None), P("seq", None), P(), P(), P(None, None, None, "heads"), P(None, None, "heads"),
        P(None, "heads", None), P(), P(None, None, "heads"), P(None, "heads"), P(None, "heads", None), P(),
    )
    return jax.shard_map(shards, mesh=mesh, in_specs=in_specs, out_specs=out_specs, check_vma=False)
```

```python
import functools
import math

import jax
import jax.numpy as jnp
import ml_dtypes
import numpy as np
from jax import lax
from jax.experimental import pallas as pl
from jax.experimental.pallas import tpu as pltpu
from jax.sharding import PartitionSpec as P

HEAD_DIM = 48
BRANCHES = 5
DOCS = 3
TOP = BRANCHES - 1
STRIDE = 2**TOP
LANES = 128
EPSILON = 1e-05
BIG = 2.0**100
SCALE = HEAD_DIM**-0.5
LOG2E = math.log2(math.e)
LN2 = math.log(2.0)
DOC_LANE = HEAD_DIM
MULT_LANE = DOC_LANE + DOCS
LSE_LANE = MULT_LANE + 2 * TOP
VALUE_LANE = LANES // 2
ONE_LANE = VALUE_LANE + HEAD_DIM
F32 = jnp.float32
BF16 = jnp.bfloat16
VMEM_LIMIT = 28 * 1024 * 1024
HEADS_PLACE = DOCS
SEQ_PLACE = DOCS + 1
PART_PLACE = DOCS + 2


class View:
    def __init__(self, shape, index=None, near=False, loose=False):
        self.shape, self.index, self.near, self.loose = tuple(shape), index, near, loose

    def of(self, ref, step, place):
        if not self.near or self.index is None:
            return ref
        cuts = []
        for size, at, whole in zip(self.shape, self.index(step, place), ref.shape):
            cuts.append(pl.ds(0, size) if size == whole else pl.ds(pl.multiple_of(at * size, size), size))
        return ref.at[tuple(cuts)]

    def spec(self):
        if self.near:
            return pl.BlockSpec(memory_space=pltpu.VMEM)
        if self.index is None:
            return pl.BlockSpec(
                self.shape, lambda step, *place: (0,) * len(self.shape), pipeline_mode=pl.Buffered(1)
            )
        return pl.BlockSpec(self.shape, lambda step, *place: self.index(step, place[0] if place else None))


def near(view):
    return View(view.shape, view.index, near=True)


def loose(view):
    return View(view.shape, view.index, loose=True)


def call(kernel, out_shape, grid, in_specs, out_specs, name, scratch_shapes=()):
    single = not isinstance(out_shape, (list, tuple))
    outs = [out_specs] if single else list(out_specs)
    shapes = [out_shape] if single else list(out_shape)
    scalars = int(in_specs[0] is SMALL_SPEC)
    ins = list(in_specs[scalars:])
    views = [*ins, *outs]

    def body(*refs):
        step = pl.program_id(0)
        place = refs[:scalars]
        rest = refs[scalars:]
        shown = [view.of(ref, step, *(place or (None,))) for view, ref in zip(views, rest)]
        kernel(*place, *shown, *rest[len(views) :])

    specs = [item.spec() for item in outs]
    kinds = [
        jax.ShapeDtypeStruct(item.shape, item.dtype) if view.near else pltpu.HBM(item.shape, item.dtype)
        for item, view in zip(shapes, outs)
    ]
    inner = pl.pallas_call(
        body,
        out_shape=kinds[0] if single else kinds,
        grid_spec=pltpu.PrefetchScalarGridSpec(
            num_scalar_prefetch=scalars,
            grid=grid,
            in_specs=[item.spec() for item in ins],
            out_specs=specs[0] if single else specs,
            scratch_shapes=scratch_shapes,
        ),
        compiler_params=pltpu.CompilerParams(vmem_limit_bytes=VMEM_LIMIT),
        name=name,
    )

    def run(*arrays):
        placed = [
            jnp.asarray(item) if view.near or view.loose else pltpu.with_memory_space_constraint(jnp.asarray(item), pltpu.HBM)
            for item, view in zip(arrays[scalars:], ins)
        ]
        return inner(*arrays[:scalars], *placed)

    return run


def bit_reversed(block):
    return sum(((block >> bit) & 1) << (TOP - 1 - bit) for bit in range(TOP))


def level_columns(rows):
    table = np.zeros((rows, LANES), np.float32)
    for level in range(1, TOP + 1):
        table[: rows >> level, MULT_LANE + level - 1] = 1.0
        table[: rows >> level, MULT_LANE + TOP + level - 1] = 1.0
    return table.astype(ml_dtypes.bfloat16)


def count_columns(rows, groups):
    table = np.zeros((groups, rows, LANES), np.float32)
    for group in range(groups):
        for level in range(group + 1, TOP + 1):
            step = math.log2((level - group + 1) / (level - group))
            high = float(np.float32(step).astype(ml_dtypes.bfloat16))
            table[group, : rows >> level, MULT_LANE + level - 1] = high
            table[group, : rows >> level, MULT_LANE + TOP + level - 1] = step - high
    return table.astype(ml_dtypes.bfloat16)


def spread_table(heads, first_lane):
    table = np.zeros((heads * HEAD_DIM, heads * LANES), np.float32)
    for head in range(heads):
        for item in range(HEAD_DIM):
            table[head * HEAD_DIM + item, head * LANES + first_lane + item] = 1.0
    return table.astype(ml_dtypes.bfloat16)


def dot_nn(left, right):
    return jnp.dot(left, right, preferred_element_type=F32)


def dot_nt(left, right):
    return lax.dot_general(left, right, (((1,), (1,)), ((), ())), preferred_element_type=F32)


def dot_tn(left, right):
    return lax.dot_general(left, right, (((0,), (0,)), ((), ())), preferred_element_type=F32)


def norm_rows(values, gain_row, shift_row):
    center = values - jnp.mean(values, axis=-1, keepdims=True)
    spread = jnp.mean(center * center, axis=-1, keepdims=True)
    return center * lax.rsqrt(spread + EPSILON) * gain_row + shift_row


def norm_back(values, gain_row, grad_rows):
    center = values - jnp.mean(values, axis=-1, keepdims=True)
    spread = jnp.mean(center * center, axis=-1, keepdims=True)
    inverse = lax.rsqrt(spread + EPSILON)
    unit = center * inverse
    scaled = grad_rows * gain_row
    grad_in = inverse * (
        scaled
        - jnp.mean(scaled, axis=-1, keepdims=True)
        - unit * jnp.mean(scaled * unit, axis=-1, keepdims=True)
    )
    return grad_in, jnp.sum(grad_rows * unit, axis=0, keepdims=True), jnp.sum(grad_rows, axis=0, keepdims=True)


def full_spec(shape):
    return View(shape)


def head_spec(rows):
    return View((1, rows, LANES), lambda head, place: (head, 0, 0))


SMALL_SPEC = None


def project_kernel(
    first_ref, x_ref, gain_ref, shift_ref, w_ref, bias_ref, level_ref, spread_k_ref, spread_v_ref,
    normed_ref, q_ref, kv_ref, *refs,
):
    *message_refs, q_rows, kv_rows = refs
    step = pl.program_id(0)
    tile = x_ref.shape[0]
    heads, rows = q_rows.shape[0], q_rows.shape[1]
    block = rows // STRIDE
    tiles = rows // tile

    @pl.when(step < tiles)
    def _():
        project_rows(
            step, first_ref, x_ref, gain_ref, shift_ref, w_ref, bias_ref, spread_k_ref, spread_v_ref, normed_ref, q_rows, kv_rows
        )

    @pl.when(step >= tiles)
    def _():
        head = step - tiles
        turn = (first_ref[0] + head) & (STRIDE - 1)
        for item in range(STRIDE):
            start = bit_reversed(item) ^ turn
            there = slice(item * block, (item + 1) * block)
            q_ref[0, there, :] = q_rows[head, pl.ds(start, block, stride=STRIDE), :].astype(BF16)
            pair = (kv_rows[head, pl.ds(start, block, stride=STRIDE), :] + level_ref[there, :].astype(F32)).astype(BF16)
            kv_ref[0, there, :] = pair
            for ref in message_refs:
                if item * block < ref.shape[1]:
                    ref[0, there, :] = pair


def project_rows(
    step, first_ref, x_ref, gain_ref, shift_ref, w_ref, bias_ref, spread_k_ref, spread_v_ref, normed_ref, q_rows, kv_rows
):
    tile = x_ref.shape[0]
    heads = q_rows.shape[0]
    normed = norm_rows(x_ref[...].astype(F32), gain_ref[...], shift_ref[...]).astype(BF16)
    normed_ref[...] = normed
    query = ((dot_nn(normed, w_ref[0]) + bias_ref[0:1]) * (SCALE * LOG2E)).astype(BF16)
    key = dot_nn(normed, w_ref[1]).astype(BF16)
    value = (dot_nn(normed, w_ref[2]) + bias_ref[1:2]).astype(BF16)
    query_wide = dot_nn(query, spread_k_ref[...])
    pair_wide = dot_nn(key, spread_k_ref[...]) + dot_nn(value, spread_v_ref[...])
    here = pl.ds(pl.multiple_of(step * tile, tile), tile)
    row = lax.broadcasted_iota(jnp.int32, (tile, LANES), 0) + step * tile
    lane = lax.broadcasted_iota(jnp.int32, (tile, LANES), 1)
    doc_lane = functools.reduce(
        jnp.add, [(row >= first_ref[1 + item]).astype(jnp.int32) for item in range(DOCS - 1)], DOC_LANE
    )
    query_extra = (lane == doc_lane).astype(F32)
    other = (lane >= DOC_LANE) & (lane < DOC_LANE + DOCS) & (lane != doc_lane)
    ones = ((lane >= LSE_LANE) & (lane < LSE_LANE + 3)) | ((lane >= ONE_LANE) & (lane < ONE_LANE + 3))
    pair_extra = jnp.where(other, -BIG, ones.astype(F32))
    for head in range(heads):
        lanes = slice(head * LANES, (head + 1) * LANES)
        q_rows[head, here, :] = query_wide[:, lanes] + query_extra
        kv_rows[head, here, :] = pair_wide[:, lanes] + pair_extra


def project(first, tokens, gain, shift, weights, bias, bits):
    rows, width = tokens.shape
    feats = weights.shape[2]
    heads = feats // HEAD_DIM
    tile = min(rows, 256)
    tiles = rows // tile
    row_spec = View((tile, width), lambda i, place: (jnp.minimum(i, tiles - 1), 0))
    shape = (heads, rows, LANES)
    messages = [(heads, rows >> (bit + 1), LANES) for bit in range(bits)]
    return call(
        project_kernel,
        grid=(tiles + heads,),
        in_specs=[
            SMALL_SPEC, row_spec, full_spec((1, width)), full_spec((1, width)), full_spec(weights.shape),
            full_spec(bias.shape), full_spec((rows, LANES)),
            full_spec((feats, heads * LANES)), full_spec((feats, heads * LANES)),
        ],
        out_specs=[row_spec]
        + [
            View((1, *item[1:]), lambda i, place: (jnp.maximum(i - tiles, 0), 0, 0)) for item in (shape, shape, *messages)
        ],
        out_shape=[
            jax.ShapeDtypeStruct((rows, width), BF16),
        ]
        + [jax.ShapeDtypeStruct(item, BF16) for item in (shape, shape, *messages)],
        scratch_shapes=[pltpu.VMEM(shape, F32), pltpu.VMEM(shape, F32)],
        name="project",
    )(
        first, tokens, gain, shift, weights, bias, level_columns(rows),
        spread_table(heads, 0), spread_table(heads, VALUE_LANE),
    )


def group_of(distance):
    return distance.bit_length()


def message_layout(rows, bits):
    direct = [1] + list(range(2, 1 << bits, 2)) if bits else []
    layout = [((item, 0, rows >> group_of(item)),) for item in direct]
    passed, offset = [], 0
    for item in direct[1:]:
        passed.append((item + 1, offset, rows >> group_of(item)))
        offset += rows >> group_of(item)
    return tuple(layout + [tuple(passed)]) if passed else tuple(layout)


def far_pieces(layout, refs):
    return [(ref, *entry) for ref, entries in zip(refs, layout) for entry in entries]


def attend_own_kernel(q_ref, kv_ref, count_ref, out_ref):
    rows = q_ref.shape[1]
    tile = min(rows, 512)
    for low in range(0, rows, tile):
        there = slice(low, low + tile)
        scores = dot_nt(q_ref[0, there, :] + count_ref[0, there, :], kv_ref[0])
        peak = jnp.max(scores, axis=-1, keepdims=True)
        total = dot_nn(jnp.exp2(scores - peak).astype(BF16), kv_ref[0])
        lane = lax.broadcasted_iota(jnp.int32, total.shape, 1)
        out_ref[0, there, :] = jnp.where(lane == 0, peak, total)


def attend_own(queries, pairs, counts):
    heads, rows, _ = queries.shape
    return call(
        attend_own_kernel,
        grid=(heads,),
        in_specs=[head_spec(rows), head_spec(rows), full_spec(counts.shape)],
        out_specs=head_spec(rows),
        out_shape=jax.ShapeDtypeStruct((heads, rows, LANES), F32),
        name="attend_own",
    )(queries, pairs, counts)


def attend_far_kernel(layout, first_ref, q_ref, own_ref, count_ref, gather_ref, *refs):
    pieces_all = far_pieces(layout, refs[: len(layout)])
    out_ref, mine_ref, theirs_ref, placed = refs[len(layout) :]
    head = pl.program_id(0)
    rows = q_ref.shape[1]
    block = rows // STRIDE
    turn = (first_ref[0] + head) & (STRIDE - 1)
    counts = [count for _, _, _, count in pieces_all]
    keys = [ref[0, offset : offset + count, :] for ref, _, offset, count in pieces_all]
    scores = [
        dot_nt(q_ref[0, :count, :] + count_ref[group_of(distance) - 1, :count, :], key)
        for key, (_, distance, _, count) in zip(keys, pieces_all)
    ]
    peaks = [jnp.max(item, axis=-1, keepdims=True) for item in scores]
    edges = sorted({0, rows, *counts})
    tiles = list(zip(edges[:-1], edges[1:]))
    own_peaks = [own_ref[0, low:high, 0:1] for low, high in tiles]
    tops = [
        functools.reduce(jnp.maximum, [peak[low:high] for peak, count in zip(peaks, counts) if low < count], own)
        for (low, high), own in zip(tiles, own_peaks)
    ]
    terms = []
    for score, key, count in zip(scores, keys, counts):
        top = [item for item, (low, _) in zip(tops, tiles) if low < count]
        top = top[0] if len(top) == 1 else jnp.concatenate(top, axis=0)
        terms.append(dot_nn(jnp.exp2(score - top).astype(BF16), key))
    for (low, high), own, top in zip(tiles, own_peaks, tops):
        total = own_ref[0, low:high, :]
        near = [term[low:high] for term, count in zip(terms, counts) if low < count]
        if near:
            total = functools.reduce(jnp.add, near, total * jnp.exp2(own - top))
        mass = total[:, ONE_LANE : ONE_LANE + 1]
        result = total * (1.0 / mass)
        lane = lax.broadcasted_iota(jnp.int32, result.shape, 1)
        out_ref[0, low:high, :] = jnp.where(lane == 0, top + jnp.log2(mass), result)
        for offset in range(low, high, block):
            start = bit_reversed(offset // block) ^ turn
            placed[head, pl.ds(start, block, stride=STRIDE), :] = result[offset - low : offset - low + block]

    @pl.when(head == pl.num_programs(0) - 1)
    def _():
        half = rows // 2
        for side, ref in enumerate((mine_ref, theirs_ref)):
            here = pl.ds(pl.multiple_of(((first_ref[HEADS_PLACE] & 1) ^ side) * half, half), half)
            ref[...] = functools.reduce(
                jnp.add,
                [
                    dot_nn(placed[item, here, :].astype(BF16), gather_ref[item * LANES : (item + 1) * LANES])
                    for item in range(placed.shape[0])
                ],
            ).astype(BF16)


def attend_far(first, queries, own, far, layout, counts):
    heads, rows, _ = queries.shape
    feats = heads * HEAD_DIM
    gather = spread_table(heads, VALUE_LANE).T.copy()
    return call(
        functools.partial(attend_far_kernel, layout),
        grid=(heads,),
        in_specs=[SMALL_SPEC, head_spec(rows), head_spec(rows), full_spec(counts.shape), full_spec(gather.shape)]
        + [loose(head_spec(item.shape[1])) for item in far],
        out_specs=[head_spec(rows), full_spec((rows // 2, feats)), full_spec((rows // 2, feats))],
        out_shape=[
            jax.ShapeDtypeStruct((heads, rows, LANES), F32),
            jax.ShapeDtypeStruct((rows // 2, feats), BF16),
            jax.ShapeDtypeStruct((rows // 2, feats), BF16),
        ],
        scratch_shapes=[pltpu.VMEM((heads, rows, LANES), F32)],
        name="attend_far",
    )(first, queries, own, counts, gather, *far)


def three_parts(values):
    high = values.astype(BF16).astype(F32)
    middle = (values - high).astype(BF16).astype(F32)
    return high, middle, values - high - middle


def pair_grads(keys, query, counted, grad):
    prob = jnp.exp2(dot_nt(keys, counted))
    slope = (prob * dot_nt(keys, grad)).astype(BF16)
    return dot_nn(prob.astype(BF16), grad) + dot_nn(slope, query), dot_tn(slope, keys)


def back_far_kernel(layout, pieces, place_ref, q_ref, out_ref, count_ref, spread_ref, *refs):
    grad_refs = refs[:pieces]
    far = far_pieces(layout, refs[pieces : pieces + len(layout)])
    query, grad, dq_ref = refs[pieces + len(layout) : pieces + len(layout) + 3]
    rows_half = q_ref.shape[1] // 2
    *message_refs, wide = refs[pieces + len(layout) + 3 :]
    targets = []
    for index, entries in enumerate(layout):
        passed = index == len(message_refs)
        for _, offset, _ in entries:
            targets.append((message_refs[0], rows_half + offset) if passed else (message_refs[index], 0))
    head = pl.program_id(0)
    rows = q_ref.shape[1]
    block = rows // STRIDE
    part = grad_refs[0].shape[0]
    turn = (place_ref[0] + head) & (STRIDE - 1)

    @pl.when(head == 0)
    def _():
        for index, ref in enumerate(grad_refs):
            start = pl.multiple_of(place_ref[PART_PLACE + index], part)
            for item in range(wide.shape[0]):
                wide[item, pl.ds(start, part), :] = dot_nn(ref[...], spread_ref[:, item * LANES : (item + 1) * LANES])

    for item in range(STRIDE):
        there = slice(item * block, (item + 1) * block)
        start = bit_reversed(item) ^ turn
        rows_grad = wide[head, pl.ds(start, block, stride=STRIDE), :]
        rows_out = out_ref[0, there, :]
        lane = lax.broadcasted_iota(jnp.int32, rows_grad.shape, 1)
        rows_query = q_ref[0, there, :].astype(F32)
        parts = three_parts(jnp.sum(rows_grad * rows_out, axis=-1, keepdims=True))
        for index, value in enumerate(parts):
            rows_grad = jnp.where(lane == ONE_LANE + index, -value, rows_grad)
        for index, value in enumerate(three_parts(rows_out[:, 0:1])):
            rows_query = jnp.where(lane == LSE_LANE + index, -value, rows_query)
        grad[0, there, :] = rows_grad.astype(BF16)
        query[0, there, :] = rows_query.astype(BF16)

    dq_ref[...] = jnp.zeros_like(dq_ref)
    for (ref, distance, offset, count), (dref, doffset) in zip(far, targets):
        counted = query[0, :count, :] + count_ref[group_of(distance) - 1, :count, :]
        step = min(count, 256)
        for low in range(offset, offset + count, step):
            dkv, dq = pair_grads(ref[0, low : low + step, :], query[0, :count, :], counted, grad[0, :count, :])
            there = slice(doffset + low - offset, doffset + low - offset + step)
            dref[0, there, :] = dkv.astype(BF16)
            dq_ref[0, :count, :] += dq


def back_far(places, grads, queries, outs, far, layout, counts):
    heads, rows, _ = queries.shape
    spread = spread_table(heads, VALUE_LANE)
    limit = rows // 2 if layout else rows // STRIDE
    messages = [sum(item[2] for item in entries) for entries in layout]
    if len(messages) > 1:
        messages = [messages[0] + messages[-1]] + messages[1:-1]
    messages = [(heads, count, LANES) for count in messages]
    return call(
        functools.partial(back_far_kernel, layout, len(grads)),
        grid=(heads,),
        in_specs=[SMALL_SPEC, head_spec(rows), head_spec(rows), full_spec(counts.shape), full_spec(spread.shape)]
        + [near(full_spec(item.shape)) for item in grads]
        + [loose(head_spec(item.shape[1])) for item in far],
        out_specs=[head_spec(rows), head_spec(rows), head_spec(limit)] + [head_spec(item[1]) for item in messages],
        out_shape=[
            jax.ShapeDtypeStruct((heads, rows, LANES), BF16),
            jax.ShapeDtypeStruct((heads, rows, LANES), BF16),
            jax.ShapeDtypeStruct((heads, limit, LANES), F32),
        ]
        + [jax.ShapeDtypeStruct(item, BF16) for item in messages],
        scratch_shapes=[pltpu.VMEM((heads, rows, LANES), F32)],
        name="back_far",
    )(places, queries, outs, counts, spread, *grads, *far)


def back_own_kernel(query, grad, kv_ref, count_ref, dq_far_ref, dq_ref, dkv_ref):
    rows = kv_ref.shape[1]
    limit = dq_far_ref.shape[1]
    counted = query[0] + count_ref[0]
    tile = min(rows, 256)
    for low in range(0, rows, tile):
        there = slice(low, low + tile)
        dkv, dq = pair_grads(kv_ref[0, there, :], query[0], counted, grad[0])
        dkv_ref[0, there, :] = dkv
        if low == 0:
            dq_ref[0] = dq
        else:
            dq_ref[0] += dq
    dq_ref[0, :limit, :] += dq_far_ref[0]


def back_own(queries, grads, pairs, counts, dq_far):
    heads, rows, _ = queries.shape
    return call(
        back_own_kernel,
        grid=(heads,),
        in_specs=[head_spec(rows)] * 3 + [full_spec(counts.shape), head_spec(dq_far.shape[1])],
        out_specs=[near(head_spec(rows))] * 2,
        out_shape=[jax.ShapeDtypeStruct((heads, rows, LANES), F32)] * 2,
        name="back_own",
    )(queries, grads, pairs, counts, dq_far)


def collect_kernel(counts, peers, first_ref, dq_ref, dkv_ref, gather_k_ref, gather_v_ref, w_ref, *refs):
    far_refs = refs[: len(counts)]
    *three_refs, term_ref = refs[len(counts) : len(counts) + 4]
    q_rows, kv_rows = refs[-2:]
    head = pl.program_id(0)
    rows = dq_ref.shape[1]
    part = rows // peers
    block = rows // STRIDE
    turn = (first_ref[0] + head) & (STRIDE - 1)
    for item in range(STRIDE):
        there = slice(item * block, (item + 1) * block)
        start = bit_reversed(item) ^ turn
        pair = dkv_ref[0, there, :]
        for ref, count in zip(far_refs, counts):
            if item * block < count:
                pair = pair + ref[0, there, :].astype(F32)
        lane = lax.broadcasted_iota(jnp.int32, pair.shape, 1)
        q_rows[head, pl.ds(start, block, stride=STRIDE), :] = dq_ref[0, there, :] * SCALE
        kv_rows[head, pl.ds(start, block, stride=STRIDE), :] = jnp.where(lane < VALUE_LANE, pair * LN2, pair)

    @pl.when(head == pl.num_programs(0) - 1)
    def _():
        total = [None] * 3
        for item in range(q_rows.shape[0]):
            lanes = slice(item * LANES, (item + 1) * LANES)
            query = q_rows[item].astype(BF16)
            pair = kv_rows[item].astype(BF16)
            terms = (
                dot_nn(query, gather_k_ref[lanes]),
                dot_nn(pair, gather_k_ref[lanes]),
                dot_nn(pair, gather_v_ref[lanes]),
            )
            total = [term if old is None else old + term for old, term in zip(total, terms)]
        for ref, value in zip(three_refs, total):
            ref[...] = value.astype(BF16)
        for peer in range(peers):
            start = (peer & 1) * (rows // 2) + (peer >> 1) * part
            here = slice(start, start + part)
            term_ref[peer * part : (peer + 1) * part, :] = functools.reduce(
                jnp.add, [dot_nt(ref[here, :], w_ref[item]) for item, ref in enumerate(three_refs)]
            ).astype(BF16)


def collect(places, dq, dkv, far, weights, peers):
    heads, rows, _ = dq.shape
    width, feats = weights.shape[1:]
    gather_k = spread_table(heads, 0).T.copy()
    gather_v = spread_table(heads, VALUE_LANE).T.copy()
    return call(
        functools.partial(collect_kernel, [count for _, count in far], peers),
        grid=(heads,),
        in_specs=[
            SMALL_SPEC, near(head_spec(rows)), near(head_spec(rows)), full_spec(gather_k.shape), full_spec(gather_v.shape),
            full_spec(weights.shape),
        ]
        + [near(head_spec(item.shape[1])) for item, _ in far],
        out_specs=[near(full_spec((rows, feats)))] * 3 + [full_spec((rows, width))],
        out_shape=[jax.ShapeDtypeStruct((rows, feats), BF16)] * 3
        + [jax.ShapeDtypeStruct((rows, width), BF16)],
        scratch_shapes=[pltpu.VMEM((heads, rows, LANES), F32), pltpu.VMEM((heads, rows, LANES), F32)],
        name="collect",
    )(places, dq, dkv, gather_k, gather_v, weights, *[item for item, _ in far])


def pick(core, low, high):
    return jnp.where(core == 0, low, high), jnp.where(core == 0, high, low)


def halves(array):
    half = array.shape[-1] // 2
    return array[:, :half], array[:, half:]


FETCHED = 2
BIAS_ROWS = 16


def fetched_weights(refs, up_shape, down_shape):
    sides = []
    for ref in refs:
        count = up_shape[0] // 2
        down = ref[count : 2 * count].reshape(down_shape[0] // 2, down_shape[1])
        bias = ref[2 * count : 2 * count + 1].astype(F32)
        for index in (1, 2):
            bias = bias + ref[2 * count + index : 2 * count + index + 1].astype(F32)
        sides.append((ref.at[:count], down, bias))
    return sides


def feed_kernel(
    place_ref, tok_ref, cot_ref, w_out_ref, b_out_ref, gain_ref, shift_ref, up_ref, down_ref, bias_ref, *refs,
):
    fetched, refs = refs[:FETCHED], refs[FETCHED:]
    (up_one, down_one, bias_other), (up_two, down_two, _) = fetched_weights(fetched, up_ref.shape, down_ref.shape)
    attn_refs = refs[:-10]
    resid_ref, normed_ref, cot_out_ref, h0_ref, h1_ref, p0_ref, p1_ref, da_ref, out_ref, sums_ref = refs[-10:]
    feats = attn_refs[0].shape[1]
    core = place_ref[SEQ_PLACE] & 1
    resid = tok_ref[...].astype(F32) + b_out_ref[...]
    for index, ref in enumerate(attn_refs):
        here = pl.ds(pl.multiple_of((place_ref[HEADS_PLACE] ^ index) * feats, feats), feats)
        resid = resid + dot_nn(ref[...], w_out_ref[here, :])
    resid_ref[0] = resid
    normed = norm_rows(resid, gain_ref[...], shift_ref[...]).astype(BF16)
    normed_ref[0] = normed
    cot = cot_ref[...]
    cot_out_ref[0] = cot
    normed_pair = pick(core, *halves(normed))
    pres = (
        dot_nn(normed, up_ref[...]) + bias_ref[...],
        dot_nn(normed_pair[0], up_one[...]) + dot_nn(normed_pair[1], up_two[...]) + bias_other,
    )
    acts = (
        dot_nt(cot, down_ref[...]),
        jnp.concatenate(pick(core, dot_nt(cot, down_one[...]), dot_nt(cot, down_two[...])), axis=1),
    )
    grads = []
    for pre, act, h_ref, p_ref in zip(pres, acts, (h0_ref, h1_ref), (p0_ref, p1_ref)):
        share = 0.5 * (1.0 + lax.erf(pre * math.sqrt(0.5)))
        h_ref[0] = (pre * share).astype(BF16)
        slope = share + pre * jnp.exp(-0.5 * pre * pre) * (1.0 / math.sqrt(2.0 * math.pi))
        grads.append((act * slope).astype(BF16))
        p_ref[0] = grads[-1]
    other = pick(core, dot_nt(grads[1], up_one[...]), dot_nt(grads[1], up_two[...]))
    da_ref[0] = (dot_nt(grads[0], up_ref[...]) + jnp.concatenate(other, axis=1)).astype(da_ref.dtype)
    hidden_pair = pick(core, *halves(h1_ref[0]))
    out_ref[0] = (
        dot_nn(h0_ref[0], down_ref[...])
        + dot_nn(hidden_pair[0], down_one[...])
        + dot_nn(hidden_pair[1], down_two[...])
    ).astype(out_ref.dtype)
    ones = jnp.ones((8, cot.shape[0]), BF16)
    sums_ref[0, 0] = dot_nn(ones, grads[0])
    sums_ref[0, 1] = dot_nn(ones, grads[1])


def feed(places, part, steps, kind, tokens, cotangent, w_out, b_out, gain, shift, up, down, bias, fetched, attns):
    rows, width = tokens.shape
    hidden = up.shape[1]
    feats = attns[0].shape[1]
    inner = attns[0].shape[0] // part
    first = steps[0]

    def piece(i, place):
        return (place[HEADS_PLACE] >> 1) ^ (i + first)

    def row_block(i, place):
        return ((place[HEADS_PLACE] & 1) * inner + piece(i, place), 0)

    def stacked(columns):
        return View((1, part, columns), lambda i, place: (i, 0, 0))

    constants = (w_out, b_out, gain, shift, up, down, bias)
    outs = [(width, F32), (width, BF16), (width, BF16)] + [(hidden, BF16)] * 4 + [(width, kind)] * 2
    count = len(steps)
    return call(
        feed_kernel,
        grid=(count,),
        in_specs=[SMALL_SPEC]
        + [View((part, width), row_block)] * 2
        + [full_spec(item.shape) for item in constants]
        + [loose(full_spec(item.shape)) for item in fetched]
        + [View((part, feats), lambda i, place: (piece(i, place), 0), loose=True)] * len(attns),
        out_specs=[near(stacked(columns)) for columns, _ in outs]
        + [View((1, 2, 8, hidden), lambda i, place: (i, 0, 0, 0))],
        out_shape=[jax.ShapeDtypeStruct((count, part, columns), dtype) for columns, dtype in outs]
        + [jax.ShapeDtypeStruct((count, 2, 8, hidden), F32)],
        name="feed",
    )(places, tokens, cotangent, *constants, *fetched, *attns)


def outer_kernel(pairs, place_ref, *refs):
    ins, (keep_ref, give_ref) = refs[:-2], refs[-2:]
    step = pl.program_id(0)
    core = place_ref[SEQ_PLACE] & 1
    for index in range(pairs):

        @pl.when(step == index)
        def _():
            total = None
            for left_ref, right_ref in zip(ins[4 * index : 4 * index + 2], ins[4 * index + 2 : 4 * index + 4]):
                for item in range(left_ref.shape[0]):
                    left = pick(core, *halves(left_ref[item]))
                    terms = [dot_tn(side, right_ref[item]) for side in left]
                    total = terms if total is None else [old + term for old, term in zip(total, terms)]
            keep_ref[0] = total[0].astype(BF16)
            give_ref[0] = total[1].astype(BF16)


def outer_sums(places, pairs):
    lefts = pairs[0][0][0].shape[2] // 2
    rights = pairs[0][1][0].shape[2]
    arrays = [item for pair in pairs for side in pair for item in side]
    spec = View((1, lefts, rights), lambda i, place: (i, 0, 0))
    shape = jax.ShapeDtypeStruct((len(pairs), lefts, rights), BF16)
    return call(
        functools.partial(outer_kernel, len(pairs)),
        grid=(len(pairs),),
        in_specs=[SMALL_SPEC] + [near(full_spec(item.shape)) for item in arrays],
        out_specs=[spec, near(spec)],
        out_shape=[shape, shape],
        name="outer_sums",
    )(places, *arrays)


def out_grads_kernel(place_ref, low_ref, *refs):
    *attn_refs, keep_ref, give_ref = refs
    half = attn_refs[0].shape[1] // 2
    core = place_ref[SEQ_PLACE] & 1
    bits = len(attn_refs).bit_length() - 1
    for distance, ref in enumerate(attn_refs):
        index = sum(((distance >> bit) & 1) << (bits - 1 - bit) for bit in range(bits))
        product = dot_tn(ref[...], low_ref[...])
        keep, give = pick(core, product[:half], product[half:])
        keep_ref[index] = keep.astype(BF16)
        give_ref[index] = give.astype(BF16)


def out_grads(places, low, attns):
    part, width = low.shape
    feats = attns[0].shape[1]
    shape = (len(attns), feats // 2, width)
    return call(
        out_grads_kernel,
        grid=(1,),
        in_specs=[SMALL_SPEC, near(full_spec((part, width)))]
        + [View((part, feats), lambda i, place: (place[HEADS_PLACE] >> 1, 0), loose=True)] * len(attns),
        out_specs=[near(full_spec(shape))] * 2,
        out_shape=[jax.ShapeDtypeStruct(shape, BF16)] * 2,
        name="out_grads",
    )(places, low, *attns)


def tail_kernel(normed_ref, tok_ref, w_ref, _, stats_ref, up_ref, *refs):
    *three_refs, out_ref, sums_ref = refs
    rows, width = normed_ref.shape
    feats = three_refs[0].shape[1]
    hidden = up_ref.shape[1]
    for index, ref in enumerate(three_refs):
        out_ref[index * feats : (index + 1) * feats, :] = dot_tn(ref[...], normed_ref[...]).astype(BF16)
    gain = jnp.zeros((1, width), F32)
    shift = jnp.zeros((1, width), F32)
    tile = min(rows, 256)
    for low in range(0, rows, tile):
        here = slice(low, low + tile)
        term = functools.reduce(
            jnp.add, [dot_nt(ref[here, :], w_ref[index]) for index, ref in enumerate(three_refs)]
        )
        center = tok_ref[here, :].astype(F32)
        center = center - jnp.mean(center, axis=-1, keepdims=True)
        unit = center * lax.rsqrt(jnp.mean(center * center, axis=-1, keepdims=True) + EPSILON)
        gain = gain + column_sums(term * unit)
        shift = shift + column_sums(term)
    row = lax.broadcasted_iota(jnp.int32, (SUM_ROWS, width), 0)
    other = up_ref[1:2, :]
    if hidden < width:
        other = jnp.concatenate([other, jnp.zeros((1, width - hidden), F32)], axis=1)
    lines = (gain, stats_ref[0:1], shift, stats_ref[1:2], stats_ref[2:3], stats_ref[3:4], other)
    block = jnp.zeros((SUM_ROWS, width), F32)
    for index, line in enumerate(lines):
        block = jnp.where(row == index, line, block)
    sums_ref[:SUM_ROWS, :] = block.astype(BF16)
    sums_ref[SUM_ROWS:, :] = jnp.zeros((3 * SUM_ROWS, width), BF16)
    ones = jnp.ones((SUM_ROWS, rows), BF16)
    own = jnp.broadcast_to(up_ref[0:1, :], (SUM_ROWS, hidden))
    for index, value in enumerate((own, dot_nn(ones, three_refs[0][...]), dot_nn(ones, three_refs[2][...]))):
        here = (index + 1) * SUM_ROWS
        sums_ref[here : here + SUM_ROWS, : value.shape[1]] = value.astype(BF16)


SUM_ROWS = 16


def tail_grads(normed, tokens, weights, earlier, stats, ups, three):
    rows, width = normed.shape
    feats = three[0].shape[1]
    ins = (normed, tokens, weights, stats, ups, *three)
    specs = [full_spec(item.shape) for item in ins[:5]] + [near(full_spec(item.shape)) for item in three]
    ins = (*ins[:3], earlier, *ins[3:])
    return call(
        tail_kernel,
        grid=(1,),
        in_specs=[*specs[:3], View((1, 16, LANES), lambda step, place: (0, 0, 0)), *specs[3:]],
        out_specs=[near(full_spec((3 * feats, width))), near(full_spec((4 * SUM_ROWS, width)))],
        out_shape=[jax.ShapeDtypeStruct((count, width), BF16) for count in (3 * feats, 4 * SUM_ROWS)],
        name="tail_grads",
    )(*ins)


def pack_kernel(core_ref, up_ref, down_ref, bias_ref, out_ref):
    count = up_ref.shape[0]
    out_ref[:count, :] = up_ref[...]
    out_ref[count : 2 * count, :] = down_ref[...]
    row = lax.broadcasted_iota(jnp.int32, (BIAS_ROWS, bias_ref.shape[1]), 0)
    block = jnp.zeros(row.shape, F32)
    for index, line in enumerate(three_parts(bias_ref[...])):
        block = jnp.where(row == index, line, block)
    out_ref[2 * count :, :] = block.astype(BF16)


def pack_weights(core, up, down, bias):
    hidden = up.shape[1]
    shape = (up.shape[0] + BIAS_ROWS, hidden)
    if up.shape != down.shape:
        cuts = [
            lax.dynamic_slice_in_dim(item, core * (item.shape[0] // 2), item.shape[0] // 2).reshape(-1, hidden)
            for item in (up, down)
        ]
        zeros = jnp.zeros((BIAS_ROWS - 3, hidden), F32)
        return jnp.concatenate([*cuts, jnp.concatenate([*three_parts(bias), zeros]).astype(BF16)])
    return call(
        pack_kernel,
        grid=(1,),
        in_specs=[SMALL_SPEC]
        + [View((up.shape[0] // 2, hidden), lambda i, place: (place[0], 0))] * 2
        + [full_spec(bias.shape)],
        out_specs=full_spec(shape),
        out_shape=jax.ShapeDtypeStruct(shape, BF16),
        name="pack_weights",
    )(core.reshape(1), up, down, bias)


def column_sums(array):
    return jnp.sum(array, axis=0, keepdims=True)


def turn_kernel(received, place_ref, resid_ref, cot_ref, da_ref, gain_ref, w_out_ref, *refs):
    more_refs = refs[:received]
    dres_ref, low_ref, stats_ref, *grad_refs = refs[received:]
    feats = grad_refs[0].shape[1]
    total = da_ref[0]
    for ref in more_refs:
        total = total + ref[...].reshape(total.shape).astype(F32)
    cot = cot_ref[0].astype(F32)
    grad_n, gain_sum, shift_sum = norm_back(resid_ref[0], gain_ref[...], total)
    dres = cot + grad_n
    dres_ref[...] = dres
    low = dres.astype(BF16)
    low_ref[...] = low
    for index, ref in enumerate(grad_refs):
        here = pl.ds(pl.multiple_of((place_ref[HEADS_PLACE] ^ index) * feats, feats), feats)
        ref[...] = dot_nt(low, w_out_ref[here, :]).astype(BF16)
    stats_ref[0:1] = gain_sum
    stats_ref[1:2] = shift_sum
    stats_ref[2:3] = column_sums(dres)
    stats_ref[3:4] = column_sums(cot)
    stats_ref[4:8] = jnp.zeros_like(stats_ref[4:8])


def turn_back(places, resid, cot, gain, da, more, w_out, peers):
    _, part, width = resid.shape
    feats = width // peers
    ins = (resid, cot, da, gain, w_out)
    return call(
        functools.partial(turn_kernel, len(more)),
        grid=(1,),
        in_specs=[SMALL_SPEC]
        + [near(full_spec(item.shape)) for item in ins[:3]]
        + [full_spec(item.shape) for item in ins[3:]]
        + [near(full_spec(item.shape)) for item in more],
        out_specs=[full_spec((part, width)), near(full_spec((part, width))), full_spec((8, width))]
        + [near(full_spec((part, feats)))] * peers,
        out_shape=[
            jax.ShapeDtypeStruct((part, width), F32),
            jax.ShapeDtypeStruct((part, width), BF16),
            jax.ShapeDtypeStruct((8, width), F32),
        ]
        + [jax.ShapeDtypeStruct((part, feats), BF16)] * peers,
        name="turn_back",
    )(places, *ins, *more)


def finish_kernel(place_ref, tok_ref, gain_ref, term_ref, dres_ref, grad_ref):
    grad_n, _, _ = norm_back(tok_ref[...].astype(F32), gain_ref[...], term_ref[...].astype(F32))
    grad_ref[...] = (dres_ref[...] + grad_n).astype(BF16)


def finish(places, tokens, gain, term, dres):
    part, width = term.shape
    return call(
        finish_kernel,
        grid=(1,),
        in_specs=[SMALL_SPEC, View((part, width), lambda i, place: (place[PART_PLACE] // part, 0))]
        + [full_spec(item.shape) for item in (gain, term, dres)],
        out_specs=full_spec((part, width)),
        out_shape=jax.ShapeDtypeStruct((part, width), BF16),
        name="finish",
    )(places, tokens, gain, term, dres)


def flipped(array, distance):
    return lax.ppermute(array, "seq", [(i, i ^ distance) for i in range(lax.axis_size("seq"))])


def crossed(array, distance):
    if distance == 0:
        return array
    return lax.ppermute(array, "heads", [(i, i ^ distance) for i in range(lax.axis_size("heads"))])


def added(left, right):
    return (left.astype(F32) + right.astype(F32)).astype(BF16)


def halved(array, axis, bit):
    side = (lax.axis_index("seq") >> bit) & 1
    count = array.shape[axis] // 2
    keep = lax.dynamic_slice_in_dim(array, side * count, count, axis)
    give = lax.dynamic_slice_in_dim(array, (1 - side) * count, count, axis)
    other = flipped(give, 1 << bit)
    return added(keep, other), other


def doubled(array, axis, bit):
    side = (lax.axis_index("seq") >> bit) & 1
    other = flipped(array, 1 << bit)
    whole = jnp.where(side == 0, jnp.concatenate([array, other], axis), jnp.concatenate([other, array], axis))
    return whole, other


def after(value, earlier):
    return lax.optimization_barrier((value, earlier))[0]


def shards(tokens, docs, ln_gain, ln_bias, w_qkv, b_qv, w_out, b_out, w_up, b_up, w_down, b_down, cotangent):
    rows, width = tokens.shape
    feats = w_qkv.shape[3]
    heads = feats // HEAD_DIM
    seq_count = lax.axis_size("seq")
    head_count = lax.axis_size("heads")
    seq_pos = lax.axis_index("seq")
    head_pos = lax.axis_index("heads")
    seq_bits = seq_count.bit_length() - 1
    gains, shifts = ln_gain[0], ln_bias[0]
    half = rows // 2
    part = rows // head_count
    peers = [head_pos ^ distance for distance in range(head_count)]
    part_starts = [(peer & 1) * half + (peer >> 1) * part for peer in peers]
    edges = [jnp.sum((docs <= item).astype(jnp.int32)) - seq_pos * rows for item in range(DOCS - 1)]
    places = jnp.stack(
        [item.astype(jnp.int32) for item in (head_pos * heads, *edges, head_pos, seq_pos, *part_starts)]
    )

    core = seq_pos & 1
    hidden = w_up.shape[2]
    w_out_all = lax.all_gather(w_out[0], "heads", axis=0, tiled=True)
    fetched_one = crossed(pack_weights(core.astype(jnp.int32), w_up[0], w_down[0], b_up), 1)

    w_three = jnp.transpose(w_qkv[0], (1, 0, 2))
    bits = min(seq_bits, TOP)
    normed, queries, pairs, *messages = project(places, tokens, gains[0:1], shifts[0:1], w_three, b_qv[0], bits)
    layout = message_layout(rows, bits)
    counts = count_columns(rows, bits + 1)
    own_counts, far_counts = counts[:1], counts[1:, : rows // 2]
    direct = layout[:-1] if bits > 1 else layout
    far = [flipped(messages[group_of(entries[0][0]) - 1], entries[0][0]) for entries in direct]
    own_outs = attend_own(queries, pairs, own_counts)
    if bits > 1:
        far.append(flipped(after(jnp.concatenate(far[1:], axis=1), own_outs), 1))
    outs, attn_mine, attn_theirs = attend_far(places, queries, own_outs, far, layout, far_counts)
    fetched = [fetched_one, flipped(after(fetched_one, outs), 1)]
    attns = [attn_mine] + [
        crossed(attn_theirs if distance & 1 else attn_mine, distance) for distance in range(1, head_count)
    ]

    def in_rows(array):
        return jnp.transpose(array.reshape(steps, 2, part, width), (1, 0, 2, 3)).reshape(rows, width)

    steps = head_count // 2
    shared = (
        tokens, cotangent, w_out_all, b_out, gains[1:2], shifts[1:2], w_up[0], w_down[0], b_up, fetched, attns,
    )
    sent = feed(places, part, range(1, steps), BF16, *shared) if steps > 1 else None
    da_more = [crossed(sent[7][step - 1], 2 * step) for step in range(1, steps)]
    own = feed(places, part, range(0, 1), F32, *shared)
    if sent is None:
        sent = [item[:0] for item in own]
    resid, normed_two, cots, h0, h1, p0, p1, da_two, out_term, up_sums = zip(own, sent)

    dres, dres_low, stats_two, *grad_attns = turn_back(
        places, resid[0], cots[0], gains[1:2], da_two[0], da_more, w_out_all, head_count
    )
    grad_attns = [crossed(item, distance) for distance, item in enumerate(grad_attns)]
    later = after(places, dres)
    out_keep, out_give = out_grads(later, dres_low, attns)
    later = after(later, out_keep)
    out_core = flipped(out_give, 1)
    out_grad = added(out_keep, out_core)
    products = [(normed_two, p0), (h0, cots), (normed_two, p1), (h1, cots)]
    if hidden == width:
        packs = [outer_sums(later, products)]
    else:
        packs = [outer_sums(later, products[0::2]), outer_sums(later, products[1::2])]
    packs = after(packs, grad_attns)
    arrived = [flipped(give, 1) for _, give in packs]
    packs = [(keep, item) for (keep, _), item in zip(packs, arrived)]

    out_terms = after(out_term[1], grad_attns)
    out_more = [crossed(out_terms[step - 1], 2 * step) for step in range(1, steps)]
    out_other = crossed(out_grad[steps:], 1)
    queries_b, grads_b, dq_far, *dfar = back_far(
        after(places, (*arrived, out_core)), grad_attns, queries, outs, far, layout, far_counts
    )
    out_sum = functools.reduce(jnp.add, [item.astype(F32) for item in after(out_more, dq_far)], out_term[0][0])
    out_part = (resid[0][0] + out_sum + b_down[0]).astype(BF16)
    back = []
    if bits:
        arrived = flipped(after(dfar[0], (out_more, out_other)), 1)
        arrived = after(arrived, out_part)
        offset = rows // 2
        onward = []
        for item in dfar[1:]:
            count = item.shape[1]
            onward.append(added(item, arrived[:, offset : offset + count]))
            offset += count
        queries_b = after(queries_b, onward)
        back = [(arrived, rows // 2)] + [
            (flipped(item, entries[0][0]), item.shape[1]) for entries, item in zip(direct[1:], onward)
        ]
    out_grad = added(out_grad[:steps], out_other)
    queries_b, out_part = lax.optimization_barrier((queries_b, out_part))
    gathered = lax.all_gather(out_part, "heads", axis=0)
    output = in_rows(gathered)
    dq, dkv = back_own(queries_b, grads_b, pairs, own_counts, dq_far)
    ups = (up_sums[0][:, :, 0], up_sums[1][:, :, 0])
    ups = jnp.sum(ups[0], axis=0) + jnp.sum(ups[1], axis=0)
    *grads_three, terms = collect(after(places, ups), dq, dkv, back, w_three, head_count)
    term = lax.psum_scatter(terms, "heads", scatter_dimension=0, tiled=True)
    orders = [list(range(1, seq_bits))] * 2
    if seq_bits > 2:
        orders[1] = [2, 1] + orders[0][2:]
    packs = [added(*item) for item in after(packs, terms)]
    count = packs[0].shape[1] // 2
    packs = [[item[:, :count], item[:, count:]] for item in packs]
    arrived = []
    for step in range(seq_bits - 1):
        for pack in packs:
            for side, order in enumerate(orders):
                pack[side], other = halved(pack[side], 1, order[step])
                if not step:
                    arrived.append(other)
    packs = [jnp.concatenate(pack, axis=1) for pack in packs]
    passed = [crossed(item[item.shape[0] // 2 :], 1) for item in packs]
    packs = [added(item[: item.shape[0] // 2], other) for item, other in zip(packs, passed)]
    distance = 2
    while distance < head_count:
        count = out_grad.shape[0] // 2
        out_grad = added(out_grad[:count], crossed(out_grad[count:], distance))
        distance = 2 * distance
    grad_w_out = out_grad[0]

    rest, sums = tail_grads(normed, tokens, w_three, gathered, stats_two, ups, grads_three)
    count = rest.shape[0] // 2
    keep, give = (lax.dynamic_slice_in_dim(rest, side * count, count) for side in (core, 1 - core))
    rest = added(jnp.concatenate([keep, sums]), flipped(jnp.concatenate([give, sums]), 1))
    rest = jnp.concatenate([rest, grad_w_out])
    cut = rest.shape[0] // 2
    rest = [rest[:cut], rest[cut:]]

    def swap(step):
        others = [flipped(item, 1 << order[step]) for item, order in zip(rest, orders)]
        return [added(item, other) for item, other in zip(rest, others)], others

    others = []
    if seq_bits > 1:
        rest, others = swap(0)
    arrived = (passed, others)
    grad_part = finish(after(places, arrived), tokens, gains[0:1], term, dres)
    grad_tokens = in_rows(lax.all_gather(grad_part, "heads", axis=0)).astype(F32)
    packs, rest = after((packs, rest), grad_part)
    for step in range(1, seq_bits - 1):
        rest, _ = swap(step)
    rest = jnp.concatenate(rest)
    half_rows = packs[0].shape[1] // 2
    packs = [[item[:, :half_rows], item[:, half_rows:]] for item in packs]
    for step in reversed(range(seq_bits - 1)):
        for pack in packs:
            for side, order in enumerate(orders):
                pack[side], _ = doubled(pack[side], 1, order[step])
    packs = [doubled(jnp.concatenate(pack, axis=1), 1, 0)[0] for pack in packs]
    sums = rest[count : count + 4 * SUM_ROWS]
    rest = jnp.concatenate([rest[:count], rest[count + 4 * SUM_ROWS :]])
    rest = doubled(rest, 0, 0)[0].astype(F32).reshape(2, -1, width)
    grad_w_out = rest[:, count:].reshape(feats, width)
    rest = rest[:, :count]
    more = [crossed(sums[:SUM_ROWS], distance).astype(F32) for distance in range(1, head_count)]
    sums = sums.astype(F32)
    wide = functools.reduce(jnp.add, more, sums[:SUM_ROWS])[:6]
    grad_b_up = sums[SUM_ROWS, :hidden] + more[0][6, :hidden]
    grad_b_qv = jnp.stack([sums[(index + 2) * SUM_ROWS, :feats] for index in range(2)])
    packs = [packs[0][0], packs[0][1]] if hidden == width else [packs[0][0], packs[1][0]]
    grad_w_up, grad_w_down = (item.astype(F32) for item in packs)
    grad_w_qkv = jnp.transpose(rest.reshape(3, feats, width), (2, 0, 1))
    return (
        output, grad_tokens, wide[None, 0:2], wide[None, 2:4], grad_w_qkv[None], grad_b_qv[None],
        grad_w_out[None], wide[4:5], grad_w_up[None], grad_b_up[None], grad_w_down[None], wide[5:6],
    )


def solution(mesh):
    in_specs = (
        P("seq", None), P(), P(), P(), P(None, None, None, "heads"), P(None, None, "heads"),
        P(None, "heads", None), P(), P(None, None, "heads"), P(None, "heads"), P(None, "heads", None), P(),
        P("seq", None),
    )
    out_specs = (
        P("seq", None), P("seq", None), P(), P(), P(None, None, None, "heads"), P(None, None, "heads"),
        P(None, "heads", None), P(), P(None, None, "heads"), P(None, "heads"), P(None, "heads", None), P(),
    )
    return jax.shard_map(shards, mesh=mesh, in_specs=in_specs, out_specs=out_specs, check_vma=False)
```

```python
import functools
import math

import jax
import jax.numpy as jnp
import ml_dtypes
import numpy as np
from jax import lax
from jax.experimental import pallas as pl
from jax.experimental.pallas import tpu as pltpu
from jax.sharding import PartitionSpec as P

HEAD_DIM = 48
BRANCHES = 5
DOCS = 3
TOP = BRANCHES - 1
STRIDE = 2**TOP
LANES = 128
EPSILON = 1e-05
BIG = 2.0**100
SCALE = HEAD_DIM**-0.5
LOG2E = math.log2(math.e)
LN2 = math.log(2.0)
DOC_LANE = HEAD_DIM
MULT_LANE = DOC_LANE + DOCS
LSE_LANE = MULT_LANE + 2 * TOP
VALUE_LANE = LANES // 2
ONE_LANE = VALUE_LANE + HEAD_DIM
F32 = jnp.float32
BF16 = jnp.bfloat16
VMEM_LIMIT = 28 * 1024 * 1024
HEADS_PLACE = DOCS
SEQ_PLACE = DOCS + 1
PART_PLACE = DOCS + 2


class View:
    def __init__(self, shape, index=None, near=False, loose=False):
        self.shape, self.index, self.near, self.loose = tuple(shape), index, near, loose

    def of(self, ref, step, place):
        if not self.near or self.index is None:
            return ref
        cuts = []
        for size, at, whole in zip(self.shape, self.index(step, place), ref.shape):
            cuts.append(pl.ds(0, size) if size == whole else pl.ds(pl.multiple_of(at * size, size), size))
        return ref.at[tuple(cuts)]

    def spec(self):
        if self.near:
            return pl.BlockSpec(memory_space=pltpu.VMEM)
        if self.index is None:
            return pl.BlockSpec(
                self.shape, lambda step, *place: (0,) * len(self.shape), pipeline_mode=pl.Buffered(1)
            )
        return pl.BlockSpec(self.shape, lambda step, *place: self.index(step, place[0] if place else None))


def near(view):
    return View(view.shape, view.index, near=True)


def loose(view):
    return View(view.shape, view.index, loose=True)


def call(kernel, out_shape, grid, in_specs, out_specs, name, scratch_shapes=()):
    single = not isinstance(out_shape, (list, tuple))
    outs = [out_specs] if single else list(out_specs)
    shapes = [out_shape] if single else list(out_shape)
    scalars = int(in_specs[0] is SMALL_SPEC)
    ins = list(in_specs[scalars:])
    views = [*ins, *outs]

    def body(*refs):
        step = pl.program_id(0)
        place = refs[:scalars]
        rest = refs[scalars:]
        shown = [view.of(ref, step, *(place or (None,))) for view, ref in zip(views, rest)]
        kernel(*place, *shown, *rest[len(views) :])

    specs = [item.spec() for item in outs]
    kinds = [
        jax.ShapeDtypeStruct(item.shape, item.dtype) if view.near else pltpu.HBM(item.shape, item.dtype)
        for item, view in zip(shapes, outs)
    ]
    inner = pl.pallas_call(
        body,
        out_shape=kinds[0] if single else kinds,
        grid_spec=pltpu.PrefetchScalarGridSpec(
            num_scalar_prefetch=scalars,
            grid=grid,
            in_specs=[item.spec() for item in ins],
            out_specs=specs[0] if single else specs,
            scratch_shapes=scratch_shapes,
        ),
        compiler_params=pltpu.CompilerParams(vmem_limit_bytes=VMEM_LIMIT),
        name=name,
    )

    def run(*arrays):
        placed = [
            jnp.asarray(item) if view.near or view.loose else pltpu.with_memory_space_constraint(jnp.asarray(item), pltpu.HBM)
            for item, view in zip(arrays[scalars:], ins)
        ]
        return inner(*arrays[:scalars], *placed)

    return run


def bit_reversed(block):
    return sum(((block >> bit) & 1) << (TOP - 1 - bit) for bit in range(TOP))


def level_columns(rows):
    table = np.zeros((rows, LANES), np.float32)
    for level in range(1, TOP + 1):
        table[: rows >> level, MULT_LANE + level - 1] = 1.0
        table[: rows >> level, MULT_LANE + TOP + level - 1] = 1.0
    return table.astype(ml_dtypes.bfloat16)


def count_columns(rows, groups):
    table = np.zeros((groups, rows, LANES), np.float32)
    for group in range(groups):
        for level in range(group + 1, TOP + 1):
            step = math.log2((level - group + 1) / (level - group))
            high = float(np.float32(step).astype(ml_dtypes.bfloat16))
            table[group, : rows >> level, MULT_LANE + level - 1] = high
            table[group, : rows >> level, MULT_LANE + TOP + level - 1] = step - high
    return table.astype(ml_dtypes.bfloat16)


def spread_table(heads, first_lane):
    table = np.zeros((heads * HEAD_DIM, heads * LANES), np.float32)
    for head in range(heads):
        for item in range(HEAD_DIM):
            table[head * HEAD_DIM + item, head * LANES + first_lane + item] = 1.0
    return table.astype(ml_dtypes.bfloat16)


def dot_nn(left, right):
    return jnp.dot(left, right, preferred_element_type=F32)


def dot_nt(left, right):
    return lax.dot_general(left, right, (((1,), (1,)), ((), ())), preferred_element_type=F32)


def dot_tn(left, right):
    return lax.dot_general(left, right, (((0,), (0,)), ((), ())), preferred_element_type=F32)


def norm_rows(values, gain_row, shift_row):
    center = values - jnp.mean(values, axis=-1, keepdims=True)
    spread = jnp.mean(center * center, axis=-1, keepdims=True)
    return center * lax.rsqrt(spread + EPSILON) * gain_row + shift_row


def norm_back(values, gain_row, grad_rows):
    center = values - jnp.mean(values, axis=-1, keepdims=True)
    spread = jnp.mean(center * center, axis=-1, keepdims=True)
    inverse = lax.rsqrt(spread + EPSILON)
    unit = center * inverse
    scaled = grad_rows * gain_row
    grad_in = inverse * (
        scaled
        - jnp.mean(scaled, axis=-1, keepdims=True)
        - unit * jnp.mean(scaled * unit, axis=-1, keepdims=True)
    )
    return grad_in, jnp.sum(grad_rows * unit, axis=0, keepdims=True), jnp.sum(grad_rows, axis=0, keepdims=True)


def full_spec(shape):
    return View(shape)


def head_spec(rows):
    return View((1, rows, LANES), lambda head, place: (head, 0, 0))


SMALL_SPEC = None


def project_kernel(
    first_ref, x_ref, gain_ref, shift_ref, w_ref, bias_ref, level_ref, spread_k_ref, spread_v_ref,
    normed_ref, q_ref, kv_ref, *refs,
):
    *message_refs, q_rows, kv_rows = refs
    step = pl.program_id(0)
    tile = x_ref.shape[0]
    heads, rows = q_rows.shape[0], q_rows.shape[1]
    block = rows // STRIDE
    tiles = rows // tile

    @pl.when(step < tiles)
    def _():
        project_rows(
            step, first_ref, x_ref, gain_ref, shift_ref, w_ref, bias_ref, spread_k_ref, spread_v_ref, normed_ref, q_rows, kv_rows
        )

    @pl.when(step >= tiles)
    def _():
        head = step - tiles
        turn = (first_ref[0] + head) & (STRIDE - 1)
        for item in range(STRIDE):
            start = bit_reversed(item) ^ turn
            there = slice(item * block, (item + 1) * block)
            q_ref[0, there, :] = q_rows[head, pl.ds(start, block, stride=STRIDE), :].astype(BF16)
            pair = (kv_rows[head, pl.ds(start, block, stride=STRIDE), :] + level_ref[there, :].astype(F32)).astype(BF16)
            kv_ref[0, there, :] = pair
            for ref in message_refs:
                if item * block < ref.shape[1]:
                    ref[0, there, :] = pair


def project_rows(
    step, first_ref, x_ref, gain_ref, shift_ref, w_ref, bias_ref, spread_k_ref, spread_v_ref, normed_ref, q_rows, kv_rows
):
    tile = x_ref.shape[0]
    heads = q_rows.shape[0]
    normed = norm_rows(x_ref[...].astype(F32), gain_ref[...], shift_ref[...]).astype(BF16)
    normed_ref[...] = normed
    query = ((dot_nt(normed, w_ref[0]) + bias_ref[0:1]) * (SCALE * LOG2E)).astype(BF16)
    key = dot_nt(normed, w_ref[1]).astype(BF16)
    value = (dot_nt(normed, w_ref[2]) + bias_ref[1:2]).astype(BF16)
    query_wide = dot_nn(query, spread_k_ref[...])
    pair_wide = dot_nn(key, spread_k_ref[...]) + dot_nn(value, spread_v_ref[...])
    here = pl.ds(pl.multiple_of(step * tile, tile), tile)
    row = lax.broadcasted_iota(jnp.int32, (tile, LANES), 0) + step * tile
    lane = lax.broadcasted_iota(jnp.int32, (tile, LANES), 1)
    doc_lane = functools.reduce(
        jnp.add, [(row >= first_ref[1 + item]).astype(jnp.int32) for item in range(DOCS - 1)], DOC_LANE
    )
    query_extra = (lane == doc_lane).astype(F32)
    other = (lane >= DOC_LANE) & (lane < DOC_LANE + DOCS) & (lane != doc_lane)
    ones = ((lane >= LSE_LANE) & (lane < LSE_LANE + 3)) | ((lane >= ONE_LANE) & (lane < ONE_LANE + 3))
    pair_extra = jnp.where(other, -BIG, ones.astype(F32))
    for head in range(heads):
        lanes = slice(head * LANES, (head + 1) * LANES)
        q_rows[head, here, :] = query_wide[:, lanes] + query_extra
        kv_rows[head, here, :] = pair_wide[:, lanes] + pair_extra


def project(first, tokens, gain, shift, weights, bias, bits):
    rows, width = tokens.shape
    feats = weights.shape[1]
    heads = feats // HEAD_DIM
    tile = min(rows, 512)
    tiles = rows // tile
    row_spec = View((tile, width), lambda i, place: (jnp.minimum(i, tiles - 1), 0))
    shape = (heads, rows, LANES)
    messages = [(heads, rows >> (bit + 1), LANES) for bit in range(bits)]
    return call(
        project_kernel,
        grid=(tiles + heads,),
        in_specs=[
            SMALL_SPEC, row_spec, full_spec((1, width)), full_spec((1, width)), full_spec(weights.shape),
            full_spec(bias.shape), full_spec((rows, LANES)),
            full_spec((feats, heads * LANES)), full_spec((feats, heads * LANES)),
        ],
        out_specs=[row_spec]
        + [
            View((1, *item[1:]), lambda i, place: (jnp.maximum(i - tiles, 0), 0, 0)) for item in (shape, shape, *messages)
        ],
        out_shape=[
            jax.ShapeDtypeStruct((rows, width), BF16),
        ]
        + [jax.ShapeDtypeStruct(item, BF16) for item in (shape, shape, *messages)],
        scratch_shapes=[pltpu.VMEM(shape, F32), pltpu.VMEM(shape, F32)],
        name="project",
    )(
        first, tokens, gain, shift, weights, bias, level_columns(rows),
        spread_table(heads, 0), spread_table(heads, VALUE_LANE),
    )


def group_of(distance):
    return distance.bit_length()


def message_layout(rows, bits):
    direct = [1] + list(range(2, 1 << bits, 2)) if bits else []
    layout = [((item, 0, rows >> group_of(item)),) for item in direct]
    passed, offset = [], 0
    for item in direct[1:]:
        passed.append((item + 1, offset, rows >> group_of(item)))
        offset += rows >> group_of(item)
    return tuple(layout + [tuple(passed)]) if passed else tuple(layout)


def far_pieces(layout, refs):
    return [(ref, *entry) for ref, entries in zip(refs, layout) for entry in entries]


def attend_own_kernel(q_ref, kv_ref, count_ref, out_ref):
    rows = q_ref.shape[1]
    tile = min(rows, 512)
    for low in range(0, rows, tile):
        there = slice(low, low + tile)
        scores = dot_nt(q_ref[0, there, :] + count_ref[0, there, :], kv_ref[0])
        peak = jnp.max(scores, axis=-1, keepdims=True)
        total = dot_nn(jnp.exp2(scores - peak).astype(BF16), kv_ref[0])
        lane = lax.broadcasted_iota(jnp.int32, total.shape, 1)
        out_ref[0, there, :] = jnp.where(lane == 0, peak, total)


def attend_own(queries, pairs, counts):
    heads, rows, _ = queries.shape
    return call(
        attend_own_kernel,
        grid=(heads,),
        in_specs=[head_spec(rows), head_spec(rows), full_spec(counts.shape)],
        out_specs=head_spec(rows),
        out_shape=jax.ShapeDtypeStruct((heads, rows, LANES), F32),
        name="attend_own",
    )(queries, pairs, counts)


def attend_far_kernel(layout, first_ref, q_ref, own_ref, count_ref, gather_ref, *refs):
    pieces_all = far_pieces(layout, refs[: len(layout)])
    out_ref, mine_ref, theirs_ref, placed = refs[len(layout) :]
    head = pl.program_id(0)
    rows = q_ref.shape[1]
    block = rows // STRIDE
    turn = (first_ref[0] + head) & (STRIDE - 1)
    counts = [count for _, _, _, count in pieces_all]
    keys = [ref[0, offset : offset + count, :] for ref, _, offset, count in pieces_all]
    scores = [
        dot_nt(q_ref[0, :count, :] + count_ref[group_of(distance) - 1, :count, :], key)
        for key, (_, distance, _, count) in zip(keys, pieces_all)
    ]
    peaks = [jnp.max(item, axis=-1, keepdims=True) for item in scores]
    edges = sorted({0, rows, *counts})
    tiles = list(zip(edges[:-1], edges[1:]))
    own_peaks = [own_ref[0, low:high, 0:1] for low, high in tiles]
    tops = [
        functools.reduce(jnp.maximum, [peak[low:high] for peak, count in zip(peaks, counts) if low < count], own)
        for (low, high), own in zip(tiles, own_peaks)
    ]
    terms = []
    for score, key, count in zip(scores, keys, counts):
        top = [item for item, (low, _) in zip(tops, tiles) if low < count]
        top = top[0] if len(top) == 1 else jnp.concatenate(top, axis=0)
        terms.append(dot_nn(jnp.exp2(score - top).astype(BF16), key))
    for (low, high), own, top in zip(tiles, own_peaks, tops):
        total = own_ref[0, low:high, :]
        near = [term[low:high] for term, count in zip(terms, counts) if low < count]
        if near:
            total = functools.reduce(jnp.add, near, total * jnp.exp2(own - top))
        mass = total[:, ONE_LANE : ONE_LANE + 1]
        result = total * (1.0 / mass)
        lane = lax.broadcasted_iota(jnp.int32, result.shape, 1)
        out_ref[0, low:high, :] = jnp.where(lane == 0, top + jnp.log2(mass), result)
        for offset in range(low, high, block):
            start = bit_reversed(offset // block) ^ turn
            placed[head, pl.ds(start, block, stride=STRIDE), :] = result[offset - low : offset - low + block]

    @pl.when(head == pl.num_programs(0) - 1)
    def _():
        half = rows // 2
        for side, ref in enumerate((mine_ref, theirs_ref)):
            here = pl.ds(pl.multiple_of(((first_ref[HEADS_PLACE] & 1) ^ side) * half, half), half)
            ref[...] = functools.reduce(
                jnp.add,
                [
                    dot_nn(placed[item, here, :].astype(BF16), gather_ref[item * LANES : (item + 1) * LANES])
                    for item in range(placed.shape[0])
                ],
            ).astype(BF16)


def attend_far(first, queries, own, far, layout, counts):
    heads, rows, _ = queries.shape
    feats = heads * HEAD_DIM
    gather = spread_table(heads, VALUE_LANE).T.copy()
    return call(
        functools.partial(attend_far_kernel, layout),
        grid=(heads,),
        in_specs=[SMALL_SPEC, head_spec(rows), head_spec(rows), full_spec(counts.shape), full_spec(gather.shape)]
        + [loose(head_spec(item.shape[1])) for item in far],
        out_specs=[head_spec(rows), full_spec((rows // 2, feats)), full_spec((rows // 2, feats))],
        out_shape=[
            jax.ShapeDtypeStruct((heads, rows, LANES), F32),
            jax.ShapeDtypeStruct((rows // 2, feats), BF16),
            jax.ShapeDtypeStruct((rows // 2, feats), BF16),
        ],
        scratch_shapes=[pltpu.VMEM((heads, rows, LANES), F32)],
        name="attend_far",
    )(first, queries, own, counts, gather, *far)


def three_parts(values):
    high = values.astype(BF16).astype(F32)
    middle = (values - high).astype(BF16).astype(F32)
    return high, middle, values - high - middle


def pair_grads(keys, query, counted, grad):
    prob = jnp.exp2(dot_nt(keys, counted))
    slope = (prob * dot_nt(keys, grad)).astype(BF16)
    return dot_nn(prob.astype(BF16), grad) + dot_nn(slope, query), dot_tn(slope, keys)


def back_far_kernel(layout, pieces, place_ref, q_ref, out_ref, count_ref, spread_ref, *refs):
    grad_refs = refs[:pieces]
    far = far_pieces(layout, refs[pieces : pieces + len(layout)])
    query, grad, dq_ref = refs[pieces + len(layout) : pieces + len(layout) + 3]
    rows_half = q_ref.shape[1] // 2
    *message_refs, wide = refs[pieces + len(layout) + 3 :]
    targets = []
    for index, entries in enumerate(layout):
        passed = index == len(message_refs)
        for _, offset, _ in entries:
            targets.append((message_refs[0], rows_half + offset) if passed else (message_refs[index], 0))
    head = pl.program_id(0)
    rows = q_ref.shape[1]
    block = rows // STRIDE
    part = grad_refs[0].shape[0]
    turn = (place_ref[0] + head) & (STRIDE - 1)

    @pl.when(head == 0)
    def _():
        for index, ref in enumerate(grad_refs):
            start = pl.multiple_of(place_ref[PART_PLACE + index], part)
            for item in range(wide.shape[0]):
                wide[item, pl.ds(start, part), :] = dot_nn(ref[...], spread_ref[:, item * LANES : (item + 1) * LANES])

    for item in range(STRIDE):
        there = slice(item * block, (item + 1) * block)
        start = bit_reversed(item) ^ turn
        rows_grad = wide[head, pl.ds(start, block, stride=STRIDE), :]
        rows_out = out_ref[0, there, :]
        lane = lax.broadcasted_iota(jnp.int32, rows_grad.shape, 1)
        rows_query = q_ref[0, there, :].astype(F32)
        parts = three_parts(jnp.sum(rows_grad * rows_out, axis=-1, keepdims=True))
        for index, value in enumerate(parts):
            rows_grad = jnp.where(lane == ONE_LANE + index, -value, rows_grad)
        for index, value in enumerate(three_parts(rows_out[:, 0:1])):
            rows_query = jnp.where(lane == LSE_LANE + index, -value, rows_query)
        grad[0, there, :] = rows_grad.astype(BF16)
        query[0, there, :] = rows_query.astype(BF16)

    dq_ref[...] = jnp.zeros_like(dq_ref)
    for (ref, distance, offset, count), (dref, doffset) in zip(far, targets):
        counted = query[0, :count, :] + count_ref[group_of(distance) - 1, :count, :]
        step = min(count, 256)
        for low in range(offset, offset + count, step):
            dkv, dq = pair_grads(ref[0, low : low + step, :], query[0, :count, :], counted, grad[0, :count, :])
            there = slice(doffset + low - offset, doffset + low - offset + step)
            dref[0, there, :] = dkv.astype(BF16)
            dq_ref[0, :count, :] += dq


def back_far(places, grads, queries, outs, far, layout, counts):
    heads, rows, _ = queries.shape
    spread = spread_table(heads, VALUE_LANE)
    limit = rows // 2 if layout else rows // STRIDE
    messages = [sum(item[2] for item in entries) for entries in layout]
    if len(messages) > 1:
        messages = [messages[0] + messages[-1]] + messages[1:-1]
    messages = [(heads, count, LANES) for count in messages]
    return call(
        functools.partial(back_far_kernel, layout, len(grads)),
        grid=(heads,),
        in_specs=[SMALL_SPEC, head_spec(rows), head_spec(rows), full_spec(counts.shape), full_spec(spread.shape)]
        + [near(full_spec(item.shape)) for item in grads]
        + [loose(head_spec(item.shape[1])) for item in far],
        out_specs=[head_spec(rows), head_spec(rows), head_spec(limit)] + [head_spec(item[1]) for item in messages],
        out_shape=[
            jax.ShapeDtypeStruct((heads, rows, LANES), BF16),
            jax.ShapeDtypeStruct((heads, rows, LANES), BF16),
            jax.ShapeDtypeStruct((heads, limit, LANES), F32),
        ]
        + [jax.ShapeDtypeStruct(item, BF16) for item in messages],
        scratch_shapes=[pltpu.VMEM((heads, rows, LANES), F32)],
        name="back_far",
    )(places, queries, outs, counts, spread, *grads, *far)


def back_own_kernel(query, grad, kv_ref, count_ref, dq_far_ref, dq_ref, dkv_ref):
    rows = kv_ref.shape[1]
    limit = dq_far_ref.shape[1]
    counted = query[0] + count_ref[0]
    tile = min(rows, 256)
    for low in range(0, rows, tile):
        there = slice(low, low + tile)
        dkv, dq = pair_grads(kv_ref[0, there, :], query[0], counted, grad[0])
        dkv_ref[0, there, :] = dkv
        if low == 0:
            dq_ref[0] = dq
        else:
            dq_ref[0] += dq
    dq_ref[0, :limit, :] += dq_far_ref[0]


def back_own(queries, grads, pairs, counts, dq_far):
    heads, rows, _ = queries.shape
    return call(
        back_own_kernel,
        grid=(heads,),
        in_specs=[head_spec(rows)] * 3 + [full_spec(counts.shape), head_spec(dq_far.shape[1])],
        out_specs=[near(head_spec(rows))] * 2,
        out_shape=[jax.ShapeDtypeStruct((heads, rows, LANES), F32)] * 2,
        name="back_own",
    )(queries, grads, pairs, counts, dq_far)


def collect_kernel(counts, peers, first_ref, dq_ref, dkv_ref, gather_k_ref, gather_v_ref, w_ref, *refs):
    far_refs = refs[: len(counts)]
    *three_refs, term_ref = refs[len(counts) : len(counts) + 4]
    q_rows, kv_rows = refs[-2:]
    head = pl.program_id(0)
    rows = dq_ref.shape[1]
    part = rows // peers
    block = rows // STRIDE
    turn = (first_ref[0] + head) & (STRIDE - 1)
    for item in range(STRIDE):
        there = slice(item * block, (item + 1) * block)
        start = bit_reversed(item) ^ turn
        pair = dkv_ref[0, there, :]
        for ref, count in zip(far_refs, counts):
            if item * block < count:
                pair = pair + ref[0, there, :].astype(F32)
        lane = lax.broadcasted_iota(jnp.int32, pair.shape, 1)
        q_rows[head, pl.ds(start, block, stride=STRIDE), :] = dq_ref[0, there, :] * SCALE
        kv_rows[head, pl.ds(start, block, stride=STRIDE), :] = jnp.where(lane < VALUE_LANE, pair * LN2, pair)

    @pl.when(head == pl.num_programs(0) - 1)
    def _():
        total = [None] * 3
        for item in range(q_rows.shape[0]):
            lanes = slice(item * LANES, (item + 1) * LANES)
            query = q_rows[item].astype(BF16)
            pair = kv_rows[item].astype(BF16)
            terms = (
                dot_nn(query, gather_k_ref[lanes]),
                dot_nn(pair, gather_k_ref[lanes]),
                dot_nn(pair, gather_v_ref[lanes]),
            )
            total = [term if old is None else old + term for old, term in zip(total, terms)]
        for ref, value in zip(three_refs, total):
            ref[...] = value.astype(BF16)
        for peer in range(peers):
            start = (peer & 1) * (rows // 2) + (peer >> 1) * part
            here = slice(start, start + part)
            term_ref[peer * part : (peer + 1) * part, :] = functools.reduce(
                jnp.add, [dot_nn(ref[here, :], w_ref[item]) for item, ref in enumerate(three_refs)]
            ).astype(BF16)


def collect(places, dq, dkv, far, weights, peers):
    heads, rows, _ = dq.shape
    feats, width = weights.shape[1:]
    gather_k = spread_table(heads, 0).T.copy()
    gather_v = spread_table(heads, VALUE_LANE).T.copy()
    return call(
        functools.partial(collect_kernel, [count for _, count in far], peers),
        grid=(heads,),
        in_specs=[
            SMALL_SPEC, near(head_spec(rows)), near(head_spec(rows)), full_spec(gather_k.shape), full_spec(gather_v.shape),
            full_spec(weights.shape),
        ]
        + [near(head_spec(item.shape[1])) for item, _ in far],
        out_specs=[near(full_spec((rows, feats)))] * 3 + [full_spec((rows, width))],
        out_shape=[jax.ShapeDtypeStruct((rows, feats), BF16)] * 3
        + [jax.ShapeDtypeStruct((rows, width), BF16)],
        scratch_shapes=[pltpu.VMEM((heads, rows, LANES), F32), pltpu.VMEM((heads, rows, LANES), F32)],
        name="collect",
    )(places, dq, dkv, gather_k, gather_v, weights, *[item for item, _ in far])


def bring_kernel(*refs):
    count = len(refs) // 2
    for source, target in zip(refs[:count], refs[count:]):
        target[...] = source[...]


def bring(arrays):
    return call(
        bring_kernel,
        grid=(1,),
        in_specs=[loose(full_spec(item.shape)) for item in arrays],
        out_specs=[near(full_spec(item.shape)) for item in arrays],
        out_shape=[jax.ShapeDtypeStruct(item.shape, item.dtype) for item in arrays],
        name="bring",
    )(*arrays)


def pick(core, low, high):
    return jnp.where(core == 0, low, high), jnp.where(core == 0, high, low)


def halves(array):
    half = array.shape[-1] // 2
    return array[:, :half], array[:, half:]


FETCHED = 2
BIAS_ROWS = 16


def fetched_weights(refs, up_shape, down_shape):
    sides = []
    for ref in refs:
        count = up_shape[0] // 2
        down = ref[count : 2 * count].reshape(down_shape[0] // 2, down_shape[1])
        bias = ref[2 * count : 2 * count + 1].astype(F32)
        for index in (1, 2):
            bias = bias + ref[2 * count + index : 2 * count + index + 1].astype(F32)
        sides.append((ref.at[:count], down, bias))
    return sides


def feed_kernel(
    place_ref, tok_ref, cot_ref, w_out_ref, b_out_ref, gain_ref, shift_ref, up_ref, down_ref, bias_ref, *refs,
):
    fetched, refs = refs[:FETCHED], refs[FETCHED:]
    (up_one, down_one, bias_other), (up_two, down_two, _) = fetched_weights(fetched, up_ref.shape, down_ref.shape)
    attn_refs = refs[:-10]
    resid_ref, normed_ref, cot_out_ref, h0_ref, h1_ref, p0_ref, p1_ref, da_ref, out_ref, sums_ref = refs[-10:]
    feats = attn_refs[0].shape[1]
    core = place_ref[SEQ_PLACE] & 1
    resid = tok_ref[...].astype(F32) + b_out_ref[...]
    for index, ref in enumerate(attn_refs):
        here = pl.ds(pl.multiple_of((place_ref[HEADS_PLACE] ^ index) * feats, feats), feats)
        resid = resid + dot_nn(ref[...], w_out_ref[here, :])
    resid_ref[0] = resid
    normed = norm_rows(resid, gain_ref[...], shift_ref[...]).astype(BF16)
    normed_ref[0] = normed
    cot = cot_ref[...]
    cot_out_ref[0] = cot
    normed_pair = pick(core, *halves(normed))
    pres = (
        dot_nn(normed, up_ref[...]) + bias_ref[...],
        dot_nn(normed_pair[0], up_one[...]) + dot_nn(normed_pair[1], up_two[...]) + bias_other,
    )
    acts = (
        dot_nt(cot, down_ref[...]),
        jnp.concatenate(pick(core, dot_nt(cot, down_one[...]), dot_nt(cot, down_two[...])), axis=1),
    )
    grads = []
    for pre, act, h_ref, p_ref in zip(pres, acts, (h0_ref, h1_ref), (p0_ref, p1_ref)):
        share = 0.5 * (1.0 + lax.erf(pre * math.sqrt(0.5)))
        h_ref[0] = (pre * share).astype(BF16)
        slope = share + pre * jnp.exp(-0.5 * pre * pre) * (1.0 / math.sqrt(2.0 * math.pi))
        grads.append((act * slope).astype(BF16))
        p_ref[0] = grads[-1]
    other = pick(core, dot_nt(grads[1], up_one[...]), dot_nt(grads[1], up_two[...]))
    da_ref[0] = (dot_nt(grads[0], up_ref[...]) + jnp.concatenate(other, axis=1)).astype(da_ref.dtype)
    hidden_pair = pick(core, *halves(h1_ref[0]))
    out_ref[0] = (
        dot_nn(h0_ref[0], down_ref[...])
        + dot_nn(hidden_pair[0], down_one[...])
        + dot_nn(hidden_pair[1], down_two[...])
    ).astype(out_ref.dtype)
    ones = jnp.ones((8, cot.shape[0]), BF16)
    sums_ref[0, 0] = dot_nn(ones, grads[0])
    sums_ref[0, 1] = dot_nn(ones, grads[1])


def feed(places, block, piece_cut, steps, kind, tokens, cotangent, w_out, b_out, gain, shift, up, down, bias, fetched, attns):
    rows, width = tokens.shape
    hidden = up.shape[1]
    feats = attns[0].shape[1]
    inner = attns[0].shape[0] // block
    first = steps[0]

    def piece(i, place):
        return ((place[HEADS_PLACE] >> 1) ^ (i + first)) * piece_cut[1] + piece_cut[0]

    def row_block(i, place):
        return ((place[HEADS_PLACE] & 1) * inner + piece(i, place), 0)

    def stacked(columns):
        return View((1, block, columns), lambda i, place: (i, 0, 0))

    constants = (w_out, b_out, gain, shift, up, down, bias)
    outs = [(width, F32), (width, BF16), (width, BF16)] + [(hidden, BF16)] * 4 + [(width, kind)] * 2
    count = len(steps)
    return call(
        feed_kernel,
        grid=(count,),
        in_specs=[SMALL_SPEC]
        + [View((block, width), row_block)] * 2
        + [
            near(full_spec(item.shape)) if item.size >= width * feats else full_spec(item.shape)
            for item in (*constants, *fetched)
        ]
        + [View((block, feats), lambda i, place: (piece(i, place), 0))] * len(attns),
        out_specs=[near(stacked(columns)) for columns, _ in outs]
        + [View((1, 2, 8, hidden), lambda i, place: (i, 0, 0, 0))],
        out_shape=[jax.ShapeDtypeStruct((count, block, columns), dtype) for columns, dtype in outs]
        + [jax.ShapeDtypeStruct((count, 2, 8, hidden), F32)],
        name="feed",
    )(places, tokens, cotangent, *constants, *fetched, *attns)


def outer_kernel(pairs, parts, place_ref, *refs):
    ins, (keep_ref, give_ref) = refs[:-2], refs[-2:]
    step = pl.program_id(0)
    core = place_ref[SEQ_PLACE] & 1
    for index in range(pairs):

        @pl.when(step == index)
        def _():
            total = None
            first = 2 * parts * index
            for left_ref, right_ref in zip(ins[first : first + parts], ins[first + parts : first + 2 * parts]):
                for item in range(left_ref.shape[0]):
                    left = pick(core, *halves(left_ref[item]))
                    terms = [dot_tn(side, right_ref[item]) for side in left]
                    total = terms if total is None else [old + term for old, term in zip(total, terms)]
            keep_ref[0] = total[0].astype(BF16)
            give_ref[0] = total[1].astype(BF16)


def outer_sums(places, pairs):
    lefts = pairs[0][0][0].shape[2] // 2
    rights = pairs[0][1][0].shape[2]
    arrays = [item for pair in pairs for side in pair for item in side]
    spec = View((1, lefts, rights), lambda i, place: (i, 0, 0))
    shape = jax.ShapeDtypeStruct((len(pairs), lefts, rights), BF16)
    return call(
        functools.partial(outer_kernel, len(pairs), len(pairs[0][0])),
        grid=(len(pairs),),
        in_specs=[SMALL_SPEC] + [near(full_spec(item.shape)) for item in arrays],
        out_specs=[spec, near(spec)],
        out_shape=[shape, shape],
        name="outer_sums",
    )(places, *arrays)


def out_grads_kernel(place_ref, low_ref, *refs):
    *attn_refs, keep_ref, give_ref = refs
    half = attn_refs[0].shape[1] // 2
    core = place_ref[SEQ_PLACE] & 1
    bits = len(attn_refs).bit_length() - 1
    for distance, ref in enumerate(attn_refs):
        index = sum(((distance >> bit) & 1) << (bits - 1 - bit) for bit in range(bits))
        product = dot_tn(ref[...], low_ref[...])
        keep, give = pick(core, product[:half], product[half:])
        keep_ref[index] = keep.astype(BF16)
        give_ref[index] = give.astype(BF16)


def out_grads(places, low, attns):
    part, width = low.shape
    feats = attns[0].shape[1]
    shape = (len(attns), feats // 2, width)
    return call(
        out_grads_kernel,
        grid=(1,),
        in_specs=[SMALL_SPEC, near(full_spec((part, width)))]
        + [View((part, feats), lambda i, place: (place[HEADS_PLACE] >> 1, 0))] * len(attns),
        out_specs=[near(full_spec(shape))] * 2,
        out_shape=[jax.ShapeDtypeStruct(shape, BF16)] * 2,
        name="out_grads",
    )(places, low, *attns)


def tail_kernel(normed_ref, tok_ref, w_ref, _, stats_ref, up_ref, *refs):
    *three_refs, out_ref, sums_ref = refs
    rows, width = normed_ref.shape
    feats = three_refs[0].shape[1]
    hidden = up_ref.shape[1]
    for index, ref in enumerate(three_refs):
        out_ref[index * feats : (index + 1) * feats, :] = dot_tn(ref[...], normed_ref[...]).astype(BF16)
    gain = jnp.zeros((1, width), F32)
    shift = jnp.zeros((1, width), F32)
    tile = min(rows, 256)
    for low in range(0, rows, tile):
        here = slice(low, low + tile)
        term = functools.reduce(
            jnp.add, [dot_nn(ref[here, :], w_ref[index]) for index, ref in enumerate(three_refs)]
        )
        center = tok_ref[here, :].astype(F32)
        center = center - jnp.mean(center, axis=-1, keepdims=True)
        unit = center * lax.rsqrt(jnp.mean(center * center, axis=-1, keepdims=True) + EPSILON)
        gain = gain + column_sums(term * unit)
        shift = shift + column_sums(term)
    row = lax.broadcasted_iota(jnp.int32, (SUM_ROWS, width), 0)
    other = up_ref[1:2, :]
    if hidden < width:
        other = jnp.concatenate([other, jnp.zeros((1, width - hidden), F32)], axis=1)
    lines = (gain, stats_ref[0:1], shift, stats_ref[1:2], stats_ref[2:3], stats_ref[3:4], other)
    block = jnp.zeros((SUM_ROWS, width), F32)
    for index, line in enumerate(lines):
        block = jnp.where(row == index, line, block)
    sums_ref[:SUM_ROWS, :] = block.astype(BF16)
    sums_ref[SUM_ROWS:, :] = jnp.zeros((3 * SUM_ROWS, width), BF16)
    ones = jnp.ones((SUM_ROWS, rows), BF16)
    own = jnp.broadcast_to(up_ref[0:1, :], (SUM_ROWS, hidden))
    for index, value in enumerate((own, dot_nn(ones, three_refs[0][...]), dot_nn(ones, three_refs[2][...]))):
        here = (index + 1) * SUM_ROWS
        sums_ref[here : here + SUM_ROWS, : value.shape[1]] = value.astype(BF16)


SUM_ROWS = 16


def tail_grads(normed, tokens, weights, earlier, stats, ups, three):
    rows, width = normed.shape
    feats = three[0].shape[1]
    ins = (normed, tokens, weights, stats, ups, *three)
    specs = [full_spec(item.shape) for item in ins[:5]] + [near(full_spec(item.shape)) for item in three]
    ins = (*ins[:3], earlier, *ins[3:])
    return call(
        tail_kernel,
        grid=(1,),
        in_specs=[*specs[:3], View((1, 16, LANES), lambda step, place: (0, 0, 0)), *specs[3:]],
        out_specs=[near(full_spec((3 * feats, width))), near(full_spec((4 * SUM_ROWS, width)))],
        out_shape=[jax.ShapeDtypeStruct((count, width), BF16) for count in (3 * feats, 4 * SUM_ROWS)],
        name="tail_grads",
    )(*ins)


def pack_kernel(core_ref, up_ref, down_ref, bias_ref, out_ref):
    count = up_ref.shape[0]
    out_ref[:count, :] = up_ref[...]
    out_ref[count : 2 * count, :] = down_ref[...]
    row = lax.broadcasted_iota(jnp.int32, (BIAS_ROWS, bias_ref.shape[1]), 0)
    block = jnp.zeros(row.shape, F32)
    for index, line in enumerate(three_parts(bias_ref[...])):
        block = jnp.where(row == index, line, block)
    out_ref[2 * count :, :] = block.astype(BF16)


def pack_weights(core, up, down, bias):
    hidden = up.shape[1]
    shape = (up.shape[0] + BIAS_ROWS, hidden)
    if up.shape != down.shape:
        cuts = [
            lax.dynamic_slice_in_dim(item, core * (item.shape[0] // 2), item.shape[0] // 2).reshape(-1, hidden)
            for item in (up, down)
        ]
        zeros = jnp.zeros((BIAS_ROWS - 3, hidden), F32)
        return jnp.concatenate([*cuts, jnp.concatenate([*three_parts(bias), zeros]).astype(BF16)])
    return call(
        pack_kernel,
        grid=(1,),
        in_specs=[SMALL_SPEC]
        + [View((up.shape[0] // 2, hidden), lambda i, place: (place[0], 0))] * 2
        + [full_spec(bias.shape)],
        out_specs=full_spec(shape),
        out_shape=jax.ShapeDtypeStruct(shape, BF16),
        name="pack_weights",
    )(core.reshape(1), up, down, bias)


def column_sums(array):
    return jnp.sum(array, axis=0, keepdims=True)


def turn_kernel(received, place_ref, resid_ref, cot_ref, da_ref, w_out_ref, gain_ref, *refs):
    more_refs = refs[:received]
    dres_ref, low_ref, stats_ref, *grad_refs = refs[received:]
    feats = grad_refs[0].shape[1]
    total = da_ref[0]
    block = more_refs[0].shape[0]
    blocks = total.shape[0] // block
    more = [ref[...].astype(F32) for ref in more_refs]
    total = total + jnp.concatenate(
        [functools.reduce(jnp.add, more[index::blocks]) for index in range(blocks)], axis=0
    )
    cot = cot_ref[0].astype(F32)
    grad_n, gain_sum, shift_sum = norm_back(resid_ref[0], gain_ref[...], total)
    dres = cot + grad_n
    dres_ref[...] = dres
    low = dres.astype(BF16)
    low_ref[...] = low
    for index, ref in enumerate(grad_refs):
        here = pl.ds(pl.multiple_of((place_ref[HEADS_PLACE] ^ index) * feats, feats), feats)
        ref[...] = dot_nt(low, w_out_ref[here, :]).astype(BF16)
    stats_ref[0:1] = gain_sum
    stats_ref[1:2] = shift_sum
    stats_ref[2:3] = column_sums(dres)
    stats_ref[3:4] = column_sums(cot)
    stats_ref[4:8] = jnp.zeros_like(stats_ref[4:8])


def turn_back(places, resid, cot, gain, da, more, w_out, peers):
    _, part, width = resid.shape
    feats = width // peers
    ins = (resid, cot, da, w_out, gain)
    return call(
        functools.partial(turn_kernel, len(more)),
        grid=(1,),
        in_specs=[SMALL_SPEC]
        + [near(full_spec(item.shape)) for item in ins[:4]]
        + [full_spec(item.shape) for item in ins[4:]]
        + [near(full_spec(item.shape)) for item in more],
        out_specs=[full_spec((part, width)), near(full_spec((part, width))), full_spec((8, width))]
        + [near(full_spec((part, feats)))] * peers,
        out_shape=[
            jax.ShapeDtypeStruct((part, width), F32),
            jax.ShapeDtypeStruct((part, width), BF16),
            jax.ShapeDtypeStruct((8, width), F32),
        ]
        + [jax.ShapeDtypeStruct((part, feats), BF16)] * peers,
        name="turn_back",
    )(places, *ins, *more)


def finish_kernel(place_ref, tok_ref, gain_ref, term_ref, dres_ref, grad_ref):
    grad_n, _, _ = norm_back(tok_ref[...].astype(F32), gain_ref[...], term_ref[...].astype(F32))
    grad_ref[...] = (dres_ref[...] + grad_n).astype(BF16)


def finish(places, tokens, gain, term, dres):
    part, width = term.shape
    return call(
        finish_kernel,
        grid=(1,),
        in_specs=[SMALL_SPEC, View((part, width), lambda i, place: (place[PART_PLACE] // part, 0))]
        + [full_spec(item.shape) for item in (gain, term, dres)],
        out_specs=full_spec((part, width)),
        out_shape=jax.ShapeDtypeStruct((part, width), BF16),
        name="finish",
    )(places, tokens, gain, term, dres)


def flipped(array, distance):
    return lax.ppermute(array, "seq", [(i, i ^ distance) for i in range(lax.axis_size("seq"))])


def crossed(array, distance):
    if distance == 0:
        return array
    return lax.ppermute(array, "heads", [(i, i ^ distance) for i in range(lax.axis_size("heads"))])


def added(left, right):
    return (left.astype(F32) + right.astype(F32)).astype(BF16)


def halved(array, axis, bit):
    side = (lax.axis_index("seq") >> bit) & 1
    count = array.shape[axis] // 2
    keep = lax.dynamic_slice_in_dim(array, side * count, count, axis)
    give = lax.dynamic_slice_in_dim(array, (1 - side) * count, count, axis)
    other = flipped(give, 1 << bit)
    return added(keep, other), other


def doubled(array, axis, bit):
    side = (lax.axis_index("seq") >> bit) & 1
    other = flipped(array, 1 << bit)
    whole = jnp.where(side == 0, jnp.concatenate([array, other], axis), jnp.concatenate([other, array], axis))
    return whole, other


def after(value, earlier):
    return lax.optimization_barrier((value, earlier))[0]


def shards(tokens, docs, ln_gain, ln_bias, w_qkv, b_qv, w_out, b_out, w_up, b_up, w_down, b_down, cotangent):
    rows, width = tokens.shape
    feats = w_qkv.shape[3]
    heads = feats // HEAD_DIM
    seq_count = lax.axis_size("seq")
    head_count = lax.axis_size("heads")
    seq_pos = lax.axis_index("seq")
    head_pos = lax.axis_index("heads")
    seq_bits = seq_count.bit_length() - 1
    gains, shifts = ln_gain[0], ln_bias[0]
    half = rows // 2
    part = rows // head_count
    peers = [head_pos ^ distance for distance in range(head_count)]
    part_starts = [(peer & 1) * half + (peer >> 1) * part for peer in peers]
    edges = [jnp.sum((docs <= item).astype(jnp.int32)) - seq_pos * rows for item in range(DOCS - 1)]
    places = jnp.stack(
        [item.astype(jnp.int32) for item in (head_pos * heads, *edges, head_pos, seq_pos, *part_starts)]
    )

    core = seq_pos & 1
    hidden = w_up.shape[2]
    w_out_all = lax.all_gather(w_out[0], "heads", axis=0, tiled=True)
    fetched_one = crossed(pack_weights(core.astype(jnp.int32), w_up[0], w_down[0], b_up), 1)

    w_three = jnp.transpose(w_qkv[0], (1, 2, 0))
    bits = min(seq_bits, TOP)
    normed, queries, pairs, *messages = project(places, tokens, gains[0:1], shifts[0:1], w_three, b_qv[0], bits)
    layout = message_layout(rows, bits)
    counts = count_columns(rows, bits + 1)
    own_counts, far_counts = counts[:1], counts[1:, : rows // 2]
    direct = layout[:-1] if bits > 1 else layout
    far = [flipped(messages[group_of(entries[0][0]) - 1], entries[0][0]) for entries in direct]
    own_outs = attend_own(queries, pairs, own_counts)
    if bits > 1:
        far.append(flipped(after(jnp.concatenate(far[1:], axis=1), own_outs), 1))
    outs, attn_mine, attn_theirs = attend_far(places, queries, own_outs, far, layout, far_counts)
    fetched = [fetched_one, flipped(after(fetched_one, outs), 1)]
    attns = [attn_mine] + [
        crossed(attn_theirs if distance & 1 else attn_mine, distance) for distance in range(1, head_count)
    ]

    def in_rows(array):
        return jnp.concatenate([array[2 * inner + side] for side in range(2) for inner in range(head_count // 2)])

    steps = head_count // 2
    w_out_all, up_here, down_here, *fetched = bring([w_out_all, w_up[0], w_down[0], *fetched])
    shared = (
        tokens, cotangent, w_out_all, b_out, gains[1:2], shifts[1:2], up_here, down_here, b_up, fetched, attns,
    )
    cuts = 2
    sent = [feed(places, part // cuts, (index, cuts), range(1, steps), BF16, *shared) for index in range(cuts)]
    da_more = [crossed(item[7][step - 1], 2 * step) for step in range(1, steps) for item in sent]
    own = feed(places, part, (0, 1), range(0, 1), F32, *shared)
    resid, normed_two, cots, h0, h1, p0, p1, da_two, out_term, up_sums = zip(own, *sent)
    dres, dres_low, stats_two, *grad_attns = turn_back(
        places, resid[0], cots[0], gains[1:2], da_two[0], da_more, w_out_all, head_count
    )
    grad_attns = [crossed(item, distance) for distance, item in enumerate(grad_attns)]
    later = after(places, dres)
    out_keep, out_give = out_grads(later, dres_low, attns)
    later = after(later, out_keep)
    out_core = flipped(after(out_give, grad_attns), 1)
    out_grad = added(out_keep, out_core)
    products = [(normed_two, p0), (h0, cots), (normed_two, p1), (h1, cots)]
    if hidden == width:
        packs = [outer_sums(later, products)]
    else:
        packs = [outer_sums(later, products[0::2]), outer_sums(later, products[1::2])]
    packs = after(packs, grad_attns)

    out_terms = after(jnp.concatenate(out_term[1:], axis=1), grad_attns)
    out_more = [crossed(out_terms[step - 1], 2 * step) for step in range(1, steps)]
    queries_b, grads_b, dq_far, *dfar = back_far(
        after(places, packs), grad_attns, queries, outs, far, layout, far_counts
    )
    out_sum = functools.reduce(jnp.add, [item.astype(F32) for item in after(out_more, dq_far)], out_term[0][0])
    out_part = (resid[0][0] + out_sum + b_down[0]).astype(BF16)
    back = []
    if bits:
        arrived = flipped(after(dfar[0], (out_more, out_core)), 1)
        arrived = after(arrived, out_part)
        offset = rows // 2
        onward = []
        for item in dfar[1:]:
            count = item.shape[1]
            onward.append(added(item, arrived[:, offset : offset + count]))
            offset += count
        queries_b = after(queries_b, onward)
        back = [(arrived, rows // 2)] + [
            (flipped(item, entries[0][0]), item.shape[1]) for entries, item in zip(direct[1:], onward)
        ]
    out_other = crossed(after(out_grad, out_part)[steps:], 1)
    out_grad = added(out_grad[:steps], out_other)
    arrived = [flipped(give, 1) for _, give in after(packs, out_part)]
    packs = [(keep, item) for (keep, _), item in zip(packs, arrived)]
    queries_b, out_part = lax.optimization_barrier((queries_b, out_part))
    gathered = lax.all_gather(out_part, "heads", axis=0)
    output = in_rows(gathered)
    dq, dkv = back_own(queries_b, grads_b, pairs, own_counts, dq_far)
    ups = functools.reduce(jnp.add, [jnp.sum(item[:, :, 0], axis=0) for item in up_sums])
    *grads_three, terms = collect(after(places, (ups, arrived, out_other)), dq, dkv, back, w_three, head_count)
    term = lax.psum_scatter(terms, "heads", scatter_dimension=0, tiled=True)
    orders = [list(range(1, seq_bits))] * 2
    if seq_bits > 2:
        orders[1] = [2, 1] + orders[0][2:]
    packs = [added(*item) for item in after(packs, terms)]
    count = packs[0].shape[1] // 2
    packs = [[item[:, :count], item[:, count:]] for item in packs]
    arrived = []
    for step in range(seq_bits - 1):
        for pack in packs:
            for side, order in enumerate(orders):
                pack[side], other = halved(pack[side], 1, order[step])
                if not step:
                    arrived.append(other)
    packs = [jnp.concatenate(pack, axis=1) for pack in packs]
    distance = 2
    while distance < head_count:
        count = out_grad.shape[0] // 2
        out_grad = added(out_grad[:count], crossed(out_grad[count:], distance))
        distance = 2 * distance
    grad_w_out = out_grad[0]

    rest, sums = tail_grads(normed, tokens, w_three, gathered, stats_two, ups, grads_three)
    count = rest.shape[0] // 2
    keep, give = (lax.dynamic_slice_in_dim(rest, side * count, count) for side in (core, 1 - core))
    rest = added(jnp.concatenate([keep, sums]), flipped(jnp.concatenate([give, sums]), 1))
    rest = jnp.concatenate([rest, grad_w_out])
    cut = rest.shape[0] // 2
    rest = [rest[:cut], rest[cut:]]

    def swap(step):
        others = [flipped(item, 1 << order[step]) for item, order in zip(rest, orders)]
        return [added(item, other) for item, other in zip(rest, others)], others

    others = []
    if seq_bits > 1:
        rest, others = swap(0)
    arrived = (packs, others)
    grad_part = finish(after(places, arrived), tokens, gains[0:1], term, dres)
    grad_tokens = in_rows(lax.all_gather(grad_part, "heads", axis=0)).astype(F32)
    packs, rest = after((packs, rest), grad_part)
    passed = [crossed(item[item.shape[0] // 2 :], 1) for item in packs]
    packs = [added(item[: item.shape[0] // 2], other) for item, other in zip(packs, passed)]
    for step in range(1, seq_bits - 1):
        rest, _ = swap(step)
    rest = jnp.concatenate(rest)
    half_rows = packs[0].shape[1] // 2
    packs = [[item[:, :half_rows], item[:, half_rows:]] for item in packs]
    for step in reversed(range(seq_bits - 1)):
        for pack in packs:
            for side, order in enumerate(orders):
                pack[side], _ = doubled(pack[side], 1, order[step])
    packs = [doubled(jnp.concatenate(pack, axis=1), 1, 0)[0] for pack in packs]
    sums = rest[count : count + 4 * SUM_ROWS]
    rest = jnp.concatenate([rest[:count], rest[count + 4 * SUM_ROWS :]])
    rest = doubled(rest, 0, 0)[0].astype(F32).reshape(2, -1, width)
    grad_w_out = rest[:, count:].reshape(feats, width)
    rest = rest[:, :count]
    more = [crossed(sums[:SUM_ROWS], distance).astype(F32) for distance in range(1, head_count)]
    sums = sums.astype(F32)
    wide = functools.reduce(jnp.add, more, sums[:SUM_ROWS])[:6]
    grad_b_up = sums[SUM_ROWS, :hidden] + more[0][6, :hidden]
    grad_b_qv = jnp.stack([sums[(index + 2) * SUM_ROWS, :feats] for index in range(2)])
    packs = [packs[0][0], packs[0][1]] if hidden == width else [packs[0][0], packs[1][0]]
    grad_w_up, grad_w_down = (item.astype(F32) for item in packs)
    grad_w_qkv = jnp.transpose(rest.reshape(3, feats, width), (2, 0, 1))
    return (
        output, grad_tokens, wide[None, 0:2], wide[None, 2:4], grad_w_qkv[None], grad_b_qv[None],
        grad_w_out[None], wide[4:5], grad_w_up[None], grad_b_up[None], grad_w_down[None], wide[5:6],
    )


def solution(mesh):
    in_specs = (
        P("seq", None), P(), P(), P(), P(None, None, None, "heads"), P(None, None, "heads"),
        P(None, "heads", None), P(), P(None, None, "heads"), P(None, "heads"), P(None, "heads", None), P(),
        P("seq", None),
    )
    out_specs = (
        P("seq", None), P("seq", None), P(), P(), P(None, None, None, "heads"), P(None, None, "heads"),
        P(None, "heads", None), P(), P(None, None, "heads"), P(None, "heads"), P(None, "heads", None), P(),
    )
    return jax.shard_map(shards, mesh=mesh, in_specs=in_specs, out_specs=out_specs, check_vma=False)
```

```python
import functools
import math

import jax
import jax.numpy as jnp
import ml_dtypes
import numpy as np
from jax import lax
from jax.experimental import pallas as pl
from jax.experimental.pallas import tpu as pltpu
from jax.sharding import PartitionSpec as P

HEAD_DIM = 48
BRANCHES = 5
DOCS = 3
TOP = BRANCHES - 1
STRIDE = 2**TOP
LANES = 128
EPSILON = 1e-05
BIG = 2.0**100
SCALE = HEAD_DIM**-0.5
LOG2E = math.log2(math.e)
LN2 = math.log(2.0)
DOC_LANE = HEAD_DIM
MULT_LANE = DOC_LANE + DOCS
LSE_LANE = MULT_LANE + 2 * TOP
VALUE_LANE = LANES // 2
ONE_LANE = VALUE_LANE + HEAD_DIM
F32 = jnp.float32
BF16 = jnp.bfloat16
VMEM_LIMIT = 28 * 1024 * 1024
HEADS_PLACE = DOCS
SEQ_PLACE = DOCS + 1
PART_PLACE = DOCS + 2


class View:
    def __init__(self, shape, index=None, near=False, loose=False):
        self.shape, self.index, self.near, self.loose = tuple(shape), index, near, loose

    def of(self, ref, step, place):
        if not self.near or self.index is None:
            return ref
        cuts = []
        for size, at, whole in zip(self.shape, self.index(step, place), ref.shape):
            cuts.append(pl.ds(0, size) if size == whole else pl.ds(pl.multiple_of(at * size, size), size))
        return ref.at[tuple(cuts)]

    def spec(self):
        if self.near:
            return pl.BlockSpec(memory_space=pltpu.VMEM)
        if self.index is None:
            return pl.BlockSpec(
                self.shape, lambda step, *place: (0,) * len(self.shape), pipeline_mode=pl.Buffered(1)
            )
        return pl.BlockSpec(self.shape, lambda step, *place: self.index(step, place[0] if place else None))


def near(view):
    return View(view.shape, view.index, near=True)


def loose(view):
    return View(view.shape, view.index, loose=True)


def call(kernel, out_shape, grid, in_specs, out_specs, name, scratch_shapes=()):
    single = not isinstance(out_shape, (list, tuple))
    outs = [out_specs] if single else list(out_specs)
    shapes = [out_shape] if single else list(out_shape)
    scalars = int(in_specs[0] is SMALL_SPEC)
    ins = list(in_specs[scalars:])
    views = [*ins, *outs]

    def body(*refs):
        step = pl.program_id(0)
        place = refs[:scalars]
        rest = refs[scalars:]
        shown = [view.of(ref, step, *(place or (None,))) for view, ref in zip(views, rest)]
        kernel(*place, *shown, *rest[len(views) :])

    specs = [item.spec() for item in outs]
    kinds = [
        jax.ShapeDtypeStruct(item.shape, item.dtype) if view.near else pltpu.HBM(item.shape, item.dtype)
        for item, view in zip(shapes, outs)
    ]
    inner = pl.pallas_call(
        body,
        out_shape=kinds[0] if single else kinds,
        grid_spec=pltpu.PrefetchScalarGridSpec(
            num_scalar_prefetch=scalars,
            grid=grid,
            in_specs=[item.spec() for item in ins],
            out_specs=specs[0] if single else specs,
            scratch_shapes=scratch_shapes,
        ),
        compiler_params=pltpu.CompilerParams(vmem_limit_bytes=VMEM_LIMIT),
        name=name,
    )

    def run(*arrays):
        placed = [
            jnp.asarray(item) if view.near or view.loose else pltpu.with_memory_space_constraint(jnp.asarray(item), pltpu.HBM)
            for item, view in zip(arrays[scalars:], ins)
        ]
        return inner(*arrays[:scalars], *placed)

    return run


def bit_reversed(block):
    return sum(((block >> bit) & 1) << (TOP - 1 - bit) for bit in range(TOP))


def level_columns(rows):
    table = np.zeros((rows, LANES), np.float32)
    for level in range(1, TOP + 1):
        table[: rows >> level, MULT_LANE + level - 1] = 1.0
        table[: rows >> level, MULT_LANE + TOP + level - 1] = 1.0
    return table.astype(ml_dtypes.bfloat16)


def count_columns(rows, groups):
    table = np.zeros((groups, rows, LANES), np.float32)
    for group in range(groups):
        for level in range(group + 1, TOP + 1):
            step = math.log2((level - group + 1) / (level - group))
            high = float(np.float32(step).astype(ml_dtypes.bfloat16))
            table[group, : rows >> level, MULT_LANE + level - 1] = high
            table[group, : rows >> level, MULT_LANE + TOP + level - 1] = step - high
    return table.astype(ml_dtypes.bfloat16)


def spread_table(heads, first_lane):
    table = np.zeros((heads * HEAD_DIM, heads * LANES), np.float32)
    for head in range(heads):
        for item in range(HEAD_DIM):
            table[head * HEAD_DIM + item, head * LANES + first_lane + item] = 1.0
    return table.astype(ml_dtypes.bfloat16)


def dot_nn(left, right):
    return jnp.dot(left, right, preferred_element_type=F32)


def dot_nt(left, right):
    return lax.dot_general(left, right, (((1,), (1,)), ((), ())), preferred_element_type=F32)


def dot_tn(left, right):
    return lax.dot_general(left, right, (((0,), (0,)), ((), ())), preferred_element_type=F32)


def norm_rows(values, gain_row, shift_row):
    center = values - jnp.mean(values, axis=-1, keepdims=True)
    spread = jnp.mean(center * center, axis=-1, keepdims=True)
    return center * lax.rsqrt(spread + EPSILON) * gain_row + shift_row


def norm_back(values, gain_row, grad_rows):
    center = values - jnp.mean(values, axis=-1, keepdims=True)
    spread = jnp.mean(center * center, axis=-1, keepdims=True)
    inverse = lax.rsqrt(spread + EPSILON)
    unit = center * inverse
    scaled = grad_rows * gain_row
    grad_in = inverse * (
        scaled
        - jnp.mean(scaled, axis=-1, keepdims=True)
        - unit * jnp.mean(scaled * unit, axis=-1, keepdims=True)
    )
    return grad_in, jnp.sum(grad_rows * unit, axis=0, keepdims=True), jnp.sum(grad_rows, axis=0, keepdims=True)


def full_spec(shape):
    return View(shape)


def head_spec(rows):
    return View((1, rows, LANES), lambda head, place: (head, 0, 0))


SMALL_SPEC = None


def project_kernel(
    first_ref, x_ref, gain_ref, shift_ref, w_ref, bias_ref, level_ref, spread_k_ref, spread_v_ref,
    normed_ref, q_ref, kv_ref, *refs,
):
    *message_refs, q_rows, kv_rows = refs
    step = pl.program_id(0)
    tile = x_ref.shape[0]
    heads, rows = q_rows.shape[0], q_rows.shape[1]
    block = rows // STRIDE
    tiles = rows // tile

    @pl.when(step < tiles)
    def _():
        project_rows(
            step, first_ref, x_ref, gain_ref, shift_ref, w_ref, bias_ref, spread_k_ref, spread_v_ref, normed_ref, q_rows, kv_rows
        )

    @pl.when(step >= tiles)
    def _():
        head = step - tiles
        turn = (first_ref[0] + head) & (STRIDE - 1)
        for item in range(STRIDE):
            start = bit_reversed(item) ^ turn
            there = slice(item * block, (item + 1) * block)
            q_ref[0, there, :] = q_rows[head, pl.ds(start, block, stride=STRIDE), :].astype(BF16)
            pair = (kv_rows[head, pl.ds(start, block, stride=STRIDE), :] + level_ref[there, :].astype(F32)).astype(BF16)
            kv_ref[0, there, :] = pair
            for ref in message_refs:
                if item * block < ref.shape[1]:
                    ref[0, there, :] = pair


def project_rows(
    step, first_ref, x_ref, gain_ref, shift_ref, w_ref, bias_ref, spread_k_ref, spread_v_ref, normed_ref, q_rows, kv_rows
):
    tile = x_ref.shape[0]
    heads = q_rows.shape[0]
    normed = norm_rows(x_ref[...].astype(F32), gain_ref[...], shift_ref[...]).astype(BF16)
    normed_ref[...] = normed
    query = ((dot_nt(normed, w_ref[0]) + bias_ref[0:1]) * (SCALE * LOG2E)).astype(BF16)
    key = dot_nt(normed, w_ref[1]).astype(BF16)
    value = (dot_nt(normed, w_ref[2]) + bias_ref[1:2]).astype(BF16)
    query_wide = dot_nn(query, spread_k_ref[...])
    pair_wide = dot_nn(key, spread_k_ref[...]) + dot_nn(value, spread_v_ref[...])
    here = pl.ds(pl.multiple_of(step * tile, tile), tile)
    row = lax.broadcasted_iota(jnp.int32, (tile, LANES), 0) + step * tile
    lane = lax.broadcasted_iota(jnp.int32, (tile, LANES), 1)
    doc_lane = functools.reduce(
        jnp.add, [(row >= first_ref[1 + item]).astype(jnp.int32) for item in range(DOCS - 1)], DOC_LANE
    )
    query_extra = (lane == doc_lane).astype(F32)
    other = (lane >= DOC_LANE) & (lane < DOC_LANE + DOCS) & (lane != doc_lane)
    ones = ((lane >= LSE_LANE) & (lane < LSE_LANE + 3)) | ((lane >= ONE_LANE) & (lane < ONE_LANE + 3))
    pair_extra = jnp.where(other, -BIG, ones.astype(F32))
    for head in range(heads):
        lanes = slice(head * LANES, (head + 1) * LANES)
        q_rows[head, here, :] = query_wide[:, lanes] + query_extra
        kv_rows[head, here, :] = pair_wide[:, lanes] + pair_extra


def project(first, tokens, gain, shift, weights, bias, bits):
    rows, width = tokens.shape
    feats = weights.shape[1]
    heads = feats // HEAD_DIM
    tile = min(rows, 512)
    tiles = rows // tile
    row_spec = View((tile, width), lambda i, place: (jnp.minimum(i, tiles - 1), 0))
    shape = (heads, rows, LANES)
    messages = [(heads, rows >> (bit + 1), LANES) for bit in range(bits)]
    return call(
        project_kernel,
        grid=(tiles + heads,),
        in_specs=[
            SMALL_SPEC, row_spec, full_spec((1, width)), full_spec((1, width)), full_spec(weights.shape),
            full_spec(bias.shape), full_spec((rows, LANES)),
            full_spec((feats, heads * LANES)), full_spec((feats, heads * LANES)),
        ],
        out_specs=[row_spec]
        + [
            View((1, *item[1:]), lambda i, place: (jnp.maximum(i - tiles, 0), 0, 0)) for item in (shape, shape, *messages)
        ],
        out_shape=[
            jax.ShapeDtypeStruct((rows, width), BF16),
        ]
        + [jax.ShapeDtypeStruct(item, BF16) for item in (shape, shape, *messages)],
        scratch_shapes=[pltpu.VMEM(shape, F32), pltpu.VMEM(shape, F32)],
        name="project",
    )(
        first, tokens, gain, shift, weights, bias, level_columns(rows),
        spread_table(heads, 0), spread_table(heads, VALUE_LANE),
    )


def group_of(distance):
    return distance.bit_length()


def message_layout(rows, bits):
    direct = [1] + list(range(2, 1 << bits, 2)) if bits else []
    layout = [((item, 0, rows >> group_of(item)),) for item in direct]
    passed, offset = [], 0
    for item in direct[1:]:
        passed.append((item + 1, offset, rows >> group_of(item)))
        offset += rows >> group_of(item)
    return tuple(layout + [tuple(passed)]) if passed else tuple(layout)


def far_pieces(layout, refs):
    return [(ref, *entry) for ref, entries in zip(refs, layout) for entry in entries]


def attend_own_kernel(q_ref, kv_ref, count_ref, out_ref):
    rows = q_ref.shape[1]
    tile = min(rows, 512)
    for low in range(0, rows, tile):
        there = slice(low, low + tile)
        scores = dot_nt(q_ref[0, there, :] + count_ref[0, there, :], kv_ref[0])
        peak = jnp.max(scores, axis=-1, keepdims=True)
        total = dot_nn(jnp.exp2(scores - peak).astype(BF16), kv_ref[0])
        lane = lax.broadcasted_iota(jnp.int32, total.shape, 1)
        out_ref[0, there, :] = jnp.where(lane == 0, peak, total)


def attend_own(queries, pairs, counts):
    heads, rows, _ = queries.shape
    return call(
        attend_own_kernel,
        grid=(heads,),
        in_specs=[head_spec(rows), head_spec(rows), full_spec(counts.shape)],
        out_specs=head_spec(rows),
        out_shape=jax.ShapeDtypeStruct((heads, rows, LANES), F32),
        name="attend_own",
    )(queries, pairs, counts)


def attend_far_kernel(layout, first_ref, q_ref, own_ref, count_ref, gather_ref, *refs):
    pieces_all = far_pieces(layout, refs[: len(layout)])
    out_ref, mine_ref, theirs_ref, placed = refs[len(layout) :]
    head = pl.program_id(0)
    rows = q_ref.shape[1]
    block = rows // STRIDE
    turn = (first_ref[0] + head) & (STRIDE - 1)
    counts = [count for _, _, _, count in pieces_all]
    keys = [ref[0, offset : offset + count, :] for ref, _, offset, count in pieces_all]
    scores = [
        dot_nt(q_ref[0, :count, :] + count_ref[group_of(distance) - 1, :count, :], key)
        for key, (_, distance, _, count) in zip(keys, pieces_all)
    ]
    peaks = [jnp.max(item, axis=-1, keepdims=True) for item in scores]
    edges = sorted({0, rows, *counts})
    tiles = list(zip(edges[:-1], edges[1:]))
    own_peaks = [own_ref[0, low:high, 0:1] for low, high in tiles]
    tops = [
        functools.reduce(jnp.maximum, [peak[low:high] for peak, count in zip(peaks, counts) if low < count], own)
        for (low, high), own in zip(tiles, own_peaks)
    ]
    terms = []
    for score, key, count in zip(scores, keys, counts):
        top = [item for item, (low, _) in zip(tops, tiles) if low < count]
        top = top[0] if len(top) == 1 else jnp.concatenate(top, axis=0)
        terms.append(dot_nn(jnp.exp2(score - top).astype(BF16), key))
    for (low, high), own, top in zip(tiles, own_peaks, tops):
        total = own_ref[0, low:high, :]
        near = [term[low:high] for term, count in zip(terms, counts) if low < count]
        if near:
            total = functools.reduce(jnp.add, near, total * jnp.exp2(own - top))
        mass = total[:, ONE_LANE : ONE_LANE + 1]
        result = total * (1.0 / mass)
        lane = lax.broadcasted_iota(jnp.int32, result.shape, 1)
        out_ref[0, low:high, :] = jnp.where(lane == 0, top + jnp.log2(mass), result)
        for offset in range(low, high, block):
            start = bit_reversed(offset // block) ^ turn
            placed[head, pl.ds(start, block, stride=STRIDE), :] = result[offset - low : offset - low + block]

    @pl.when(head == pl.num_programs(0) - 1)
    def _():
        half = rows // 2
        for side, ref in enumerate((mine_ref, theirs_ref)):
            here = pl.ds(pl.multiple_of(((first_ref[HEADS_PLACE] & 1) ^ side) * half, half), half)
            ref[...] = functools.reduce(
                jnp.add,
                [
                    dot_nn(placed[item, here, :].astype(BF16), gather_ref[item * LANES : (item + 1) * LANES])
                    for item in range(placed.shape[0])
                ],
            ).astype(BF16)


def attend_far(first, queries, own, far, layout, counts):
    heads, rows, _ = queries.shape
    feats = heads * HEAD_DIM
    gather = spread_table(heads, VALUE_LANE).T.copy()
    return call(
        functools.partial(attend_far_kernel, layout),
        grid=(heads,),
        in_specs=[SMALL_SPEC, head_spec(rows), head_spec(rows), full_spec(counts.shape), full_spec(gather.shape)]
        + [loose(head_spec(item.shape[1])) for item in far],
        out_specs=[head_spec(rows), full_spec((rows // 2, feats)), full_spec((rows // 2, feats))],
        out_shape=[
            jax.ShapeDtypeStruct((heads, rows, LANES), F32),
            jax.ShapeDtypeStruct((rows // 2, feats), BF16),
            jax.ShapeDtypeStruct((rows // 2, feats), BF16),
        ],
        scratch_shapes=[pltpu.VMEM((heads, rows, LANES), F32)],
        name="attend_far",
    )(first, queries, own, counts, gather, *far)


def three_parts(values):
    high = values.astype(BF16).astype(F32)
    middle = (values - high).astype(BF16).astype(F32)
    return high, middle, values - high - middle


def pair_grads(keys, query, counted, grad):
    prob = jnp.exp2(dot_nt(keys, counted))
    slope = (prob * dot_nt(keys, grad)).astype(BF16)
    return dot_nn(prob.astype(BF16), grad) + dot_nn(slope, query), dot_tn(slope, keys)


def back_far_kernel(layout, pieces, place_ref, q_ref, out_ref, count_ref, spread_ref, *refs):
    grad_refs = refs[:pieces]
    far = far_pieces(layout, refs[pieces : pieces + len(layout)])
    query, grad, dq_ref = refs[pieces + len(layout) : pieces + len(layout) + 3]
    rows_half = q_ref.shape[1] // 2
    *message_refs, wide = refs[pieces + len(layout) + 3 :]
    targets = []
    for index, entries in enumerate(layout):
        passed = index == len(message_refs)
        for _, offset, _ in entries:
            targets.append((message_refs[0], rows_half + offset) if passed else (message_refs[index], 0))
    head = pl.program_id(0)
    rows = q_ref.shape[1]
    block = rows // STRIDE
    part = grad_refs[0].shape[0]
    turn = (place_ref[0] + head) & (STRIDE - 1)

    @pl.when(head == 0)
    def _():
        for index, ref in enumerate(grad_refs):
            start = pl.multiple_of(place_ref[PART_PLACE + index], part)
            for item in range(wide.shape[0]):
                wide[item, pl.ds(start, part), :] = dot_nn(ref[...], spread_ref[:, item * LANES : (item + 1) * LANES])

    for item in range(STRIDE):
        there = slice(item * block, (item + 1) * block)
        start = bit_reversed(item) ^ turn
        rows_grad = wide[head, pl.ds(start, block, stride=STRIDE), :]
        rows_out = out_ref[0, there, :]
        lane = lax.broadcasted_iota(jnp.int32, rows_grad.shape, 1)
        rows_query = q_ref[0, there, :].astype(F32)
        parts = three_parts(jnp.sum(rows_grad * rows_out, axis=-1, keepdims=True))
        for index, value in enumerate(parts):
            rows_grad = jnp.where(lane == ONE_LANE + index, -value, rows_grad)
        for index, value in enumerate(three_parts(rows_out[:, 0:1])):
            rows_query = jnp.where(lane == LSE_LANE + index, -value, rows_query)
        grad[0, there, :] = rows_grad.astype(BF16)
        query[0, there, :] = rows_query.astype(BF16)

    dq_ref[...] = jnp.zeros_like(dq_ref)
    for (ref, distance, offset, count), (dref, doffset) in zip(far, targets):
        counted = query[0, :count, :] + count_ref[group_of(distance) - 1, :count, :]
        step = min(count, 256)
        for low in range(offset, offset + count, step):
            dkv, dq = pair_grads(ref[0, low : low + step, :], query[0, :count, :], counted, grad[0, :count, :])
            there = slice(doffset + low - offset, doffset + low - offset + step)
            dref[0, there, :] = dkv.astype(BF16)
            dq_ref[0, :count, :] += dq


def back_far(places, grads, queries, outs, far, layout, counts):
    heads, rows, _ = queries.shape
    spread = spread_table(heads, VALUE_LANE)
    limit = rows // 2 if layout else rows // STRIDE
    messages = [sum(item[2] for item in entries) for entries in layout]
    if len(messages) > 1:
        messages = [messages[0] + messages[-1]] + messages[1:-1]
    messages = [(heads, count, LANES) for count in messages]
    return call(
        functools.partial(back_far_kernel, layout, len(grads)),
        grid=(heads,),
        in_specs=[SMALL_SPEC, head_spec(rows), head_spec(rows), full_spec(counts.shape), full_spec(spread.shape)]
        + [near(full_spec(item.shape)) for item in grads]
        + [loose(head_spec(item.shape[1])) for item in far],
        out_specs=[head_spec(rows), head_spec(rows), head_spec(limit)] + [head_spec(item[1]) for item in messages],
        out_shape=[
            jax.ShapeDtypeStruct((heads, rows, LANES), BF16),
            jax.ShapeDtypeStruct((heads, rows, LANES), BF16),
            jax.ShapeDtypeStruct((heads, limit, LANES), F32),
        ]
        + [jax.ShapeDtypeStruct(item, BF16) for item in messages],
        scratch_shapes=[pltpu.VMEM((heads, rows, LANES), F32)],
        name="back_far",
    )(places, queries, outs, counts, spread, *grads, *far)


def back_own_kernel(query, grad, kv_ref, count_ref, dq_far_ref, dq_ref, dkv_ref):
    rows = kv_ref.shape[1]
    limit = dq_far_ref.shape[1]
    counted = query[0] + count_ref[0]
    tile = min(rows, 256)
    for low in range(0, rows, tile):
        there = slice(low, low + tile)
        dkv, dq = pair_grads(kv_ref[0, there, :], query[0], counted, grad[0])
        dkv_ref[0, there, :] = dkv
        if low == 0:
            dq_ref[0] = dq
        else:
            dq_ref[0] += dq
    dq_ref[0, :limit, :] += dq_far_ref[0]


def back_own(queries, grads, pairs, counts, dq_far):
    heads, rows, _ = queries.shape
    return call(
        back_own_kernel,
        grid=(heads,),
        in_specs=[head_spec(rows)] * 3 + [full_spec(counts.shape), head_spec(dq_far.shape[1])],
        out_specs=[near(head_spec(rows))] * 2,
        out_shape=[jax.ShapeDtypeStruct((heads, rows, LANES), F32)] * 2,
        name="back_own",
    )(queries, grads, pairs, counts, dq_far)


def collect_kernel(counts, peers, first_ref, dq_ref, dkv_ref, gather_k_ref, gather_v_ref, w_ref, *refs):
    far_refs = refs[: len(counts)]
    *three_refs, term_ref = refs[len(counts) : len(counts) + 4]
    q_rows, kv_rows = refs[-2:]
    head = pl.program_id(0)
    rows = dq_ref.shape[1]
    part = rows // peers
    block = rows // STRIDE
    turn = (first_ref[0] + head) & (STRIDE - 1)
    for item in range(STRIDE):
        there = slice(item * block, (item + 1) * block)
        start = bit_reversed(item) ^ turn
        pair = dkv_ref[0, there, :]
        for ref, count in zip(far_refs, counts):
            if item * block < count:
                pair = pair + ref[0, there, :].astype(F32)
        lane = lax.broadcasted_iota(jnp.int32, pair.shape, 1)
        q_rows[head, pl.ds(start, block, stride=STRIDE), :] = dq_ref[0, there, :] * SCALE
        kv_rows[head, pl.ds(start, block, stride=STRIDE), :] = jnp.where(lane < VALUE_LANE, pair * LN2, pair)

    @pl.when(head == pl.num_programs(0) - 1)
    def _():
        total = [None] * 3
        for item in range(q_rows.shape[0]):
            lanes = slice(item * LANES, (item + 1) * LANES)
            query = q_rows[item].astype(BF16)
            pair = kv_rows[item].astype(BF16)
            terms = (
                dot_nn(query, gather_k_ref[lanes]),
                dot_nn(pair, gather_k_ref[lanes]),
                dot_nn(pair, gather_v_ref[lanes]),
            )
            total = [term if old is None else old + term for old, term in zip(total, terms)]
        for ref, value in zip(three_refs, total):
            ref[...] = value.astype(BF16)
        for peer in range(peers):
            start = (peer & 1) * (rows // 2) + (peer >> 1) * part
            here = slice(start, start + part)
            term_ref[peer * part : (peer + 1) * part, :] = functools.reduce(
                jnp.add, [dot_nn(ref[here, :], w_ref[item]) for item, ref in enumerate(three_refs)]
            ).astype(BF16)


def collect(places, dq, dkv, far, weights, peers):
    heads, rows, _ = dq.shape
    feats, width = weights.shape[1:]
    gather_k = spread_table(heads, 0).T.copy()
    gather_v = spread_table(heads, VALUE_LANE).T.copy()
    return call(
        functools.partial(collect_kernel, [count for _, count in far], peers),
        grid=(heads,),
        in_specs=[
            SMALL_SPEC, near(head_spec(rows)), near(head_spec(rows)), full_spec(gather_k.shape), full_spec(gather_v.shape),
            full_spec(weights.shape),
        ]
        + [near(head_spec(item.shape[1])) for item, _ in far],
        out_specs=[near(full_spec((rows, feats)))] * 3 + [full_spec((rows, width))],
        out_shape=[jax.ShapeDtypeStruct((rows, feats), BF16)] * 3
        + [jax.ShapeDtypeStruct((rows, width), BF16)],
        scratch_shapes=[pltpu.VMEM((heads, rows, LANES), F32), pltpu.VMEM((heads, rows, LANES), F32)],
        name="collect",
    )(places, dq, dkv, gather_k, gather_v, weights, *[item for item, _ in far])


def bring_kernel(*refs):
    count = len(refs) // 2
    for source, target in zip(refs[:count], refs[count:]):
        target[...] = source[...]


def bring(arrays):
    return call(
        bring_kernel,
        grid=(1,),
        in_specs=[loose(full_spec(item.shape)) for item in arrays],
        out_specs=[near(full_spec(item.shape)) for item in arrays],
        out_shape=[jax.ShapeDtypeStruct(item.shape, item.dtype) for item in arrays],
        name="bring",
    )(*arrays)


def pick(core, low, high):
    return jnp.where(core == 0, low, high), jnp.where(core == 0, high, low)


def halves(array):
    half = array.shape[-1] // 2
    return array[:, :half], array[:, half:]


FETCHED = 2
BIAS_ROWS = 16


def fetched_weights(refs, up_shape, down_shape):
    sides = []
    for ref in refs:
        count = up_shape[0] // 2
        down = ref[count : 2 * count].reshape(down_shape[0] // 2, down_shape[1])
        bias = ref[2 * count : 2 * count + 1].astype(F32)
        for index in (1, 2):
            bias = bias + ref[2 * count + index : 2 * count + index + 1].astype(F32)
        sides.append((ref.at[:count], down, bias))
    return sides


def feed_kernel(
    place_ref, tok_ref, cot_ref, w_out_ref, b_out_ref, gain_ref, shift_ref, up_ref, down_ref, bias_ref, *refs,
):
    fetched, refs = refs[:FETCHED], refs[FETCHED:]
    (up_one, down_one, bias_other), (up_two, down_two, _) = fetched_weights(fetched, up_ref.shape, down_ref.shape)
    attn_refs = refs[:-10]
    resid_ref, normed_ref, cot_out_ref, h0_ref, h1_ref, p0_ref, p1_ref, da_ref, out_ref, sums_ref = refs[-10:]
    feats = attn_refs[0].shape[1]
    core = place_ref[SEQ_PLACE] & 1
    resid = tok_ref[...].astype(F32) + b_out_ref[...]
    for index, ref in enumerate(attn_refs):
        here = pl.ds(pl.multiple_of((place_ref[HEADS_PLACE] ^ index) * feats, feats), feats)
        resid = resid + dot_nn(ref[...], w_out_ref[here, :])
    resid_ref[0] = resid
    normed = norm_rows(resid, gain_ref[...], shift_ref[...]).astype(BF16)
    normed_ref[0] = normed
    cot = cot_ref[...]
    cot_out_ref[0] = cot
    normed_pair = pick(core, *halves(normed))
    pres = (
        dot_nn(normed, up_ref[...]) + bias_ref[...],
        dot_nn(normed_pair[0], up_one[...]) + dot_nn(normed_pair[1], up_two[...]) + bias_other,
    )
    acts = (
        dot_nt(cot, down_ref[...]),
        jnp.concatenate(pick(core, dot_nt(cot, down_one[...]), dot_nt(cot, down_two[...])), axis=1),
    )
    grads = []
    for pre, act, h_ref, p_ref in zip(pres, acts, (h0_ref, h1_ref), (p0_ref, p1_ref)):
        share = 0.5 * (1.0 + lax.erf(pre * math.sqrt(0.5)))
        h_ref[0] = (pre * share).astype(BF16)
        slope = share + pre * jnp.exp(-0.5 * pre * pre) * (1.0 / math.sqrt(2.0 * math.pi))
        grads.append((act * slope).astype(BF16))
        p_ref[0] = grads[-1]
    other = pick(core, dot_nt(grads[1], up_one[...]), dot_nt(grads[1], up_two[...]))
    da_ref[0] = (dot_nt(grads[0], up_ref[...]) + jnp.concatenate(other, axis=1)).astype(da_ref.dtype)
    hidden_pair = pick(core, *halves(h1_ref[0]))
    out_ref[0] = (
        dot_nn(h0_ref[0], down_ref[...])
        + dot_nn(hidden_pair[0], down_one[...])
        + dot_nn(hidden_pair[1], down_two[...])
    ).astype(out_ref.dtype)
    ones = jnp.ones((8, cot.shape[0]), BF16)
    sums_ref[0, 0] = dot_nn(ones, grads[0])
    sums_ref[0, 1] = dot_nn(ones, grads[1])


def feed(places, block, piece_cut, steps, kind, tokens, cotangent, w_out, b_out, gain, shift, up, down, bias, fetched, attns):
    rows, width = tokens.shape
    hidden = up.shape[1]
    feats = attns[0].shape[1]
    inner = attns[0].shape[0] // block
    first = steps[0]

    def piece(i, place):
        return ((place[HEADS_PLACE] >> 1) ^ (i + first)) * piece_cut[1] + piece_cut[0]

    def row_block(i, place):
        return ((place[HEADS_PLACE] & 1) * inner + piece(i, place), 0)

    def stacked(columns):
        return View((1, block, columns), lambda i, place: (i, 0, 0))

    constants = (w_out, b_out, gain, shift, up, down, bias)
    outs = [(width, F32), (width, BF16), (width, BF16)] + [(hidden, BF16)] * 4 + [(width, kind)] * 2
    count = len(steps)
    return call(
        feed_kernel,
        grid=(count,),
        in_specs=[SMALL_SPEC]
        + [View((block, width), row_block)] * 2
        + [
            near(full_spec(item.shape)) if item.size >= width * feats else full_spec(item.shape)
            for item in (*constants, *fetched)
        ]
        + [View((block, feats), lambda i, place: (piece(i, place), 0))] * len(attns),
        out_specs=[near(stacked(columns)) for columns, _ in outs]
        + [View((1, 2, 8, hidden), lambda i, place: (i, 0, 0, 0))],
        out_shape=[jax.ShapeDtypeStruct((count, block, columns), dtype) for columns, dtype in outs]
        + [jax.ShapeDtypeStruct((count, 2, 8, hidden), F32)],
        name="feed",
    )(places, tokens, cotangent, *constants, *fetched, *attns)


def outer_kernel(pairs, parts, place_ref, *refs):
    ins, (keep_ref, give_ref) = refs[:-2], refs[-2:]
    step = pl.program_id(0)
    core = place_ref[SEQ_PLACE] & 1
    for index in range(pairs):

        @pl.when(step == index)
        def _():
            total = None
            first = 2 * parts * index
            for left_ref, right_ref in zip(ins[first : first + parts], ins[first + parts : first + 2 * parts]):
                for item in range(left_ref.shape[0]):
                    left = pick(core, *halves(left_ref[item]))
                    terms = [dot_tn(side, right_ref[item]) for side in left]
                    total = terms if total is None else [old + term for old, term in zip(total, terms)]
            keep_ref[0] = total[0].astype(BF16)
            give_ref[0] = total[1].astype(BF16)


def outer_sums(places, pairs):
    lefts = pairs[0][0][0].shape[2] // 2
    rights = pairs[0][1][0].shape[2]
    arrays = [item for pair in pairs for side in pair for item in side]
    spec = View((1, lefts, rights), lambda i, place: (i, 0, 0))
    shape = jax.ShapeDtypeStruct((len(pairs), lefts, rights), BF16)
    return call(
        functools.partial(outer_kernel, len(pairs), len(pairs[0][0])),
        grid=(len(pairs),),
        in_specs=[SMALL_SPEC] + [near(full_spec(item.shape)) for item in arrays],
        out_specs=[spec, near(spec)],
        out_shape=[shape, shape],
        name="outer_sums",
    )(places, *arrays)


def out_grads_kernel(place_ref, low_ref, *refs):
    *attn_refs, keep_ref, give_ref = refs
    half = attn_refs[0].shape[1] // 2
    core = place_ref[SEQ_PLACE] & 1
    bits = len(attn_refs).bit_length() - 1
    for distance, ref in enumerate(attn_refs):
        index = sum(((distance >> bit) & 1) << (bits - 1 - bit) for bit in range(bits))
        product = dot_tn(ref[...], low_ref[...])
        keep, give = pick(core, product[:half], product[half:])
        keep_ref[index] = keep.astype(BF16)
        give_ref[index] = give.astype(BF16)


def out_grads(places, low, attns):
    part, width = low.shape
    feats = attns[0].shape[1]
    shape = (len(attns), feats // 2, width)
    return call(
        out_grads_kernel,
        grid=(1,),
        in_specs=[SMALL_SPEC, near(full_spec((part, width)))]
        + [View((part, feats), lambda i, place: (place[HEADS_PLACE] >> 1, 0))] * len(attns),
        out_specs=[near(full_spec(shape))] * 2,
        out_shape=[jax.ShapeDtypeStruct(shape, BF16)] * 2,
        name="out_grads",
    )(places, low, *attns)


def tail_kernel(normed_ref, tok_ref, w_ref, _, stats_ref, up_ref, *refs):
    *three_refs, out_ref, sums_ref = refs
    rows, width = normed_ref.shape
    feats = three_refs[0].shape[1]
    hidden = up_ref.shape[1]
    for index, ref in enumerate(three_refs):
        out_ref[index * feats : (index + 1) * feats, :] = dot_tn(ref[...], normed_ref[...]).astype(BF16)
    gain = jnp.zeros((1, width), F32)
    shift = jnp.zeros((1, width), F32)
    tile = min(rows, 256)
    for low in range(0, rows, tile):
        here = slice(low, low + tile)
        term = functools.reduce(
            jnp.add, [dot_nn(ref[here, :], w_ref[index]) for index, ref in enumerate(three_refs)]
        )
        center = tok_ref[here, :].astype(F32)
        center = center - jnp.mean(center, axis=-1, keepdims=True)
        unit = center * lax.rsqrt(jnp.mean(center * center, axis=-1, keepdims=True) + EPSILON)
        gain = gain + column_sums(term * unit)
        shift = shift + column_sums(term)
    row = lax.broadcasted_iota(jnp.int32, (SUM_ROWS, width), 0)
    other = up_ref[1:2, :]
    if hidden < width:
        other = jnp.concatenate([other, jnp.zeros((1, width - hidden), F32)], axis=1)
    lines = (gain, stats_ref[0:1], shift, stats_ref[1:2], stats_ref[2:3], stats_ref[3:4], other)
    block = jnp.zeros((SUM_ROWS, width), F32)
    for index, line in enumerate(lines):
        block = jnp.where(row == index, line, block)
    sums_ref[:SUM_ROWS, :] = block.astype(BF16)
    sums_ref[SUM_ROWS:, :] = jnp.zeros((3 * SUM_ROWS, width), BF16)
    ones = jnp.ones((SUM_ROWS, rows), BF16)
    own = jnp.broadcast_to(up_ref[0:1, :], (SUM_ROWS, hidden))
    for index, value in enumerate((own, dot_nn(ones, three_refs[0][...]), dot_nn(ones, three_refs[2][...]))):
        here = (index + 1) * SUM_ROWS
        sums_ref[here : here + SUM_ROWS, : value.shape[1]] = value.astype(BF16)


SUM_ROWS = 16


def tail_grads(normed, tokens, weights, earlier, stats, ups, three):
    rows, width = normed.shape
    feats = three[0].shape[1]
    ins = (normed, tokens, weights, stats, ups, *three)
    specs = [full_spec(item.shape) for item in ins[:5]] + [near(full_spec(item.shape)) for item in three]
    ins = (*ins[:3], earlier, *ins[3:])
    return call(
        tail_kernel,
        grid=(1,),
        in_specs=[*specs[:3], View((1, 16, LANES), lambda step, place: (0, 0, 0)), *specs[3:]],
        out_specs=[near(full_spec((3 * feats, width))), near(full_spec((4 * SUM_ROWS, width)))],
        out_shape=[jax.ShapeDtypeStruct((count, width), BF16) for count in (3 * feats, 4 * SUM_ROWS)],
        name="tail_grads",
    )(*ins)


def pack_kernel(core_ref, up_ref, down_ref, bias_ref, out_ref):
    count = up_ref.shape[0]
    out_ref[:count, :] = up_ref[...]
    out_ref[count : 2 * count, :] = down_ref[...]
    row = lax.broadcasted_iota(jnp.int32, (BIAS_ROWS, bias_ref.shape[1]), 0)
    block = jnp.zeros(row.shape, F32)
    for index, line in enumerate(three_parts(bias_ref[...])):
        block = jnp.where(row == index, line, block)
    out_ref[2 * count :, :] = block.astype(BF16)


def pack_weights(core, up, down, bias):
    hidden = up.shape[1]
    shape = (up.shape[0] + BIAS_ROWS, hidden)
    if up.shape != down.shape:
        cuts = [
            lax.dynamic_slice_in_dim(item, core * (item.shape[0] // 2), item.shape[0] // 2).reshape(-1, hidden)
            for item in (up, down)
        ]
        zeros = jnp.zeros((BIAS_ROWS - 3, hidden), F32)
        return jnp.concatenate([*cuts, jnp.concatenate([*three_parts(bias), zeros]).astype(BF16)])
    return call(
        pack_kernel,
        grid=(1,),
        in_specs=[SMALL_SPEC]
        + [View((up.shape[0] // 2, hidden), lambda i, place: (place[0], 0))] * 2
        + [full_spec(bias.shape)],
        out_specs=full_spec(shape),
        out_shape=jax.ShapeDtypeStruct(shape, BF16),
        name="pack_weights",
    )(core.reshape(1), up, down, bias)


def column_sums(array):
    return jnp.sum(array, axis=0, keepdims=True)


def turn_kernel(received, place_ref, resid_ref, cot_ref, da_ref, w_out_ref, gain_ref, *refs):
    more_refs = refs[:received]
    dres_ref, low_ref, stats_ref, *grad_refs = refs[received:]
    feats = grad_refs[0].shape[1]
    total = da_ref[0]
    block = more_refs[0].shape[0]
    blocks = total.shape[0] // block
    more = [ref[...].astype(F32) for ref in more_refs]
    total = total + jnp.concatenate(
        [functools.reduce(jnp.add, more[index::blocks]) for index in range(blocks)], axis=0
    )
    cot = cot_ref[0].astype(F32)
    grad_n, gain_sum, shift_sum = norm_back(resid_ref[0], gain_ref[...], total)
    dres = cot + grad_n
    dres_ref[...] = dres
    low = dres.astype(BF16)
    low_ref[...] = low
    for index, ref in enumerate(grad_refs):
        here = pl.ds(pl.multiple_of((place_ref[HEADS_PLACE] ^ index) * feats, feats), feats)
        ref[...] = dot_nt(low, w_out_ref[here, :]).astype(BF16)
    stats_ref[0:1] = gain_sum
    stats_ref[1:2] = shift_sum
    stats_ref[2:3] = column_sums(dres)
    stats_ref[3:4] = column_sums(cot)
    stats_ref[4:8] = jnp.zeros_like(stats_ref[4:8])


def turn_back(places, resid, cot, gain, da, more, w_out, peers):
    _, part, width = resid.shape
    feats = width // peers
    ins = (resid, cot, da, w_out, gain)
    return call(
        functools.partial(turn_kernel, len(more)),
        grid=(1,),
        in_specs=[SMALL_SPEC]
        + [near(full_spec(item.shape)) for item in ins[:4]]
        + [full_spec(item.shape) for item in ins[4:]]
        + [near(full_spec(item.shape)) for item in more],
        out_specs=[full_spec((part, width)), near(full_spec((part, width))), full_spec((8, width))]
        + [near(full_spec((part, feats)))] * peers,
        out_shape=[
            jax.ShapeDtypeStruct((part, width), F32),
            jax.ShapeDtypeStruct((part, width), BF16),
            jax.ShapeDtypeStruct((8, width), F32),
        ]
        + [jax.ShapeDtypeStruct((part, feats), BF16)] * peers,
        name="turn_back",
    )(places, *ins, *more)


def finish_kernel(place_ref, tok_ref, gain_ref, term_ref, dres_ref, grad_ref):
    grad_n, _, _ = norm_back(tok_ref[...].astype(F32), gain_ref[...], term_ref[...].astype(F32))
    grad_ref[...] = (dres_ref[...] + grad_n).astype(BF16)


def finish(places, tokens, gain, term, dres):
    part, width = term.shape
    return call(
        finish_kernel,
        grid=(1,),
        in_specs=[SMALL_SPEC, View((part, width), lambda i, place: (place[PART_PLACE] // part, 0))]
        + [full_spec(item.shape) for item in (gain, term, dres)],
        out_specs=full_spec((part, width)),
        out_shape=jax.ShapeDtypeStruct((part, width), BF16),
        name="finish",
    )(places, tokens, gain, term, dres)


def flipped(array, distance):
    return lax.ppermute(array, "seq", [(i, i ^ distance) for i in range(lax.axis_size("seq"))])


def crossed(array, distance):
    if distance == 0:
        return array
    return lax.ppermute(array, "heads", [(i, i ^ distance) for i in range(lax.axis_size("heads"))])


def added(left, right):
    return (left.astype(F32) + right.astype(F32)).astype(BF16)


def halved(array, axis, bit):
    side = (lax.axis_index("seq") >> bit) & 1
    count = array.shape[axis] // 2
    keep = lax.dynamic_slice_in_dim(array, side * count, count, axis)
    give = lax.dynamic_slice_in_dim(array, (1 - side) * count, count, axis)
    other = flipped(give, 1 << bit)
    return added(keep, other), other


def doubled(array, axis, bit):
    side = (lax.axis_index("seq") >> bit) & 1
    other = flipped(array, 1 << bit)
    whole = jnp.where(side == 0, jnp.concatenate([array, other], axis), jnp.concatenate([other, array], axis))
    return whole, other


def after(value, earlier):
    return lax.optimization_barrier((value, earlier))[0]


def shards(tokens, docs, ln_gain, ln_bias, w_qkv, b_qv, w_out, b_out, w_up, b_up, w_down, b_down, cotangent):
    rows, width = tokens.shape
    feats = w_qkv.shape[3]
    heads = feats // HEAD_DIM
    seq_count = lax.axis_size("seq")
    head_count = lax.axis_size("heads")
    seq_pos = lax.axis_index("seq")
    head_pos = lax.axis_index("heads")
    seq_bits = seq_count.bit_length() - 1
    gains, shifts = ln_gain[0], ln_bias[0]
    half = rows // 2
    part = rows // head_count
    peers = [head_pos ^ distance for distance in range(head_count)]
    part_starts = [(peer & 1) * half + (peer >> 1) * part for peer in peers]
    edges = [jnp.sum((docs <= item).astype(jnp.int32)) - seq_pos * rows for item in range(DOCS - 1)]
    places = jnp.stack(
        [item.astype(jnp.int32) for item in (head_pos * heads, *edges, head_pos, seq_pos, *part_starts)]
    )

    core = seq_pos & 1
    hidden = w_up.shape[2]
    w_out_all = lax.all_gather(w_out[0], "heads", axis=0, tiled=True)
    fetched_one = crossed(pack_weights(core.astype(jnp.int32), w_up[0], w_down[0], b_up), 1)

    w_three = jnp.transpose(w_qkv[0], (1, 2, 0))
    bits = min(seq_bits, TOP)
    normed, queries, pairs, *messages = project(places, tokens, gains[0:1], shifts[0:1], w_three, b_qv[0], bits)
    layout = message_layout(rows, bits)
    counts = count_columns(rows, bits + 1)
    own_counts, far_counts = counts[:1], counts[1:, : rows // 2]
    direct = layout[:-1] if bits > 1 else layout
    far = [flipped(messages[group_of(entries[0][0]) - 1], entries[0][0]) for entries in direct]
    own_outs = attend_own(queries, pairs, own_counts)
    if bits > 1:
        far.append(flipped(after(jnp.concatenate(far[1:], axis=1), own_outs), 1))
    outs, attn_mine, attn_theirs = attend_far(places, queries, own_outs, far, layout, far_counts)
    fetched = [fetched_one, flipped(after(fetched_one, outs), 1)]
    attns = [attn_mine] + [
        crossed(attn_theirs if distance & 1 else attn_mine, distance) for distance in range(1, head_count)
    ]

    def in_rows(array):
        return jnp.concatenate([array[2 * inner + side] for side in range(2) for inner in range(head_count // 2)])

    steps = head_count // 2
    w_out_all, up_here, down_here, *fetched = bring([w_out_all, w_up[0], w_down[0], *fetched])
    shared = (
        tokens, cotangent, w_out_all, b_out, gains[1:2], shifts[1:2], up_here, down_here, b_up, fetched, attns,
    )
    cuts = 2
    sent = [feed(places, part // cuts, (index, cuts), range(1, steps), BF16, *shared) for index in range(cuts)]
    da_more = [crossed(item[7][step - 1], 2 * step) for step in range(1, steps) for item in sent]
    own = feed(places, part, (0, 1), range(0, 1), F32, *shared)
    resid, normed_two, cots, h0, h1, p0, p1, da_two, out_term, up_sums = zip(own, *sent)
    dres, dres_low, stats_two, *grad_attns = turn_back(
        places, resid[0], cots[0], gains[1:2], da_two[0], da_more, w_out_all, head_count
    )
    grad_attns = [crossed(item, distance) for distance, item in enumerate(grad_attns)]
    later = after(places, dres)
    out_keep, out_give = out_grads(later, dres_low, attns)
    later = after(later, out_keep)
    products = [(normed_two, p0), (h0, cots), (normed_two, p1), (h1, cots)]
    if hidden == width:
        packs = [outer_sums(later, products)]
    else:
        packs = [outer_sums(later, products[0::2]), outer_sums(later, products[1::2])]
    packs = after(packs, grad_attns)
    out_core = flipped(after(out_give, (grad_attns, packs)), 1)
    out_grad = added(out_keep, out_core)

    out_terms = after(jnp.concatenate(out_term[1:], axis=1), (grad_attns, packs))
    out_more = [crossed(out_terms[step - 1], 2 * step) for step in range(1, steps)]
    queries_b, grads_b, dq_far, *dfar = back_far(
        after(places, packs), grad_attns, queries, outs, far, layout, far_counts
    )
    out_sum = functools.reduce(jnp.add, [item.astype(F32) for item in after(out_more, dq_far)], out_term[0][0])
    out_part = (resid[0][0] + out_sum + b_down[0]).astype(BF16)
    back = []
    if bits:
        arrived = flipped(after(dfar[0], (out_more, out_core)), 1)
        arrived = after(arrived, out_part)
        offset = rows // 2
        onward = []
        for item in dfar[1:]:
            count = item.shape[1]
            onward.append(added(item, arrived[:, offset : offset + count]))
            offset += count
        queries_b = after(queries_b, onward)
        back = [(arrived, rows // 2)] + [
            (flipped(item, entries[0][0]), item.shape[1]) for entries, item in zip(direct[1:], onward)
        ]
    out_other = crossed(after(out_grad, out_part)[steps:], 1)
    out_grad = added(out_grad[:steps], out_other)
    arrived = [flipped(give, 1) for _, give in after(packs, out_part)]
    packs = [(keep, item) for (keep, _), item in zip(packs, arrived)]
    queries_b, out_part = lax.optimization_barrier((queries_b, out_part))
    gathered = lax.all_gather(out_part, "heads", axis=0)
    dq, dkv = back_own(queries_b, grads_b, pairs, own_counts, dq_far)
    ups = functools.reduce(jnp.add, [jnp.sum(item[:, :, 0], axis=0) for item in up_sums])
    *grads_three, terms = collect(after(places, (ups, arrived, out_other)), dq, dkv, back, w_three, head_count)
    term = lax.psum_scatter(terms, "heads", scatter_dimension=0, tiled=True)
    orders = [list(range(1, seq_bits))] * 2
    if seq_bits > 2:
        orders[1] = [2, 1] + orders[0][2:]
    packs = [added(*item) for item in after(packs, terms)]
    count = packs[0].shape[1] // 2
    packs = [[item[:, :count], item[:, count:]] for item in packs]
    arrived = []
    for step in range(seq_bits - 1):
        for pack in packs:
            for side, order in enumerate(orders):
                pack[side], other = halved(pack[side], 1, order[step])
                if not step:
                    arrived.append(other)
    packs = [jnp.concatenate(pack, axis=1) for pack in packs]
    distance = 2
    while distance < head_count:
        count = out_grad.shape[0] // 2
        out_grad = added(out_grad[:count], crossed(out_grad[count:], distance))
        distance = 2 * distance
    grad_w_out = out_grad[0]

    rest, sums = tail_grads(normed, tokens, w_three, gathered, stats_two, ups, grads_three)
    count = rest.shape[0] // 2
    keep, give = (lax.dynamic_slice_in_dim(rest, side * count, count) for side in (core, 1 - core))
    rest = added(jnp.concatenate([keep, sums]), flipped(jnp.concatenate([give, sums]), 1))
    rest = jnp.concatenate([rest, grad_w_out])
    cut = rest.shape[0] // 2
    rest = [rest[:cut], rest[cut:]]

    def swap(step):
        others = [flipped(item, 1 << order[step]) for item, order in zip(rest, orders)]
        return [added(item, other) for item, other in zip(rest, others)], others

    others = []
    if seq_bits > 1:
        rest, others = swap(0)
    arrived = (packs, others)
    grad_part = finish(after(places, arrived), tokens, gains[0:1], term, dres)
    grad_tokens = in_rows(lax.all_gather(grad_part, "heads", axis=0)).astype(F32)
    packs, rest = after((packs, rest), grad_part)
    passed = [crossed(item[item.shape[0] // 2 :], 1) for item in packs]
    packs = [added(item[: item.shape[0] // 2], other) for item, other in zip(packs, passed)]
    for step in range(1, seq_bits - 1):
        rest, _ = swap(step)
    rest = jnp.concatenate(rest)
    half_rows = packs[0].shape[1] // 2
    packs = [[item[:, :half_rows], item[:, half_rows:]] for item in packs]
    for step in reversed(range(seq_bits - 1)):
        for pack in packs:
            for side, order in enumerate(orders):
                pack[side], _ = doubled(pack[side], 1, order[step])
    packs = [doubled(jnp.concatenate(pack, axis=1), 1, 0)[0] for pack in packs]
    sums = rest[count : count + 4 * SUM_ROWS]
    rest = jnp.concatenate([rest[:count], rest[count + 4 * SUM_ROWS :]])
    rest = doubled(rest, 0, 0)[0].astype(F32).reshape(2, -1, width)
    grad_w_out = rest[:, count:].reshape(feats, width)
    rest = rest[:, :count]
    more = [crossed(sums[:SUM_ROWS], distance).astype(F32) for distance in range(1, head_count)]
    sums = sums.astype(F32)
    wide = functools.reduce(jnp.add, more, sums[:SUM_ROWS])[:6]
    grad_b_up = sums[SUM_ROWS, :hidden] + more[0][6, :hidden]
    grad_b_qv = jnp.stack([sums[(index + 2) * SUM_ROWS, :feats] for index in range(2)])
    packs = [packs[0][0], packs[0][1]] if hidden == width else [packs[0][0], packs[1][0]]
    grad_w_up, grad_w_down = (item.astype(F32) for item in packs)
    grad_w_qkv = jnp.transpose(rest.reshape(3, feats, width), (2, 0, 1))
    output = in_rows(after(gathered, rest))
    return (
        output, grad_tokens, wide[None, 0:2], wide[None, 2:4], grad_w_qkv[None], grad_b_qv[None],
        grad_w_out[None], wide[4:5], grad_w_up[None], grad_b_up[None], grad_w_down[None], wide[5:6],
    )


def solution(mesh):
    in_specs = (
        P("seq", None), P(), P(), P(), P(None, None, None, "heads"), P(None, None, "heads"),
        P(None, "heads", None), P(), P(None, None, "heads"), P(None, "heads"), P(None, "heads", None), P(),
        P("seq", None),
    )
    out_specs = (
        P("seq", None), P("seq", None), P(), P(), P(None, None, None, "heads"), P(None, None, "heads"),
        P(None, "heads", None), P(), P(None, None, "heads"), P(None, "heads"), P(None, "heads", None), P(),
    )
    return jax.shard_map(shards, mesh=mesh, in_specs=in_specs, out_specs=out_specs, check_vma=False)
```

```python
import functools
import math

import jax
import jax.numpy as jnp
import ml_dtypes
import numpy as np
from jax import lax
from jax.experimental import pallas as pl
from jax.experimental.pallas import tpu as pltpu
from jax.sharding import PartitionSpec as P

HEAD_DIM = 48
BRANCHES = 5
DOCS = 3
TOP = BRANCHES - 1
STRIDE = 2**TOP
LANES = 128
EPSILON = 1e-05
BIG = 2.0**100
SCALE = HEAD_DIM**-0.5
LOG2E = math.log2(math.e)
LN2 = math.log(2.0)
DOC_LANE = HEAD_DIM
MULT_LANE = DOC_LANE + DOCS
LSE_LANE = MULT_LANE + 2 * TOP
VALUE_LANE = LANES // 2
ONE_LANE = VALUE_LANE + HEAD_DIM
F32 = jnp.float32
BF16 = jnp.bfloat16
VMEM_LIMIT = 28 * 1024 * 1024
HEADS_PLACE = DOCS
SEQ_PLACE = DOCS + 1
PART_PLACE = DOCS + 2


class View:
    def __init__(self, shape, index=None, near=False, loose=False):
        self.shape, self.index, self.near, self.loose = tuple(shape), index, near, loose

    def of(self, ref, step, place):
        if not self.near or self.index is None:
            return ref
        cuts = []
        for size, at, whole in zip(self.shape, self.index(step, place), ref.shape):
            cuts.append(pl.ds(0, size) if size == whole else pl.ds(pl.multiple_of(at * size, size), size))
        return ref.at[tuple(cuts)]

    def spec(self):
        if self.near:
            return pl.BlockSpec(memory_space=pltpu.VMEM)
        if self.index is None:
            return pl.BlockSpec(
                self.shape, lambda step, *place: (0,) * len(self.shape), pipeline_mode=pl.Buffered(1)
            )
        return pl.BlockSpec(self.shape, lambda step, *place: self.index(step, place[0] if place else None))


def near(view):
    return View(view.shape, view.index, near=True)


def loose(view):
    return View(view.shape, view.index, loose=True)


def call(kernel, out_shape, grid, in_specs, out_specs, name, scratch_shapes=()):
    single = not isinstance(out_shape, (list, tuple))
    outs = [out_specs] if single else list(out_specs)
    shapes = [out_shape] if single else list(out_shape)
    scalars = int(in_specs[0] is SMALL_SPEC)
    ins = list(in_specs[scalars:])
    views = [*ins, *outs]

    def body(*refs):
        step = pl.program_id(0)
        place = refs[:scalars]
        rest = refs[scalars:]
        shown = [view.of(ref, step, *(place or (None,))) for view, ref in zip(views, rest)]
        kernel(*place, *shown, *rest[len(views) :])

    specs = [item.spec() for item in outs]
    kinds = [
        jax.ShapeDtypeStruct(item.shape, item.dtype) if view.near else pltpu.HBM(item.shape, item.dtype)
        for item, view in zip(shapes, outs)
    ]
    inner = pl.pallas_call(
        body,
        out_shape=kinds[0] if single else kinds,
        grid_spec=pltpu.PrefetchScalarGridSpec(
            num_scalar_prefetch=scalars,
            grid=grid,
            in_specs=[item.spec() for item in ins],
            out_specs=specs[0] if single else specs,
            scratch_shapes=scratch_shapes,
        ),
        compiler_params=pltpu.CompilerParams(vmem_limit_bytes=VMEM_LIMIT),
        name=name,
    )

    def run(*arrays):
        placed = [
            jnp.asarray(item) if view.near or view.loose else pltpu.with_memory_space_constraint(jnp.asarray(item), pltpu.HBM)
            for item, view in zip(arrays[scalars:], ins)
        ]
        return inner(*arrays[:scalars], *placed)

    return run


def bit_reversed(block):
    return sum(((block >> bit) & 1) << (TOP - 1 - bit) for bit in range(TOP))


def level_columns(rows):
    table = np.zeros((rows, LANES), np.float32)
    for level in range(1, TOP + 1):
        table[: rows >> level, MULT_LANE + level - 1] = 1.0
        table[: rows >> level, MULT_LANE + TOP + level - 1] = 1.0
    return table.astype(ml_dtypes.bfloat16)


def count_columns(rows, groups):
    table = np.zeros((groups, rows, LANES), np.float32)
    for group in range(groups):
        for level in range(group + 1, TOP + 1):
            step = math.log2((level - group + 1) / (level - group))
            high = float(np.float32(step).astype(ml_dtypes.bfloat16))
            table[group, : rows >> level, MULT_LANE + level - 1] = high
            table[group, : rows >> level, MULT_LANE + TOP + level - 1] = step - high
    return table.astype(ml_dtypes.bfloat16)


def spread_table(heads, first_lane):
    table = np.zeros((heads * HEAD_DIM, heads * LANES), np.float32)
    for head in range(heads):
        for item in range(HEAD_DIM):
            table[head * HEAD_DIM + item, head * LANES + first_lane + item] = 1.0
    return table.astype(ml_dtypes.bfloat16)


def dot_nn(left, right):
    return jnp.dot(left, right, preferred_element_type=F32)


def dot_nt(left, right):
    return lax.dot_general(left, right, (((1,), (1,)), ((), ())), preferred_element_type=F32)


def dot_tn(left, right):
    return lax.dot_general(left, right, (((0,), (0,)), ((), ())), preferred_element_type=F32)


def norm_rows(values, gain_row, shift_row):
    center = values - jnp.mean(values, axis=-1, keepdims=True)
    spread = jnp.mean(center * center, axis=-1, keepdims=True)
    return center * lax.rsqrt(spread + EPSILON) * gain_row + shift_row


def norm_back(values, gain_row, grad_rows):
    center = values - jnp.mean(values, axis=-1, keepdims=True)
    spread = jnp.mean(center * center, axis=-1, keepdims=True)
    inverse = lax.rsqrt(spread + EPSILON)
    unit = center * inverse
    scaled = grad_rows * gain_row
    grad_in = inverse * (
        scaled
        - jnp.mean(scaled, axis=-1, keepdims=True)
        - unit * jnp.mean(scaled * unit, axis=-1, keepdims=True)
    )
    return grad_in, jnp.sum(grad_rows * unit, axis=0, keepdims=True), jnp.sum(grad_rows, axis=0, keepdims=True)


def full_spec(shape):
    return View(shape)


def head_spec(rows):
    return View((1, rows, LANES), lambda head, place: (head, 0, 0))


SMALL_SPEC = None


def project_kernel(
    first_ref, x_ref, gain_ref, shift_ref, w_ref, bias_ref, level_ref, spread_k_ref, spread_v_ref,
    normed_ref, q_ref, kv_ref, *refs,
):
    *message_refs, q_rows, kv_rows = refs
    step = pl.program_id(0)
    tile = x_ref.shape[0]
    heads, rows = q_rows.shape[0], q_rows.shape[1]
    block = rows // STRIDE
    tiles = rows // tile

    @pl.when(step < tiles)
    def _():
        project_rows(
            step, first_ref, x_ref, gain_ref, shift_ref, w_ref, bias_ref, spread_k_ref, spread_v_ref, normed_ref, q_rows, kv_rows
        )

    @pl.when(step >= tiles)
    def _():
        head = step - tiles
        turn = (first_ref[0] + head) & (STRIDE - 1)
        for item in range(STRIDE):
            start = bit_reversed(item) ^ turn
            there = slice(item * block, (item + 1) * block)
            q_ref[0, there, :] = q_rows[head, pl.ds(start, block, stride=STRIDE), :].astype(BF16)
            pair = (kv_rows[head, pl.ds(start, block, stride=STRIDE), :] + level_ref[there, :].astype(F32)).astype(BF16)
            kv_ref[0, there, :] = pair
            for ref in message_refs:
                if item * block < ref.shape[1]:
                    ref[0, there, :] = pair


def project_rows(
    step, first_ref, x_ref, gain_ref, shift_ref, w_ref, bias_ref, spread_k_ref, spread_v_ref, normed_ref, q_rows, kv_rows
):
    tile = x_ref.shape[0]
    heads = q_rows.shape[0]
    normed = norm_rows(x_ref[...].astype(F32), gain_ref[...], shift_ref[...]).astype(BF16)
    normed_ref[...] = normed
    query = ((dot_nt(normed, w_ref[0]) + bias_ref[0:1]) * (SCALE * LOG2E)).astype(BF16)
    key = dot_nt(normed, w_ref[1]).astype(BF16)
    value = (dot_nt(normed, w_ref[2]) + bias_ref[1:2]).astype(BF16)
    query_wide = dot_nn(query, spread_k_ref[...])
    pair_wide = dot_nn(key, spread_k_ref[...]) + dot_nn(value, spread_v_ref[...])
    here = pl.ds(pl.multiple_of(step * tile, tile), tile)
    row = lax.broadcasted_iota(jnp.int32, (tile, LANES), 0) + step * tile
    lane = lax.broadcasted_iota(jnp.int32, (tile, LANES), 1)
    doc_lane = functools.reduce(
        jnp.add, [(row >= first_ref[1 + item]).astype(jnp.int32) for item in range(DOCS - 1)], DOC_LANE
    )
    query_extra = (lane == doc_lane).astype(F32)
    other = (lane >= DOC_LANE) & (lane < DOC_LANE + DOCS) & (lane != doc_lane)
    ones = ((lane >= LSE_LANE) & (lane < LSE_LANE + 3)) | ((lane >= ONE_LANE) & (lane < ONE_LANE + 3))
    pair_extra = jnp.where(other, -BIG, ones.astype(F32))
    for head in range(heads):
        lanes = slice(head * LANES, (head + 1) * LANES)
        q_rows[head, here, :] = query_wide[:, lanes] + query_extra
        kv_rows[head, here, :] = pair_wide[:, lanes] + pair_extra


def project(first, tokens, gain, shift, weights, bias, bits):
    rows, width = tokens.shape
    feats = weights.shape[1]
    heads = feats // HEAD_DIM
    tile = min(rows, 512)
    tiles = rows // tile
    row_spec = View((tile, width), lambda i, place: (jnp.minimum(i, tiles - 1), 0))
    shape = (heads, rows, LANES)
    messages = [(heads, rows >> (bit + 1), LANES) for bit in range(bits)]
    return call(
        project_kernel,
        grid=(tiles + heads,),
        in_specs=[
            SMALL_SPEC, row_spec, full_spec((1, width)), full_spec((1, width)), full_spec(weights.shape),
            full_spec(bias.shape), full_spec((rows, LANES)),
            full_spec((feats, heads * LANES)), full_spec((feats, heads * LANES)),
        ],
        out_specs=[row_spec]
        + [
            View((1, *item[1:]), lambda i, place: (jnp.maximum(i - tiles, 0), 0, 0)) for item in (shape, shape, *messages)
        ],
        out_shape=[
            jax.ShapeDtypeStruct((rows, width), BF16),
        ]
        + [jax.ShapeDtypeStruct(item, BF16) for item in (shape, shape, *messages)],
        scratch_shapes=[pltpu.VMEM(shape, F32), pltpu.VMEM(shape, F32)],
        name="project",
    )(
        first, tokens, gain, shift, weights, bias, level_columns(rows),
        spread_table(heads, 0), spread_table(heads, VALUE_LANE),
    )


def group_of(distance):
    return distance.bit_length()


def message_layout(rows, bits):
    direct = [1] + list(range(2, 1 << bits, 2)) if bits else []
    layout = [((item, 0, rows >> group_of(item)),) for item in direct]
    passed, offset = [], 0
    for item in direct[1:]:
        passed.append((item + 1, offset, rows >> group_of(item)))
        offset += rows >> group_of(item)
    return tuple(layout + [tuple(passed)]) if passed else tuple(layout)


def far_pieces(layout, refs):
    return [(ref, *entry) for ref, entries in zip(refs, layout) for entry in entries]


def attend_own_kernel(q_ref, kv_ref, count_ref, out_ref):
    rows = q_ref.shape[1]
    tile = min(rows, 512)
    for low in range(0, rows, tile):
        there = slice(low, low + tile)
        scores = dot_nt(q_ref[0, there, :] + count_ref[0, there, :], kv_ref[0])
        peak = jnp.max(scores, axis=-1, keepdims=True)
        total = dot_nn(jnp.exp2(scores - peak).astype(BF16), kv_ref[0])
        lane = lax.broadcasted_iota(jnp.int32, total.shape, 1)
        out_ref[0, there, :] = jnp.where(lane == 0, peak, total)


def attend_own(queries, pairs, counts):
    heads, rows, _ = queries.shape
    return call(
        attend_own_kernel,
        grid=(heads,),
        in_specs=[head_spec(rows), head_spec(rows), full_spec(counts.shape)],
        out_specs=head_spec(rows),
        out_shape=jax.ShapeDtypeStruct((heads, rows, LANES), F32),
        name="attend_own",
    )(queries, pairs, counts)


def attend_far_kernel(layout, first_ref, q_ref, own_ref, count_ref, gather_ref, *refs):
    pieces_all = far_pieces(layout, refs[: len(layout)])
    out_ref, mine_ref, theirs_ref, placed = refs[len(layout) :]
    head = pl.program_id(0)
    rows = q_ref.shape[1]
    block = rows // STRIDE
    turn = (first_ref[0] + head) & (STRIDE - 1)
    counts = [count for _, _, _, count in pieces_all]
    keys = [ref[0, offset : offset + count, :] for ref, _, offset, count in pieces_all]
    scores = [
        dot_nt(q_ref[0, :count, :] + count_ref[group_of(distance) - 1, :count, :], key)
        for key, (_, distance, _, count) in zip(keys, pieces_all)
    ]
    peaks = [jnp.max(item, axis=-1, keepdims=True) for item in scores]
    edges = sorted({0, rows, *counts})
    tiles = list(zip(edges[:-1], edges[1:]))
    own_peaks = [own_ref[0, low:high, 0:1] for low, high in tiles]
    tops = [
        functools.reduce(jnp.maximum, [peak[low:high] for peak, count in zip(peaks, counts) if low < count], own)
        for (low, high), own in zip(tiles, own_peaks)
    ]
    terms = []
    for score, key, count in zip(scores, keys, counts):
        top = [item for item, (low, _) in zip(tops, tiles) if low < count]
        top = top[0] if len(top) == 1 else jnp.concatenate(top, axis=0)
        terms.append(dot_nn(jnp.exp2(score - top).astype(BF16), key))
    for (low, high), own, top in zip(tiles, own_peaks, tops):
        total = own_ref[0, low:high, :]
        near = [term[low:high] for term, count in zip(terms, counts) if low < count]
        if near:
            total = functools.reduce(jnp.add, near, total * jnp.exp2(own - top))
        mass = total[:, ONE_LANE : ONE_LANE + 1]
        result = total * (1.0 / mass)
        lane = lax.broadcasted_iota(jnp.int32, result.shape, 1)
        out_ref[0, low:high, :] = jnp.where(lane == 0, top + jnp.log2(mass), result)
        for offset in range(low, high, block):
            start = bit_reversed(offset // block) ^ turn
            placed[head, pl.ds(start, block, stride=STRIDE), :] = result[offset - low : offset - low + block]

    @pl.when(head == pl.num_programs(0) - 1)
    def _():
        half = rows // 2
        for side, ref in enumerate((mine_ref, theirs_ref)):
            here = pl.ds(pl.multiple_of(((first_ref[HEADS_PLACE] & 1) ^ side) * half, half), half)
            ref[...] = functools.reduce(
                jnp.add,
                [
                    dot_nn(placed[item, here, :].astype(BF16), gather_ref[item * LANES : (item + 1) * LANES])
                    for item in range(placed.shape[0])
                ],
            ).astype(BF16)


def attend_far(first, queries, own, far, layout, counts):
    heads, rows, _ = queries.shape
    feats = heads * HEAD_DIM
    gather = spread_table(heads, VALUE_LANE).T.copy()
    return call(
        functools.partial(attend_far_kernel, layout),
        grid=(heads,),
        in_specs=[SMALL_SPEC, head_spec(rows), head_spec(rows), full_spec(counts.shape), full_spec(gather.shape)]
        + [loose(head_spec(item.shape[1])) for item in far],
        out_specs=[head_spec(rows), full_spec((rows // 2, feats)), full_spec((rows // 2, feats))],
        out_shape=[
            jax.ShapeDtypeStruct((heads, rows, LANES), F32),
            jax.ShapeDtypeStruct((rows // 2, feats), BF16),
            jax.ShapeDtypeStruct((rows // 2, feats), BF16),
        ],
        scratch_shapes=[pltpu.VMEM((heads, rows, LANES), F32)],
        name="attend_far",
    )(first, queries, own, counts, gather, *far)


def three_parts(values):
    high = values.astype(BF16).astype(F32)
    middle = (values - high).astype(BF16).astype(F32)
    return high, middle, values - high - middle


def pair_grads(keys, query, counted, grad):
    prob = jnp.exp2(dot_nt(keys, counted))
    slope = (prob * dot_nt(keys, grad)).astype(BF16)
    return dot_nn(prob.astype(BF16), grad) + dot_nn(slope, query), dot_tn(slope, keys)


def back_far_kernel(layout, pieces, place_ref, q_ref, out_ref, count_ref, spread_ref, *refs):
    grad_refs = refs[:pieces]
    far = far_pieces(layout, refs[pieces : pieces + len(layout)])
    query, grad, dq_ref = refs[pieces + len(layout) : pieces + len(layout) + 3]
    rows_half = q_ref.shape[1] // 2
    *message_refs, wide = refs[pieces + len(layout) + 3 :]
    targets = []
    for index, entries in enumerate(layout):
        passed = index == len(message_refs)
        for _, offset, _ in entries:
            targets.append((message_refs[0], rows_half + offset) if passed else (message_refs[index], 0))
    head = pl.program_id(0)
    rows = q_ref.shape[1]
    block = rows // STRIDE
    part = grad_refs[0].shape[0]
    turn = (place_ref[0] + head) & (STRIDE - 1)

    @pl.when(head == 0)
    def _():
        for index, ref in enumerate(grad_refs):
            start = pl.multiple_of(place_ref[PART_PLACE + index], part)
            for item in range(wide.shape[0]):
                wide[item, pl.ds(start, part), :] = dot_nn(ref[...], spread_ref[:, item * LANES : (item + 1) * LANES])

    for item in range(STRIDE):
        there = slice(item * block, (item + 1) * block)
        start = bit_reversed(item) ^ turn
        rows_grad = wide[head, pl.ds(start, block, stride=STRIDE), :]
        rows_out = out_ref[0, there, :]
        lane = lax.broadcasted_iota(jnp.int32, rows_grad.shape, 1)
        rows_query = q_ref[0, there, :].astype(F32)
        parts = three_parts(jnp.sum(rows_grad * rows_out, axis=-1, keepdims=True))
        for index, value in enumerate(parts):
            rows_grad = jnp.where(lane == ONE_LANE + index, -value, rows_grad)
        for index, value in enumerate(three_parts(rows_out[:, 0:1])):
            rows_query = jnp.where(lane == LSE_LANE + index, -value, rows_query)
        grad[0, there, :] = rows_grad.astype(BF16)
        query[0, there, :] = rows_query.astype(BF16)

    dq_ref[...] = jnp.zeros_like(dq_ref)
    for (ref, distance, offset, count), (dref, doffset) in zip(far, targets):
        counted = query[0, :count, :] + count_ref[group_of(distance) - 1, :count, :]
        step = min(count, 256)
        for low in range(offset, offset + count, step):
            dkv, dq = pair_grads(ref[0, low : low + step, :], query[0, :count, :], counted, grad[0, :count, :])
            there = slice(doffset + low - offset, doffset + low - offset + step)
            dref[0, there, :] = dkv.astype(BF16)
            dq_ref[0, :count, :] += dq


def back_far(places, grads, queries, outs, far, layout, counts):
    heads, rows, _ = queries.shape
    spread = spread_table(heads, VALUE_LANE)
    limit = rows // 2 if layout else rows // STRIDE
    messages = [sum(item[2] for item in entries) for entries in layout]
    if len(messages) > 1:
        messages = [messages[0] + messages[-1]] + messages[1:-1]
    messages = [(heads, count, LANES) for count in messages]
    return call(
        functools.partial(back_far_kernel, layout, len(grads)),
        grid=(heads,),
        in_specs=[SMALL_SPEC, head_spec(rows), head_spec(rows), full_spec(counts.shape), full_spec(spread.shape)]
        + [near(full_spec(item.shape)) for item in grads]
        + [loose(head_spec(item.shape[1])) for item in far],
        out_specs=[head_spec(rows), head_spec(rows), head_spec(limit)] + [head_spec(item[1]) for item in messages],
        out_shape=[
            jax.ShapeDtypeStruct((heads, rows, LANES), BF16),
            jax.ShapeDtypeStruct((heads, rows, LANES), BF16),
            jax.ShapeDtypeStruct((heads, limit, LANES), F32),
        ]
        + [jax.ShapeDtypeStruct(item, BF16) for item in messages],
        scratch_shapes=[pltpu.VMEM((heads, rows, LANES), F32)],
        name="back_far",
    )(places, queries, outs, counts, spread, *grads, *far)


def back_own_kernel(query, grad, kv_ref, count_ref, dq_far_ref, dq_ref, dkv_ref):
    rows = kv_ref.shape[1]
    limit = dq_far_ref.shape[1]
    counted = query[0] + count_ref[0]
    tile = min(rows, 256)
    for low in range(0, rows, tile):
        there = slice(low, low + tile)
        dkv, dq = pair_grads(kv_ref[0, there, :], query[0], counted, grad[0])
        dkv_ref[0, there, :] = dkv
        if low == 0:
            dq_ref[0] = dq
        else:
            dq_ref[0] += dq
    dq_ref[0, :limit, :] += dq_far_ref[0]


def back_own(queries, grads, pairs, counts, dq_far):
    heads, rows, _ = queries.shape
    return call(
        back_own_kernel,
        grid=(heads,),
        in_specs=[head_spec(rows)] * 3 + [full_spec(counts.shape), head_spec(dq_far.shape[1])],
        out_specs=[near(head_spec(rows))] * 2,
        out_shape=[jax.ShapeDtypeStruct((heads, rows, LANES), F32)] * 2,
        name="back_own",
    )(queries, grads, pairs, counts, dq_far)


def collect_kernel(counts, peers, first_ref, dq_ref, dkv_ref, gather_k_ref, gather_v_ref, w_ref, *refs):
    far_refs = refs[: len(counts)]
    *three_refs, term_ref = refs[len(counts) : len(counts) + 4]
    q_rows, kv_rows = refs[-2:]
    head = pl.program_id(0)
    rows = dq_ref.shape[1]
    part = rows // peers
    block = rows // STRIDE
    turn = (first_ref[0] + head) & (STRIDE - 1)
    for item in range(STRIDE):
        there = slice(item * block, (item + 1) * block)
        start = bit_reversed(item) ^ turn
        pair = dkv_ref[0, there, :]
        for ref, count in zip(far_refs, counts):
            if item * block < count:
                pair = pair + ref[0, there, :].astype(F32)
        lane = lax.broadcasted_iota(jnp.int32, pair.shape, 1)
        q_rows[head, pl.ds(start, block, stride=STRIDE), :] = dq_ref[0, there, :] * SCALE
        kv_rows[head, pl.ds(start, block, stride=STRIDE), :] = jnp.where(lane < VALUE_LANE, pair * LN2, pair)

    @pl.when(head == pl.num_programs(0) - 1)
    def _():
        total = [None] * 3
        for item in range(q_rows.shape[0]):
            lanes = slice(item * LANES, (item + 1) * LANES)
            query = q_rows[item].astype(BF16)
            pair = kv_rows[item].astype(BF16)
            terms = (
                dot_nn(query, gather_k_ref[lanes]),
                dot_nn(pair, gather_k_ref[lanes]),
                dot_nn(pair, gather_v_ref[lanes]),
            )
            total = [term if old is None else old + term for old, term in zip(total, terms)]
        for ref, value in zip(three_refs, total):
            ref[...] = value.astype(BF16)
        for peer in range(peers):
            start = (peer & 1) * (rows // 2) + (peer >> 1) * part
            here = slice(start, start + part)
            term_ref[peer * part : (peer + 1) * part, :] = functools.reduce(
                jnp.add, [dot_nn(ref[here, :], w_ref[item]) for item, ref in enumerate(three_refs)]
            ).astype(BF16)


def collect(places, dq, dkv, far, weights, peers):
    heads, rows, _ = dq.shape
    feats, width = weights.shape[1:]
    gather_k = spread_table(heads, 0).T.copy()
    gather_v = spread_table(heads, VALUE_LANE).T.copy()
    return call(
        functools.partial(collect_kernel, [count for _, count in far], peers),
        grid=(heads,),
        in_specs=[
            SMALL_SPEC, near(head_spec(rows)), near(head_spec(rows)), full_spec(gather_k.shape), full_spec(gather_v.shape),
            full_spec(weights.shape),
        ]
        + [near(head_spec(item.shape[1])) for item, _ in far],
        out_specs=[near(full_spec((rows, feats)))] * 3 + [full_spec((rows, width))],
        out_shape=[jax.ShapeDtypeStruct((rows, feats), BF16)] * 3
        + [jax.ShapeDtypeStruct((rows, width), BF16)],
        scratch_shapes=[pltpu.VMEM((heads, rows, LANES), F32), pltpu.VMEM((heads, rows, LANES), F32)],
        name="collect",
    )(places, dq, dkv, gather_k, gather_v, weights, *[item for item, _ in far])


def bring_kernel(*refs):
    count = len(refs) // 2
    for source, target in zip(refs[:count], refs[count:]):
        target[...] = source[...]


def bring(arrays):
    return call(
        bring_kernel,
        grid=(1,),
        in_specs=[loose(full_spec(item.shape)) for item in arrays],
        out_specs=[near(full_spec(item.shape)) for item in arrays],
        out_shape=[jax.ShapeDtypeStruct(item.shape, item.dtype) for item in arrays],
        name="bring",
    )(*arrays)


def pick(core, low, high):
    return jnp.where(core == 0, low, high), jnp.where(core == 0, high, low)


def halves(array):
    half = array.shape[-1] // 2
    return array[:, :half], array[:, half:]


FETCHED = 2
BIAS_ROWS = 16


def fetched_weights(refs, up_shape, down_shape):
    sides = []
    for ref in refs:
        count = up_shape[0] // 2
        down = ref[count : 2 * count].reshape(down_shape[0] // 2, down_shape[1])
        bias = ref[2 * count : 2 * count + 1].astype(F32)
        for index in (1, 2):
            bias = bias + ref[2 * count + index : 2 * count + index + 1].astype(F32)
        sides.append((ref.at[:count], down, bias))
    return sides


def feed_kernel(
    place_ref, tok_ref, cot_ref, w_out_ref, b_out_ref, gain_ref, shift_ref, up_ref, down_ref, bias_ref, *refs,
):
    fetched, refs = refs[:FETCHED], refs[FETCHED:]
    (up_one, down_one, bias_other), (up_two, down_two, _) = fetched_weights(fetched, up_ref.shape, down_ref.shape)
    attn_refs = refs[:-10]
    resid_ref, normed_ref, cot_out_ref, h0_ref, h1_ref, p0_ref, p1_ref, da_ref, out_ref, sums_ref = refs[-10:]
    feats = attn_refs[0].shape[1]
    core = place_ref[SEQ_PLACE] & 1
    resid = tok_ref[...].astype(F32) + b_out_ref[...]
    for index, ref in enumerate(attn_refs):
        here = pl.ds(pl.multiple_of((place_ref[HEADS_PLACE] ^ index) * feats, feats), feats)
        resid = resid + dot_nn(ref[...], w_out_ref[here, :])
    resid_ref[0] = resid
    normed = norm_rows(resid, gain_ref[...], shift_ref[...]).astype(BF16)
    normed_ref[0] = normed
    cot = cot_ref[...]
    cot_out_ref[0] = cot
    normed_pair = pick(core, *halves(normed))
    pres = (
        dot_nn(normed, up_ref[...]) + bias_ref[...],
        dot_nn(normed_pair[0], up_one[...]) + dot_nn(normed_pair[1], up_two[...]) + bias_other,
    )
    acts = (
        dot_nt(cot, down_ref[...]),
        jnp.concatenate(pick(core, dot_nt(cot, down_one[...]), dot_nt(cot, down_two[...])), axis=1),
    )
    grads = []
    for pre, act, h_ref, p_ref in zip(pres, acts, (h0_ref, h1_ref), (p0_ref, p1_ref)):
        share = 0.5 * (1.0 + lax.erf(pre * math.sqrt(0.5)))
        h_ref[0] = (pre * share).astype(BF16)
        slope = share + pre * jnp.exp(-0.5 * pre * pre) * (1.0 / math.sqrt(2.0 * math.pi))
        grads.append((act * slope).astype(BF16))
        p_ref[0] = grads[-1]
    other = pick(core, dot_nt(grads[1], up_one[...]), dot_nt(grads[1], up_two[...]))
    da_ref[0] = (dot_nt(grads[0], up_ref[...]) + jnp.concatenate(other, axis=1)).astype(da_ref.dtype)
    hidden_pair = pick(core, *halves(h1_ref[0]))
    out_ref[0] = (
        dot_nn(h0_ref[0], down_ref[...])
        + dot_nn(hidden_pair[0], down_one[...])
        + dot_nn(hidden_pair[1], down_two[...])
    ).astype(out_ref.dtype)
    ones = jnp.ones((8, cot.shape[0]), BF16)
    sums_ref[0, 0] = dot_nn(ones, grads[0])
    sums_ref[0, 1] = dot_nn(ones, grads[1])


def feed(places, block, piece_cut, steps, kind, tokens, cotangent, w_out, b_out, gain, shift, up, down, bias, fetched, attns):
    rows, width = tokens.shape
    hidden = up.shape[1]
    feats = attns[0].shape[1]
    inner = attns[0].shape[0] // block
    first = steps[0]

    def piece(i, place):
        return ((place[HEADS_PLACE] >> 1) ^ (i + first)) * piece_cut[1] + piece_cut[0]

    def row_block(i, place):
        return ((place[HEADS_PLACE] & 1) * inner + piece(i, place), 0)

    def stacked(columns):
        return View((1, block, columns), lambda i, place: (i, 0, 0))

    constants = (w_out, b_out, gain, shift, up, down, bias)
    outs = [(width, F32), (width, BF16), (width, BF16)] + [(hidden, BF16)] * 4 + [(width, kind)] * 2
    count = len(steps)
    return call(
        feed_kernel,
        grid=(count,),
        in_specs=[SMALL_SPEC]
        + [View((block, width), row_block)] * 2
        + [
            near(full_spec(item.shape)) if item.size >= width * feats else full_spec(item.shape)
            for item in (*constants, *fetched)
        ]
        + [View((block, feats), lambda i, place: (piece(i, place), 0))] * len(attns),
        out_specs=[near(stacked(columns)) for columns, _ in outs]
        + [View((1, 2, 8, hidden), lambda i, place: (i, 0, 0, 0))],
        out_shape=[jax.ShapeDtypeStruct((count, block, columns), dtype) for columns, dtype in outs]
        + [jax.ShapeDtypeStruct((count, 2, 8, hidden), F32)],
        name="feed",
    )(places, tokens, cotangent, *constants, *fetched, *attns)


def outer_kernel(pairs, parts, place_ref, *refs):
    ins, (keep_ref, give_ref) = refs[:-2], refs[-2:]
    step = pl.program_id(0)
    core = place_ref[SEQ_PLACE] & 1
    for index in range(pairs):

        @pl.when(step == index)
        def _():
            total = None
            first = 2 * parts * index
            for left_ref, right_ref in zip(ins[first : first + parts], ins[first + parts : first + 2 * parts]):
                for item in range(left_ref.shape[0]):
                    left = pick(core, *halves(left_ref[item]))
                    terms = [dot_tn(side, right_ref[item]) for side in left]
                    total = terms if total is None else [old + term for old, term in zip(total, terms)]
            keep_ref[0] = total[0].astype(BF16)
            give_ref[0] = total[1].astype(BF16)


def outer_sums(places, pairs):
    lefts = pairs[0][0][0].shape[2] // 2
    rights = pairs[0][1][0].shape[2]
    arrays = [item for pair in pairs for side in pair for item in side]
    spec = View((1, lefts, rights), lambda i, place: (i, 0, 0))
    shape = jax.ShapeDtypeStruct((len(pairs), lefts, rights), BF16)
    return call(
        functools.partial(outer_kernel, len(pairs), len(pairs[0][0])),
        grid=(len(pairs),),
        in_specs=[SMALL_SPEC] + [near(full_spec(item.shape)) for item in arrays],
        out_specs=[spec, near(spec)],
        out_shape=[shape, shape],
        name="outer_sums",
    )(places, *arrays)


def out_grads_kernel(place_ref, low_ref, *refs):
    *attn_refs, keep_ref, give_ref = refs
    half = attn_refs[0].shape[1] // 2
    core = place_ref[SEQ_PLACE] & 1
    bits = len(attn_refs).bit_length() - 1
    for distance, ref in enumerate(attn_refs):
        index = sum(((distance >> bit) & 1) << (bits - 1 - bit) for bit in range(bits))
        product = dot_tn(ref[...], low_ref[...])
        keep, give = pick(core, product[:half], product[half:])
        keep_ref[index] = keep.astype(BF16)
        give_ref[index] = give.astype(BF16)


def out_grads(places, low, attns):
    part, width = low.shape
    feats = attns[0].shape[1]
    shape = (len(attns), feats // 2, width)
    return call(
        out_grads_kernel,
        grid=(1,),
        in_specs=[SMALL_SPEC, near(full_spec((part, width)))]
        + [View((part, feats), lambda i, place: (place[HEADS_PLACE] >> 1, 0))] * len(attns),
        out_specs=[near(full_spec(shape))] * 2,
        out_shape=[jax.ShapeDtypeStruct(shape, BF16)] * 2,
        name="out_grads",
    )(places, low, *attns)


def tail_kernel(normed_ref, tok_ref, w_ref, _, stats_ref, up_ref, *refs):
    *three_refs, out_ref, sums_ref = refs
    rows, width = normed_ref.shape
    feats = three_refs[0].shape[1]
    hidden = up_ref.shape[1]
    for index, ref in enumerate(three_refs):
        out_ref[index * feats : (index + 1) * feats, :] = dot_tn(ref[...], normed_ref[...]).astype(BF16)
    gain = jnp.zeros((1, width), F32)
    shift = jnp.zeros((1, width), F32)
    tile = min(rows, 256)
    for low in range(0, rows, tile):
        here = slice(low, low + tile)
        term = functools.reduce(
            jnp.add, [dot_nn(ref[here, :], w_ref[index]) for index, ref in enumerate(three_refs)]
        )
        center = tok_ref[here, :].astype(F32)
        center = center - jnp.mean(center, axis=-1, keepdims=True)
        unit = center * lax.rsqrt(jnp.mean(center * center, axis=-1, keepdims=True) + EPSILON)
        gain = gain + column_sums(term * unit)
        shift = shift + column_sums(term)
    row = lax.broadcasted_iota(jnp.int32, (SUM_ROWS, width), 0)
    other = up_ref[1:2, :]
    if hidden < width:
        other = jnp.concatenate([other, jnp.zeros((1, width - hidden), F32)], axis=1)
    lines = (gain, stats_ref[0:1], shift, stats_ref[1:2], stats_ref[2:3], stats_ref[3:4], other)
    block = jnp.zeros((SUM_ROWS, width), F32)
    for index, line in enumerate(lines):
        block = jnp.where(row == index, line, block)
    sums_ref[:SUM_ROWS, :] = block.astype(BF16)
    sums_ref[SUM_ROWS:, :] = jnp.zeros((3 * SUM_ROWS, width), BF16)
    ones = jnp.ones((SUM_ROWS, rows), BF16)
    own = jnp.broadcast_to(up_ref[0:1, :], (SUM_ROWS, hidden))
    for index, value in enumerate((own, dot_nn(ones, three_refs[0][...]), dot_nn(ones, three_refs[2][...]))):
        here = (index + 1) * SUM_ROWS
        sums_ref[here : here + SUM_ROWS, : value.shape[1]] = value.astype(BF16)


SUM_ROWS = 16


def tail_grads(normed, tokens, weights, earlier, stats, ups, three):
    rows, width = normed.shape
    feats = three[0].shape[1]
    ins = (normed, tokens, weights, stats, ups, *three)
    specs = [full_spec(item.shape) for item in ins[:5]] + [near(full_spec(item.shape)) for item in three]
    ins = (*ins[:3], earlier, *ins[3:])
    return call(
        tail_kernel,
        grid=(1,),
        in_specs=[*specs[:3], View((1, 16, LANES), lambda step, place: (0, 0, 0)), *specs[3:]],
        out_specs=[near(full_spec((3 * feats, width))), near(full_spec((4 * SUM_ROWS, width)))],
        out_shape=[jax.ShapeDtypeStruct((count, width), BF16) for count in (3 * feats, 4 * SUM_ROWS)],
        name="tail_grads",
    )(*ins)


def pack_kernel(core_ref, up_ref, down_ref, bias_ref, out_ref):
    count = up_ref.shape[0]
    out_ref[:count, :] = up_ref[...]
    out_ref[count : 2 * count, :] = down_ref[...]
    row = lax.broadcasted_iota(jnp.int32, (BIAS_ROWS, bias_ref.shape[1]), 0)
    block = jnp.zeros(row.shape, F32)
    for index, line in enumerate(three_parts(bias_ref[...])):
        block = jnp.where(row == index, line, block)
    out_ref[2 * count :, :] = block.astype(BF16)


def pack_weights(core, up, down, bias):
    hidden = up.shape[1]
    shape = (up.shape[0] + BIAS_ROWS, hidden)
    if up.shape != down.shape:
        cuts = [
            lax.dynamic_slice_in_dim(item, core * (item.shape[0] // 2), item.shape[0] // 2).reshape(-1, hidden)
            for item in (up, down)
        ]
        zeros = jnp.zeros((BIAS_ROWS - 3, hidden), F32)
        return jnp.concatenate([*cuts, jnp.concatenate([*three_parts(bias), zeros]).astype(BF16)])
    return call(
        pack_kernel,
        grid=(1,),
        in_specs=[SMALL_SPEC]
        + [View((up.shape[0] // 2, hidden), lambda i, place: (place[0], 0))] * 2
        + [full_spec(bias.shape)],
        out_specs=full_spec(shape),
        out_shape=jax.ShapeDtypeStruct(shape, BF16),
        name="pack_weights",
    )(core.reshape(1), up, down, bias)


def column_sums(array):
    return jnp.sum(array, axis=0, keepdims=True)


def turn_kernel(received, place_ref, resid_ref, cot_ref, da_ref, w_out_ref, gain_ref, *refs):
    more_refs = refs[:received]
    dres_ref, low_ref, stats_ref, *grad_refs = refs[received:]
    feats = grad_refs[0].shape[1]
    total = da_ref[0]
    block = more_refs[0].shape[0]
    blocks = total.shape[0] // block
    more = [ref[...].astype(F32) for ref in more_refs]
    total = total + jnp.concatenate(
        [functools.reduce(jnp.add, more[index::blocks]) for index in range(blocks)], axis=0
    )
    cot = cot_ref[0].astype(F32)
    grad_n, gain_sum, shift_sum = norm_back(resid_ref[0], gain_ref[...], total)
    dres = cot + grad_n
    dres_ref[...] = dres
    low = dres.astype(BF16)
    low_ref[...] = low
    for index, ref in enumerate(grad_refs):
        here = pl.ds(pl.multiple_of((place_ref[HEADS_PLACE] ^ index) * feats, feats), feats)
        ref[...] = dot_nt(low, w_out_ref[here, :]).astype(BF16)
    stats_ref[0:1] = gain_sum
    stats_ref[1:2] = shift_sum
    stats_ref[2:3] = column_sums(dres)
    stats_ref[3:4] = column_sums(cot)
    stats_ref[4:8] = jnp.zeros_like(stats_ref[4:8])


def turn_back(places, resid, cot, gain, da, more, w_out, peers):
    _, part, width = resid.shape
    feats = width // peers
    ins = (resid, cot, da, w_out, gain)
    return call(
        functools.partial(turn_kernel, len(more)),
        grid=(1,),
        in_specs=[SMALL_SPEC]
        + [near(full_spec(item.shape)) for item in ins[:4]]
        + [full_spec(item.shape) for item in ins[4:]]
        + [near(full_spec(item.shape)) for item in more],
        out_specs=[full_spec((part, width)), near(full_spec((part, width))), full_spec((8, width))]
        + [near(full_spec((part, feats)))] * peers,
        out_shape=[
            jax.ShapeDtypeStruct((part, width), F32),
            jax.ShapeDtypeStruct((part, width), BF16),
            jax.ShapeDtypeStruct((8, width), F32),
        ]
        + [jax.ShapeDtypeStruct((part, feats), BF16)] * peers,
        name="turn_back",
    )(places, *ins, *more)


def finish_kernel(place_ref, tok_ref, gain_ref, term_ref, dres_ref, grad_ref):
    grad_n, _, _ = norm_back(tok_ref[...].astype(F32), gain_ref[...], term_ref[...].astype(F32))
    grad_ref[...] = (dres_ref[...] + grad_n).astype(BF16)


def finish(places, tokens, gain, term, dres):
    part, width = term.shape
    return call(
        finish_kernel,
        grid=(1,),
        in_specs=[SMALL_SPEC, View((part, width), lambda i, place: (place[PART_PLACE] // part, 0))]
        + [full_spec(item.shape) for item in (gain, term, dres)],
        out_specs=full_spec((part, width)),
        out_shape=jax.ShapeDtypeStruct((part, width), BF16),
        name="finish",
    )(places, tokens, gain, term, dres)


def flipped(array, distance):
    return lax.ppermute(array, "seq", [(i, i ^ distance) for i in range(lax.axis_size("seq"))])


def crossed(array, distance):
    if distance == 0:
        return array
    return lax.ppermute(array, "heads", [(i, i ^ distance) for i in range(lax.axis_size("heads"))])


def added(left, right):
    return (left.astype(F32) + right.astype(F32)).astype(BF16)


def halved(array, axis, bit):
    side = (lax.axis_index("seq") >> bit) & 1
    count = array.shape[axis] // 2
    keep = lax.dynamic_slice_in_dim(array, side * count, count, axis)
    give = lax.dynamic_slice_in_dim(array, (1 - side) * count, count, axis)
    other = flipped(give, 1 << bit)
    return added(keep, other), other


def doubled(array, axis, bit):
    side = (lax.axis_index("seq") >> bit) & 1
    other = flipped(array, 1 << bit)
    whole = jnp.where(side == 0, jnp.concatenate([array, other], axis), jnp.concatenate([other, array], axis))
    return whole, other


def after(value, earlier):
    return lax.optimization_barrier((value, earlier))[0]


def shards(tokens, docs, ln_gain, ln_bias, w_qkv, b_qv, w_out, b_out, w_up, b_up, w_down, b_down, cotangent):
    rows, width = tokens.shape
    feats = w_qkv.shape[3]
    heads = feats // HEAD_DIM
    seq_count = lax.axis_size("seq")
    head_count = lax.axis_size("heads")
    seq_pos = lax.axis_index("seq")
    head_pos = lax.axis_index("heads")
    seq_bits = seq_count.bit_length() - 1
    gains, shifts = ln_gain[0], ln_bias[0]
    half = rows // 2
    part = rows // head_count
    peers = [head_pos ^ distance for distance in range(head_count)]
    part_starts = [(peer & 1) * half + (peer >> 1) * part for peer in peers]
    edges = [jnp.sum((docs <= item).astype(jnp.int32)) - seq_pos * rows for item in range(DOCS - 1)]
    places = jnp.stack(
        [item.astype(jnp.int32) for item in (head_pos * heads, *edges, head_pos, seq_pos, *part_starts)]
    )

    core = seq_pos & 1
    hidden = w_up.shape[2]
    w_out_all = lax.all_gather(w_out[0], "heads", axis=0, tiled=True)
    fetched_one = crossed(pack_weights(core.astype(jnp.int32), w_up[0], w_down[0], b_up), 1)

    w_three = jnp.transpose(w_qkv[0], (1, 2, 0))
    bits = min(seq_bits, TOP)
    normed, queries, pairs, *messages = project(places, tokens, gains[0:1], shifts[0:1], w_three, b_qv[0], bits)
    layout = message_layout(rows, bits)
    counts = count_columns(rows, bits + 1)
    own_counts, far_counts = counts[:1], counts[1:, : rows // 2]
    direct = layout[:-1] if bits > 1 else layout
    far = [flipped(messages[group_of(entries[0][0]) - 1], entries[0][0]) for entries in direct]
    own_outs = attend_own(queries, pairs, own_counts)
    if bits > 1:
        far.append(flipped(after(jnp.concatenate(far[1:], axis=1), own_outs), 1))
    outs, attn_mine, attn_theirs = attend_far(places, queries, own_outs, far, layout, far_counts)
    fetched = [fetched_one, flipped(after(fetched_one, outs), 1)]
    attns = [attn_mine] + [
        crossed(attn_theirs if distance & 1 else attn_mine, distance) for distance in range(1, head_count)
    ]

    def in_rows(array):
        return jnp.concatenate([array[2 * inner + side] for side in range(2) for inner in range(head_count // 2)])

    steps = head_count // 2
    w_out_all, up_here, down_here, *fetched = bring([w_out_all, w_up[0], w_down[0], *fetched])
    shared = (
        tokens, cotangent, w_out_all, b_out, gains[1:2], shifts[1:2], up_here, down_here, b_up, fetched, attns,
    )
    cuts = 2
    sent = [feed(places, part // cuts, (index, cuts), range(1, steps), BF16, *shared) for index in range(cuts)]
    da_more = [crossed(item[7][step - 1], 2 * step) for step in range(1, steps) for item in sent]
    own = feed(places, part, (0, 1), range(0, 1), F32, *shared)
    resid, normed_two, cots, h0, h1, p0, p1, da_two, out_term, up_sums = zip(own, *sent)
    dres, dres_low, stats_two, *grad_attns = turn_back(
        places, resid[0], cots[0], gains[1:2], da_two[0], da_more, w_out_all, head_count
    )
    grad_attns = [crossed(item, distance) for distance, item in enumerate(grad_attns)]
    later = after(places, dres)
    out_keep, out_give = out_grads(later, dres_low, attns)
    later = after(later, out_keep)
    products = [(normed_two, p0), (h0, cots), (normed_two, p1), (h1, cots)]
    if hidden == width:
        packs = [outer_sums(later, products)]
    else:
        packs = [outer_sums(later, products[0::2]), outer_sums(later, products[1::2])]
    packs = after(packs, grad_attns)
    out_core = flipped(after(out_give, (grad_attns, packs)), 1)
    out_grad = added(out_keep, out_core)

    out_terms = after(jnp.concatenate(out_term[1:], axis=1), (grad_attns, packs))
    out_more = [crossed(out_terms[step - 1], 2 * step) for step in range(1, steps)]
    queries_b, grads_b, dq_far, *dfar = back_far(
        after(places, packs), grad_attns, queries, outs, far, layout, far_counts
    )
    out_sum = functools.reduce(jnp.add, [item.astype(F32) for item in after(out_more, dq_far)], out_term[0][0])
    out_part = (resid[0][0] + out_sum + b_down[0]).astype(BF16)
    back = []
    if bits:
        arrived = flipped(after(dfar[0], (out_more, out_core)), 1)
        arrived = after(arrived, out_part)
        offset = rows // 2
        onward = []
        for item in dfar[1:]:
            count = item.shape[1]
            onward.append(added(item, arrived[:, offset : offset + count]))
            offset += count
        queries_b = after(queries_b, onward)
        back = [(arrived, rows // 2)] + [
            (flipped(item, entries[0][0]), item.shape[1]) for entries, item in zip(direct[1:], onward)
        ]
    out_other = crossed(after(out_grad, out_part)[steps:], 1)
    out_grad = added(out_grad[:steps], out_other)
    arrived = [flipped(give, 1) for _, give in after(packs, out_part)]
    packs = [(keep, item) for (keep, _), item in zip(packs, arrived)]
    queries_b, out_part = lax.optimization_barrier((queries_b, out_part))
    gathered = lax.all_gather(out_part, "heads", axis=0)
    dq, dkv = back_own(queries_b, grads_b, pairs, own_counts, dq_far)
    ups = functools.reduce(jnp.add, [jnp.sum(item[:, :, 0], axis=0) for item in up_sums])
    *grads_three, terms = collect(after(places, (ups, arrived, out_other)), dq, dkv, back, w_three, head_count)
    term = lax.psum_scatter(terms, "heads", scatter_dimension=0, tiled=True)
    orders = [list(range(1, seq_bits))] * 2
    if seq_bits > 2:
        orders[1] = [2, 1] + orders[0][2:]
    packs = [added(*item) for item in after(packs, terms)]
    count = packs[0].shape[1] // 2
    packs = [[item[:, :count], item[:, count:]] for item in packs]
    arrived = []
    for step in range(seq_bits - 1):
        for pack in packs:
            for side, order in enumerate(orders):
                pack[side], other = halved(pack[side], 1, order[step])
                if not step:
                    arrived.append(other)
    packs = [jnp.concatenate(pack, axis=1) for pack in packs]
    distance = 2
    while distance < head_count:
        count = out_grad.shape[0] // 2
        out_grad = added(out_grad[:count], crossed(out_grad[count:], distance))
        distance = 2 * distance
    grad_w_out = out_grad[0]

    rest, sums = tail_grads(normed, tokens, w_three, gathered, stats_two, ups, grads_three)
    count = rest.shape[0] // 2
    keep, give = (lax.dynamic_slice_in_dim(rest, side * count, count) for side in (core, 1 - core))
    rest = added(jnp.concatenate([keep, sums]), flipped(jnp.concatenate([give, sums]), 1))
    rest = jnp.concatenate([rest, grad_w_out])
    cut = rest.shape[0] // 2
    rest = [rest[:cut], rest[cut:]]

    def swap(step):
        others = [flipped(item, 1 << order[step]) for item, order in zip(rest, orders)]
        return [added(item, other) for item, other in zip(rest, others)], others

    others = []
    if seq_bits > 1:
        rest, others = swap(0)
    output = in_rows(gathered)
    arrived = (packs, others, output)
    grad_part = finish(after(places, arrived), tokens, gains[0:1], term, dres)
    grad_tokens = in_rows(lax.all_gather(grad_part, "heads", axis=0)).astype(F32)
    packs, rest = after((packs, rest), grad_part)
    passed = [crossed(item[item.shape[0] // 2 :], 1) for item in packs]
    packs = [added(item[: item.shape[0] // 2], other) for item, other in zip(packs, passed)]
    for step in range(1, seq_bits - 1):
        rest, _ = swap(step)
    rest = jnp.concatenate(rest)
    half_rows = packs[0].shape[1] // 2
    packs = [[item[:, :half_rows], item[:, half_rows:]] for item in packs]
    for step in reversed(range(seq_bits - 1)):
        for pack in packs:
            for side, order in enumerate(orders):
                pack[side], _ = doubled(pack[side], 1, order[step])
    packs = [doubled(jnp.concatenate(pack, axis=1), 1, 0)[0] for pack in packs]
    sums = rest[count : count + 4 * SUM_ROWS]
    rest = jnp.concatenate([rest[:count], rest[count + 4 * SUM_ROWS :]])
    rest = doubled(rest, 0, 0)[0].astype(F32).reshape(2, -1, width)
    grad_w_out = rest[:, count:].reshape(feats, width)
    rest = rest[:, :count]
    more = [crossed(sums[:SUM_ROWS], distance).astype(F32) for distance in range(1, head_count)]
    sums = sums.astype(F32)
    wide = functools.reduce(jnp.add, more, sums[:SUM_ROWS])[:6]
    grad_b_up = sums[SUM_ROWS, :hidden] + more[0][6, :hidden]
    grad_b_qv = jnp.stack([sums[(index + 2) * SUM_ROWS, :feats] for index in range(2)])
    packs = [packs[0][0], packs[0][1]] if hidden == width else [packs[0][0], packs[1][0]]
    grad_w_up, grad_w_down = (item.astype(F32) for item in packs)
    grad_w_qkv = jnp.transpose(rest.reshape(3, feats, width), (2, 0, 1))
    return (
        output, grad_tokens, wide[None, 0:2], wide[None, 2:4], grad_w_qkv[None], grad_b_qv[None],
        grad_w_out[None], wide[4:5], grad_w_up[None], grad_b_up[None], grad_w_down[None], wide[5:6],
    )


def solution(mesh):
    in_specs = (
        P("seq", None), P(), P(), P(), P(None, None, None, "heads"), P(None, None, "heads"),
        P(None, "heads", None), P(), P(None, None, "heads"), P(None, "heads"), P(None, "heads", None), P(),
        P("seq", None),
    )
    out_specs = (
        P("seq", None), P("seq", None), P(), P(), P(None, None, None, "heads"), P(None, None, "heads"),
        P(None, "heads", None), P(), P(None, None, "heads"), P(None, "heads"), P(None, "heads", None), P(),
    )
    return jax.shard_map(shards, mesh=mesh, in_specs=in_specs, out_specs=out_specs, check_vma=False)
```

```python
import functools
import math

import jax
import jax.numpy as jnp
import ml_dtypes
import numpy as np
from jax import lax
from jax.experimental import pallas as pl
from jax.experimental.pallas import tpu as pltpu
from jax.sharding import PartitionSpec as P

HEAD_DIM = 48
BRANCHES = 5
DOCS = 3
TOP = BRANCHES - 1
STRIDE = 2**TOP
LANES = 128
EPSILON = 1e-05
BIG = 2.0**100
SCALE = HEAD_DIM**-0.5
LOG2E = math.log2(math.e)
LN2 = math.log(2.0)
DOC_LANE = HEAD_DIM
MULT_LANE = DOC_LANE + DOCS
LSE_LANE = MULT_LANE + 2 * TOP
VALUE_LANE = LANES // 2
ONE_LANE = VALUE_LANE + HEAD_DIM
F32 = jnp.float32
BF16 = jnp.bfloat16
VMEM_LIMIT = 28 * 1024 * 1024
HEADS_PLACE = DOCS
SEQ_PLACE = DOCS + 1
PART_PLACE = DOCS + 2


class View:
    def __init__(self, shape, index=None, near=False, loose=False):
        self.shape, self.index, self.near, self.loose = tuple(shape), index, near, loose

    def of(self, ref, step, place):
        if not self.near or self.index is None:
            return ref
        cuts = []
        for size, at, whole in zip(self.shape, self.index(step, place), ref.shape):
            cuts.append(pl.ds(0, size) if size == whole else pl.ds(pl.multiple_of(at * size, size), size))
        return ref.at[tuple(cuts)]

    def spec(self):
        if self.near:
            return pl.BlockSpec(memory_space=pltpu.VMEM)
        if self.index is None:
            return pl.BlockSpec(
                self.shape, lambda step, *place: (0,) * len(self.shape), pipeline_mode=pl.Buffered(1)
            )
        return pl.BlockSpec(self.shape, lambda step, *place: self.index(step, place[0] if place else None))


def near(view):
    return View(view.shape, view.index, near=True)


def loose(view):
    return View(view.shape, view.index, loose=True)


def call(kernel, out_shape, grid, in_specs, out_specs, name, scratch_shapes=()):
    single = not isinstance(out_shape, (list, tuple))
    outs = [out_specs] if single else list(out_specs)
    shapes = [out_shape] if single else list(out_shape)
    scalars = int(in_specs[0] is SMALL_SPEC)
    ins = list(in_specs[scalars:])
    views = [*ins, *outs]

    def body(*refs):
        step = pl.program_id(0)
        place = refs[:scalars]
        rest = refs[scalars:]
        shown = [view.of(ref, step, *(place or (None,))) for view, ref in zip(views, rest)]
        kernel(*place, *shown, *rest[len(views) :])

    specs = [item.spec() for item in outs]
    kinds = [
        jax.ShapeDtypeStruct(item.shape, item.dtype) if view.near else pltpu.HBM(item.shape, item.dtype)
        for item, view in zip(shapes, outs)
    ]
    inner = pl.pallas_call(
        body,
        out_shape=kinds[0] if single else kinds,
        grid_spec=pltpu.PrefetchScalarGridSpec(
            num_scalar_prefetch=scalars,
            grid=grid,
            in_specs=[item.spec() for item in ins],
            out_specs=specs[0] if single else specs,
            scratch_shapes=scratch_shapes,
        ),
        compiler_params=pltpu.CompilerParams(vmem_limit_bytes=VMEM_LIMIT),
        name=name,
    )

    def run(*arrays):
        placed = [
            jnp.asarray(item) if view.near or view.loose else pltpu.with_memory_space_constraint(jnp.asarray(item), pltpu.HBM)
            for item, view in zip(arrays[scalars:], ins)
        ]
        return inner(*arrays[:scalars], *placed)

    return run


def bit_reversed(block):
    return sum(((block >> bit) & 1) << (TOP - 1 - bit) for bit in range(TOP))


def level_columns(rows):
    table = np.zeros((rows, LANES), np.float32)
    for level in range(1, TOP + 1):
        table[: rows >> level, MULT_LANE + level - 1] = 1.0
        table[: rows >> level, MULT_LANE + TOP + level - 1] = 1.0
    return table.astype(ml_dtypes.bfloat16)


def count_columns(rows, groups):
    table = np.zeros((groups, rows, LANES), np.float32)
    for group in range(groups):
        for level in range(group + 1, TOP + 1):
            step = math.log2((level - group + 1) / (level - group))
            high = float(np.float32(step).astype(ml_dtypes.bfloat16))
            table[group, : rows >> level, MULT_LANE + level - 1] = high
            table[group, : rows >> level, MULT_LANE + TOP + level - 1] = step - high
    return table.astype(ml_dtypes.bfloat16)


def spread_table(heads, first_lane):
    table = np.zeros((heads * HEAD_DIM, heads * LANES), np.float32)
    for head in range(heads):
        for item in range(HEAD_DIM):
            table[head * HEAD_DIM + item, head * LANES + first_lane + item] = 1.0
    return table.astype(ml_dtypes.bfloat16)


def dot_nn(left, right):
    return jnp.dot(left, right, preferred_element_type=F32)


def dot_nt(left, right):
    return lax.dot_general(left, right, (((1,), (1,)), ((), ())), preferred_element_type=F32)


def dot_tn(left, right):
    return lax.dot_general(left, right, (((0,), (0,)), ((), ())), preferred_element_type=F32)


def norm_rows(values, gain_row, shift_row):
    center = values - jnp.mean(values, axis=-1, keepdims=True)
    spread = jnp.mean(center * center, axis=-1, keepdims=True)
    return center * lax.rsqrt(spread + EPSILON) * gain_row + shift_row


def norm_back(values, gain_row, grad_rows):
    center = values - jnp.mean(values, axis=-1, keepdims=True)
    spread = jnp.mean(center * center, axis=-1, keepdims=True)
    inverse = lax.rsqrt(spread + EPSILON)
    unit = center * inverse
    scaled = grad_rows * gain_row
    grad_in = inverse * (
        scaled
        - jnp.mean(scaled, axis=-1, keepdims=True)
        - unit * jnp.mean(scaled * unit, axis=-1, keepdims=True)
    )
    return grad_in, jnp.sum(grad_rows * unit, axis=0, keepdims=True), jnp.sum(grad_rows, axis=0, keepdims=True)


def full_spec(shape):
    return View(shape)


def head_spec(rows):
    return View((1, rows, LANES), lambda head, place: (head, 0, 0))


SMALL_SPEC = None


def project_kernel(
    first_ref, x_ref, gain_ref, shift_ref, w_ref, bias_ref, level_ref, spread_k_ref, spread_v_ref,
    normed_ref, q_ref, kv_ref, *refs,
):
    *message_refs, q_rows, kv_rows = refs
    step = pl.program_id(0)
    tile = x_ref.shape[0]
    heads, rows = q_rows.shape[0], q_rows.shape[1]
    block = rows // STRIDE
    tiles = rows // tile

    @pl.when(step < tiles)
    def _():
        project_rows(
            step, first_ref, x_ref, gain_ref, shift_ref, w_ref, bias_ref, spread_k_ref, spread_v_ref, normed_ref, q_rows, kv_rows
        )

    @pl.when(step >= tiles)
    def _():
        head = step - tiles
        turn = (first_ref[0] + head) & (STRIDE - 1)
        for item in range(STRIDE):
            start = bit_reversed(item) ^ turn
            there = slice(item * block, (item + 1) * block)
            q_ref[0, there, :] = q_rows[head, pl.ds(start, block, stride=STRIDE), :].astype(BF16)
            pair = (kv_rows[head, pl.ds(start, block, stride=STRIDE), :] + level_ref[there, :].astype(F32)).astype(BF16)
            kv_ref[0, there, :] = pair
            for ref in message_refs:
                if item * block < ref.shape[1]:
                    ref[0, there, :] = pair


def project_rows(
    step, first_ref, x_ref, gain_ref, shift_ref, w_ref, bias_ref, spread_k_ref, spread_v_ref, normed_ref, q_rows, kv_rows
):
    tile = x_ref.shape[0]
    heads = q_rows.shape[0]
    normed = norm_rows(x_ref[...].astype(F32), gain_ref[...], shift_ref[...]).astype(BF16)
    normed_ref[...] = normed
    query = ((dot_nt(normed, w_ref[0]) + bias_ref[0:1]) * (SCALE * LOG2E)).astype(BF16)
    key = dot_nt(normed, w_ref[1]).astype(BF16)
    value = (dot_nt(normed, w_ref[2]) + bias_ref[1:2]).astype(BF16)
    query_wide = dot_nn(query, spread_k_ref[...])
    pair_wide = dot_nn(key, spread_k_ref[...]) + dot_nn(value, spread_v_ref[...])
    here = pl.ds(pl.multiple_of(step * tile, tile), tile)
    row = lax.broadcasted_iota(jnp.int32, (tile, LANES), 0) + step * tile
    lane = lax.broadcasted_iota(jnp.int32, (tile, LANES), 1)
    doc_lane = functools.reduce(
        jnp.add, [(row >= first_ref[1 + item]).astype(jnp.int32) for item in range(DOCS - 1)], DOC_LANE
    )
    query_extra = (lane == doc_lane).astype(F32)
    other = (lane >= DOC_LANE) & (lane < DOC_LANE + DOCS) & (lane != doc_lane)
    ones = ((lane >= LSE_LANE) & (lane < LSE_LANE + 3)) | ((lane >= ONE_LANE) & (lane < ONE_LANE + 3))
    pair_extra = jnp.where(other, -BIG, ones.astype(F32))
    for head in range(heads):
        lanes = slice(head * LANES, (head + 1) * LANES)
        q_rows[head, here, :] = query_wide[:, lanes] + query_extra
        kv_rows[head, here, :] = pair_wide[:, lanes] + pair_extra


def project(first, tokens, gain, shift, weights, bias, bits):
    rows, width = tokens.shape
    feats = weights.shape[1]
    heads = feats // HEAD_DIM
    tile = min(rows, 512)
    tiles = rows // tile
    row_spec = View((tile, width), lambda i, place: (jnp.minimum(i, tiles - 1), 0))
    shape = (heads, rows, LANES)
    messages = [(heads, rows >> (bit + 1), LANES) for bit in range(bits)]
    return call(
        project_kernel,
        grid=(tiles + heads,),
        in_specs=[
            SMALL_SPEC, row_spec, full_spec((1, width)), full_spec((1, width)), full_spec(weights.shape),
            full_spec(bias.shape), full_spec((rows, LANES)),
            full_spec((feats, heads * LANES)), full_spec((feats, heads * LANES)),
        ],
        out_specs=[row_spec]
        + [
            View((1, *item[1:]), lambda i, place: (jnp.maximum(i - tiles, 0), 0, 0)) for item in (shape, shape, *messages)
        ],
        out_shape=[
            jax.ShapeDtypeStruct((rows, width), BF16),
        ]
        + [jax.ShapeDtypeStruct(item, BF16) for item in (shape, shape, *messages)],
        scratch_shapes=[pltpu.VMEM(shape, F32), pltpu.VMEM(shape, F32)],
        name="project",
    )(
        first, tokens, gain, shift, weights, bias, level_columns(rows),
        spread_table(heads, 0), spread_table(heads, VALUE_LANE),
    )


def group_of(distance):
    return distance.bit_length()


def message_layout(rows, bits):
    direct = [1] + list(range(2, 1 << bits, 2)) if bits else []
    layout = [((item, 0, rows >> group_of(item)),) for item in direct]
    passed, offset = [], 0
    for item in direct[1:]:
        passed.append((item + 1, offset, rows >> group_of(item)))
        offset += rows >> group_of(item)
    return tuple(layout + [tuple(passed)]) if passed else tuple(layout)


def far_pieces(layout, refs):
    return [(ref, *entry) for ref, entries in zip(refs, layout) for entry in entries]


def attend_own_kernel(q_ref, kv_ref, count_ref, out_ref):
    rows = q_ref.shape[1]
    tile = min(rows, 512)
    for low in range(0, rows, tile):
        there = slice(low, low + tile)
        scores = dot_nt(q_ref[0, there, :] + count_ref[0, there, :], kv_ref[0])
        peak = jnp.max(scores, axis=-1, keepdims=True)
        total = dot_nn(jnp.exp2(scores - peak).astype(BF16), kv_ref[0])
        lane = lax.broadcasted_iota(jnp.int32, total.shape, 1)
        out_ref[0, there, :] = jnp.where(lane == 0, peak, total)


def attend_own(queries, pairs, counts):
    heads, rows, _ = queries.shape
    return call(
        attend_own_kernel,
        grid=(heads,),
        in_specs=[head_spec(rows), head_spec(rows), full_spec(counts.shape)],
        out_specs=head_spec(rows),
        out_shape=jax.ShapeDtypeStruct((heads, rows, LANES), F32),
        name="attend_own",
    )(queries, pairs, counts)


def attend_far_kernel(layout, first_ref, q_ref, own_ref, count_ref, gather_ref, *refs):
    pieces_all = far_pieces(layout, refs[: len(layout)])
    out_ref, mine_ref, theirs_ref, placed = refs[len(layout) :]
    head = pl.program_id(0)
    rows = q_ref.shape[1]
    block = rows // STRIDE
    turn = (first_ref[0] + head) & (STRIDE - 1)
    counts = [count for _, _, _, count in pieces_all]
    keys = [ref[0, offset : offset + count, :] for ref, _, offset, count in pieces_all]
    scores = [
        dot_nt(q_ref[0, :count, :] + count_ref[group_of(distance) - 1, :count, :], key)
        for key, (_, distance, _, count) in zip(keys, pieces_all)
    ]
    peaks = [jnp.max(item, axis=-1, keepdims=True) for item in scores]
    edges = sorted({0, rows, *counts})
    tiles = list(zip(edges[:-1], edges[1:]))
    own_peaks = [own_ref[0, low:high, 0:1] for low, high in tiles]
    tops = [
        functools.reduce(jnp.maximum, [peak[low:high] for peak, count in zip(peaks, counts) if low < count], own)
        for (low, high), own in zip(tiles, own_peaks)
    ]
    terms = []
    for score, key, count in zip(scores, keys, counts):
        top = [item for item, (low, _) in zip(tops, tiles) if low < count]
        top = top[0] if len(top) == 1 else jnp.concatenate(top, axis=0)
        terms.append(dot_nn(jnp.exp2(score - top).astype(BF16), key))
    for (low, high), own, top in zip(tiles, own_peaks, tops):
        total = own_ref[0, low:high, :]
        near = [term[low:high] for term, count in zip(terms, counts) if low < count]
        if near:
            total = functools.reduce(jnp.add, near, total * jnp.exp2(own - top))
        mass = total[:, ONE_LANE : ONE_LANE + 1]
        result = total * (1.0 / mass)
        lane = lax.broadcasted_iota(jnp.int32, result.shape, 1)
        out_ref[0, low:high, :] = jnp.where(lane == 0, top + jnp.log2(mass), result)
        for offset in range(low, high, block):
            start = bit_reversed(offset // block) ^ turn
            placed[head, pl.ds(start, block, stride=STRIDE), :] = result[offset - low : offset - low + block]

    @pl.when(head == pl.num_programs(0) - 1)
    def _():
        half = rows // 2
        for side, ref in enumerate((mine_ref, theirs_ref)):
            here = pl.ds(pl.multiple_of(((first_ref[HEADS_PLACE] & 1) ^ side) * half, half), half)
            ref[...] = functools.reduce(
                jnp.add,
                [
                    dot_nn(placed[item, here, :].astype(BF16), gather_ref[item * LANES : (item + 1) * LANES])
                    for item in range(placed.shape[0])
                ],
            ).astype(BF16)


def attend_far(first, queries, own, far, layout, counts):
    heads, rows, _ = queries.shape
    feats = heads * HEAD_DIM
    gather = spread_table(heads, VALUE_LANE).T.copy()
    return call(
        functools.partial(attend_far_kernel, layout),
        grid=(heads,),
        in_specs=[SMALL_SPEC, head_spec(rows), head_spec(rows), full_spec(counts.shape), full_spec(gather.shape)]
        + [loose(head_spec(item.shape[1])) for item in far],
        out_specs=[head_spec(rows), full_spec((rows // 2, feats)), full_spec((rows // 2, feats))],
        out_shape=[
            jax.ShapeDtypeStruct((heads, rows, LANES), F32),
            jax.ShapeDtypeStruct((rows // 2, feats), BF16),
            jax.ShapeDtypeStruct((rows // 2, feats), BF16),
        ],
        scratch_shapes=[pltpu.VMEM((heads, rows, LANES), F32)],
        name="attend_far",
    )(first, queries, own, counts, gather, *far)


def three_parts(values):
    high = values.astype(BF16).astype(F32)
    middle = (values - high).astype(BF16).astype(F32)
    return high, middle, values - high - middle


def pair_grads(keys, query, counted, grad):
    prob = jnp.exp2(dot_nt(keys, counted))
    slope = (prob * dot_nt(keys, grad)).astype(BF16)
    return dot_nn(prob.astype(BF16), grad) + dot_nn(slope, query), dot_tn(slope, keys)


def back_far_kernel(layout, pieces, place_ref, q_ref, out_ref, count_ref, spread_ref, *refs):
    grad_refs = refs[:pieces]
    far = far_pieces(layout, refs[pieces : pieces + len(layout)])
    query, grad, dq_ref = refs[pieces + len(layout) : pieces + len(layout) + 3]
    rows_half = q_ref.shape[1] // 2
    *message_refs, wide = refs[pieces + len(layout) + 3 :]
    targets = []
    for index, entries in enumerate(layout):
        passed = index == len(message_refs)
        for _, offset, _ in entries:
            targets.append((message_refs[0], rows_half + offset) if passed else (message_refs[index], 0))
    head = pl.program_id(0)
    rows = q_ref.shape[1]
    block = rows // STRIDE
    part = grad_refs[0].shape[0]
    turn = (place_ref[0] + head) & (STRIDE - 1)

    @pl.when(head == 0)
    def _():
        for index, ref in enumerate(grad_refs):
            start = pl.multiple_of(place_ref[PART_PLACE + index], part)
            for item in range(wide.shape[0]):
                wide[item, pl.ds(start, part), :] = dot_nn(ref[...], spread_ref[:, item * LANES : (item + 1) * LANES])

    for item in range(STRIDE):
        there = slice(item * block, (item + 1) * block)
        start = bit_reversed(item) ^ turn
        rows_grad = wide[head, pl.ds(start, block, stride=STRIDE), :]
        rows_out = out_ref[0, there, :]
        lane = lax.broadcasted_iota(jnp.int32, rows_grad.shape, 1)
        rows_query = q_ref[0, there, :].astype(F32)
        parts = three_parts(jnp.sum(rows_grad * rows_out, axis=-1, keepdims=True))
        for index, value in enumerate(parts):
            rows_grad = jnp.where(lane == ONE_LANE + index, -value, rows_grad)
        for index, value in enumerate(three_parts(rows_out[:, 0:1])):
            rows_query = jnp.where(lane == LSE_LANE + index, -value, rows_query)
        grad[0, there, :] = rows_grad.astype(BF16)
        query[0, there, :] = rows_query.astype(BF16)

    dq_ref[...] = jnp.zeros_like(dq_ref)
    for (ref, distance, offset, count), (dref, doffset) in zip(far, targets):
        counted = query[0, :count, :] + count_ref[group_of(distance) - 1, :count, :]
        step = min(count, 256)
        for low in range(offset, offset + count, step):
            dkv, dq = pair_grads(ref[0, low : low + step, :], query[0, :count, :], counted, grad[0, :count, :])
            there = slice(doffset + low - offset, doffset + low - offset + step)
            dref[0, there, :] = dkv.astype(BF16)
            dq_ref[0, :count, :] += dq


def back_far(places, grads, queries, outs, far, layout, counts):
    heads, rows, _ = queries.shape
    spread = spread_table(heads, VALUE_LANE)
    limit = rows // 2 if layout else rows // STRIDE
    messages = [sum(item[2] for item in entries) for entries in layout]
    if len(messages) > 1:
        messages = [messages[0] + messages[-1]] + messages[1:-1]
    messages = [(heads, count, LANES) for count in messages]
    return call(
        functools.partial(back_far_kernel, layout, len(grads)),
        grid=(heads,),
        in_specs=[SMALL_SPEC, head_spec(rows), head_spec(rows), full_spec(counts.shape), full_spec(spread.shape)]
        + [near(full_spec(item.shape)) for item in grads]
        + [loose(head_spec(item.shape[1])) for item in far],
        out_specs=[head_spec(rows), head_spec(rows), head_spec(limit)] + [head_spec(item[1]) for item in messages],
        out_shape=[
            jax.ShapeDtypeStruct((heads, rows, LANES), BF16),
            jax.ShapeDtypeStruct((heads, rows, LANES), BF16),
            jax.ShapeDtypeStruct((heads, limit, LANES), F32),
        ]
        + [jax.ShapeDtypeStruct(item, BF16) for item in messages],
        scratch_shapes=[pltpu.VMEM((heads, rows, LANES), F32)],
        name="back_far",
    )(places, queries, outs, counts, spread, *grads, *far)


def back_own_kernel(query, grad, kv_ref, count_ref, dq_far_ref, dq_ref, dkv_ref):
    rows = kv_ref.shape[1]
    limit = dq_far_ref.shape[1]
    counted = query[0] + count_ref[0]
    tile = min(rows, 256)
    for low in range(0, rows, tile):
        there = slice(low, low + tile)
        dkv, dq = pair_grads(kv_ref[0, there, :], query[0], counted, grad[0])
        dkv_ref[0, there, :] = dkv
        if low == 0:
            dq_ref[0] = dq
        else:
            dq_ref[0] += dq
    dq_ref[0, :limit, :] += dq_far_ref[0]


def back_own(queries, grads, pairs, counts, dq_far):
    heads, rows, _ = queries.shape
    return call(
        back_own_kernel,
        grid=(heads,),
        in_specs=[head_spec(rows)] * 3 + [full_spec(counts.shape), head_spec(dq_far.shape[1])],
        out_specs=[near(head_spec(rows))] * 2,
        out_shape=[jax.ShapeDtypeStruct((heads, rows, LANES), F32)] * 2,
        name="back_own",
    )(queries, grads, pairs, counts, dq_far)


def collect_kernel(counts, peers, first_ref, dq_ref, dkv_ref, gather_k_ref, gather_v_ref, w_ref, *refs):
    far_refs = refs[: len(counts)]
    *three_refs, term_ref = refs[len(counts) : len(counts) + 4]
    q_rows, kv_rows = refs[-2:]
    head = pl.program_id(0)
    rows = dq_ref.shape[1]
    part = rows // peers
    block = rows // STRIDE
    turn = (first_ref[0] + head) & (STRIDE - 1)
    for item in range(STRIDE):
        there = slice(item * block, (item + 1) * block)
        start = bit_reversed(item) ^ turn
        pair = dkv_ref[0, there, :]
        for ref, count in zip(far_refs, counts):
            if item * block < count:
                pair = pair + ref[0, there, :].astype(F32)
        lane = lax.broadcasted_iota(jnp.int32, pair.shape, 1)
        q_rows[head, pl.ds(start, block, stride=STRIDE), :] = dq_ref[0, there, :] * SCALE
        kv_rows[head, pl.ds(start, block, stride=STRIDE), :] = jnp.where(lane < VALUE_LANE, pair * LN2, pair)

    @pl.when(head == pl.num_programs(0) - 1)
    def _():
        total = [None] * 3
        for item in range(q_rows.shape[0]):
            lanes = slice(item * LANES, (item + 1) * LANES)
            query = q_rows[item].astype(BF16)
            pair = kv_rows[item].astype(BF16)
            terms = (
                dot_nn(query, gather_k_ref[lanes]),
                dot_nn(pair, gather_k_ref[lanes]),
                dot_nn(pair, gather_v_ref[lanes]),
            )
            total = [term if old is None else old + term for old, term in zip(total, terms)]
        for ref, value in zip(three_refs, total):
            ref[...] = value.astype(BF16)
        for peer in range(peers):
            start = (peer & 1) * (rows // 2) + (peer >> 1) * part
            here = slice(start, start + part)
            term_ref[peer * part : (peer + 1) * part, :] = functools.reduce(
                jnp.add, [dot_nn(ref[here, :], w_ref[item]) for item, ref in enumerate(three_refs)]
            ).astype(BF16)


def collect(places, dq, dkv, far, weights, peers):
    heads, rows, _ = dq.shape
    feats, width = weights.shape[1:]
    gather_k = spread_table(heads, 0).T.copy()
    gather_v = spread_table(heads, VALUE_LANE).T.copy()
    return call(
        functools.partial(collect_kernel, [count for _, count in far], peers),
        grid=(heads,),
        in_specs=[
            SMALL_SPEC, near(head_spec(rows)), near(head_spec(rows)), full_spec(gather_k.shape), full_spec(gather_v.shape),
            full_spec(weights.shape),
        ]
        + [near(head_spec(item.shape[1])) for item, _ in far],
        out_specs=[near(full_spec((rows, feats)))] * 3 + [full_spec((rows, width))],
        out_shape=[jax.ShapeDtypeStruct((rows, feats), BF16)] * 3
        + [jax.ShapeDtypeStruct((rows, width), BF16)],
        scratch_shapes=[pltpu.VMEM((heads, rows, LANES), F32), pltpu.VMEM((heads, rows, LANES), F32)],
        name="collect",
    )(places, dq, dkv, gather_k, gather_v, weights, *[item for item, _ in far])


def bring_kernel(*refs):
    count = len(refs) // 2
    for source, target in zip(refs[:count], refs[count:]):
        target[...] = source[...]


def bring(arrays):
    return call(
        bring_kernel,
        grid=(1,),
        in_specs=[loose(full_spec(item.shape)) for item in arrays],
        out_specs=[near(full_spec(item.shape)) for item in arrays],
        out_shape=[jax.ShapeDtypeStruct(item.shape, item.dtype) for item in arrays],
        name="bring",
    )(*arrays)


def pick(core, low, high):
    return jnp.where(core == 0, low, high), jnp.where(core == 0, high, low)


def halves(array):
    half = array.shape[-1] // 2
    return array[:, :half], array[:, half:]


FETCHED = 2
BIAS_ROWS = 16


def fetched_weights(refs, up_shape, down_shape):
    sides = []
    for ref in refs:
        count = up_shape[0] // 2
        down = ref[count : 2 * count].reshape(down_shape[0] // 2, down_shape[1])
        bias = ref[2 * count : 2 * count + 1].astype(F32)
        for index in (1, 2):
            bias = bias + ref[2 * count + index : 2 * count + index + 1].astype(F32)
        sides.append((ref.at[:count], down, bias))
    return sides


def feed_kernel(
    place_ref, tok_ref, cot_ref, w_out_ref, b_out_ref, gain_ref, shift_ref, up_ref, down_ref, bias_ref, *refs,
):
    fetched, refs = refs[:FETCHED], refs[FETCHED:]
    (up_one, down_one, bias_other), (up_two, down_two, _) = fetched_weights(fetched, up_ref.shape, down_ref.shape)
    attn_refs = refs[:-10]
    resid_ref, normed_ref, cot_out_ref, h0_ref, h1_ref, p0_ref, p1_ref, da_ref, out_ref, sums_ref = refs[-10:]
    feats = attn_refs[0].shape[1]
    core = place_ref[SEQ_PLACE] & 1
    resid = tok_ref[...].astype(F32) + b_out_ref[...]
    for index, ref in enumerate(attn_refs):
        here = pl.ds(pl.multiple_of((place_ref[HEADS_PLACE] ^ index) * feats, feats), feats)
        resid = resid + dot_nn(ref[...], w_out_ref[here, :])
    resid_ref[0] = resid
    normed = norm_rows(resid, gain_ref[...], shift_ref[...]).astype(BF16)
    normed_ref[0] = normed
    cot = cot_ref[...]
    cot_out_ref[0] = cot
    normed_pair = pick(core, *halves(normed))
    pres = (
        dot_nn(normed, up_ref[...]) + bias_ref[...],
        dot_nn(normed_pair[0], up_one[...]) + dot_nn(normed_pair[1], up_two[...]) + bias_other,
    )
    acts = (
        dot_nt(cot, down_ref[...]),
        jnp.concatenate(pick(core, dot_nt(cot, down_one[...]), dot_nt(cot, down_two[...])), axis=1),
    )
    grads = []
    for pre, act, h_ref, p_ref in zip(pres, acts, (h0_ref, h1_ref), (p0_ref, p1_ref)):
        share = 0.5 * (1.0 + lax.erf(pre * math.sqrt(0.5)))
        h_ref[0] = (pre * share).astype(BF16)
        slope = share + pre * jnp.exp(-0.5 * pre * pre) * (1.0 / math.sqrt(2.0 * math.pi))
        grads.append((act * slope).astype(BF16))
        p_ref[0] = grads[-1]
    other = pick(core, dot_nt(grads[1], up_one[...]), dot_nt(grads[1], up_two[...]))
    da_ref[0] = (dot_nt(grads[0], up_ref[...]) + jnp.concatenate(other, axis=1)).astype(da_ref.dtype)
    hidden_pair = pick(core, *halves(h1_ref[0]))
    out_ref[0] = (
        dot_nn(h0_ref[0], down_ref[...])
        + dot_nn(hidden_pair[0], down_one[...])
        + dot_nn(hidden_pair[1], down_two[...])
    ).astype(out_ref.dtype)
    ones = jnp.ones((8, cot.shape[0]), BF16)
    sums_ref[0, 0] = dot_nn(ones, grads[0])
    sums_ref[0, 1] = dot_nn(ones, grads[1])


def feed(places, block, piece_cut, steps, kind, tokens, cotangent, w_out, b_out, gain, shift, up, down, bias, fetched, attns):
    rows, width = tokens.shape
    hidden = up.shape[1]
    feats = attns[0].shape[1]
    inner = attns[0].shape[0] // block
    first = steps[0]

    def piece(i, place):
        return ((place[HEADS_PLACE] >> 1) ^ (i + first)) * piece_cut[1] + piece_cut[0]

    def row_block(i, place):
        return ((place[HEADS_PLACE] & 1) * inner + piece(i, place), 0)

    def stacked(columns):
        return View((1, block, columns), lambda i, place: (i, 0, 0))

    constants = (w_out, b_out, gain, shift, up, down, bias)
    outs = [(width, F32), (width, BF16), (width, BF16)] + [(hidden, BF16)] * 4 + [(width, kind)] * 2
    count = len(steps)
    return call(
        feed_kernel,
        grid=(count,),
        in_specs=[SMALL_SPEC]
        + [View((block, width), row_block)] * 2
        + [
            near(full_spec(item.shape)) if item.size >= width * feats else full_spec(item.shape)
            for item in (*constants, *fetched)
        ]
        + [View((block, feats), lambda i, place: (piece(i, place), 0))] * len(attns),
        out_specs=[near(stacked(columns)) for columns, _ in outs]
        + [View((1, 2, 8, hidden), lambda i, place: (i, 0, 0, 0))],
        out_shape=[jax.ShapeDtypeStruct((count, block, columns), dtype) for columns, dtype in outs]
        + [jax.ShapeDtypeStruct((count, 2, 8, hidden), F32)],
        name="feed",
    )(places, tokens, cotangent, *constants, *fetched, *attns)


def outer_kernel(pairs, parts, place_ref, *refs):
    ins, (keep_ref, give_ref) = refs[:-2], refs[-2:]
    step = pl.program_id(0)
    core = place_ref[SEQ_PLACE] & 1
    for index in range(pairs):

        @pl.when(step == index)
        def _():
            total = None
            first = 2 * parts * index
            for left_ref, right_ref in zip(ins[first : first + parts], ins[first + parts : first + 2 * parts]):
                for item in range(left_ref.shape[0]):
                    left = pick(core, *halves(left_ref[item]))
                    terms = [dot_tn(side, right_ref[item]) for side in left]
                    total = terms if total is None else [old + term for old, term in zip(total, terms)]
            keep_ref[0] = total[0].astype(BF16)
            give_ref[0] = total[1].astype(BF16)


def outer_sums(places, pairs):
    lefts = pairs[0][0][0].shape[2] // 2
    rights = pairs[0][1][0].shape[2]
    arrays = [item for pair in pairs for side in pair for item in side]
    spec = View((1, lefts, rights), lambda i, place: (i, 0, 0))
    shape = jax.ShapeDtypeStruct((len(pairs), lefts, rights), BF16)
    return call(
        functools.partial(outer_kernel, len(pairs), len(pairs[0][0])),
        grid=(len(pairs),),
        in_specs=[SMALL_SPEC] + [near(full_spec(item.shape)) for item in arrays],
        out_specs=[spec, near(spec)],
        out_shape=[shape, shape],
        name="outer_sums",
    )(places, *arrays)


def out_grads_kernel(place_ref, low_ref, *refs):
    *attn_refs, keep_ref, give_ref = refs
    half = attn_refs[0].shape[1] // 2
    core = place_ref[SEQ_PLACE] & 1
    bits = len(attn_refs).bit_length() - 1
    for distance, ref in enumerate(attn_refs):
        index = sum(((distance >> bit) & 1) << (bits - 1 - bit) for bit in range(bits))
        product = dot_tn(ref[...], low_ref[...])
        keep, give = pick(core, product[:half], product[half:])
        keep_ref[index] = keep.astype(BF16)
        give_ref[index] = give.astype(BF16)


def out_grads(places, low, attns):
    part, width = low.shape
    feats = attns[0].shape[1]
    shape = (len(attns), feats // 2, width)
    return call(
        out_grads_kernel,
        grid=(1,),
        in_specs=[SMALL_SPEC, near(full_spec((part, width)))]
        + [View((part, feats), lambda i, place: (place[HEADS_PLACE] >> 1, 0))] * len(attns),
        out_specs=[near(full_spec(shape))] * 2,
        out_shape=[jax.ShapeDtypeStruct(shape, BF16)] * 2,
        name="out_grads",
    )(places, low, *attns)


def tail_kernel(normed_ref, tok_ref, w_ref, _, stats_ref, up_ref, *refs):
    *three_refs, out_ref, sums_ref = refs
    rows, width = normed_ref.shape
    feats = three_refs[0].shape[1]
    hidden = up_ref.shape[1]
    for index, ref in enumerate(three_refs):
        out_ref[index * feats : (index + 1) * feats, :] = dot_tn(ref[...], normed_ref[...]).astype(BF16)
    gain = jnp.zeros((1, width), F32)
    shift = jnp.zeros((1, width), F32)
    tile = min(rows, 256)
    for low in range(0, rows, tile):
        here = slice(low, low + tile)
        term = functools.reduce(
            jnp.add, [dot_nn(ref[here, :], w_ref[index]) for index, ref in enumerate(three_refs)]
        )
        center = tok_ref[here, :].astype(F32)
        center = center - jnp.mean(center, axis=-1, keepdims=True)
        unit = center * lax.rsqrt(jnp.mean(center * center, axis=-1, keepdims=True) + EPSILON)
        gain = gain + column_sums(term * unit)
        shift = shift + column_sums(term)
    row = lax.broadcasted_iota(jnp.int32, (SUM_ROWS, width), 0)
    other = up_ref[1:2, :]
    if hidden < width:
        other = jnp.concatenate([other, jnp.zeros((1, width - hidden), F32)], axis=1)
    lines = (gain, stats_ref[0:1], shift, stats_ref[1:2], stats_ref[2:3], stats_ref[3:4], other)
    block = jnp.zeros((SUM_ROWS, width), F32)
    for index, line in enumerate(lines):
        block = jnp.where(row == index, line, block)
    sums_ref[:SUM_ROWS, :] = block.astype(BF16)
    sums_ref[SUM_ROWS:, :] = jnp.zeros((3 * SUM_ROWS, width), BF16)
    ones = jnp.ones((SUM_ROWS, rows), BF16)
    own = jnp.broadcast_to(up_ref[0:1, :], (SUM_ROWS, hidden))
    for index, value in enumerate((own, dot_nn(ones, three_refs[0][...]), dot_nn(ones, three_refs[2][...]))):
        here = (index + 1) * SUM_ROWS
        sums_ref[here : here + SUM_ROWS, : value.shape[1]] = value.astype(BF16)


SUM_ROWS = 16


def tail_grads(normed, tokens, weights, earlier, stats, ups, three):
    rows, width = normed.shape
    feats = three[0].shape[1]
    ins = (normed, tokens, weights, stats, ups, *three)
    specs = [full_spec(item.shape) for item in ins[:5]] + [near(full_spec(item.shape)) for item in three]
    ins = (*ins[:3], earlier, *ins[3:])
    return call(
        tail_kernel,
        grid=(1,),
        in_specs=[*specs[:3], View((1, 16, LANES), lambda step, place: (0, 0, 0)), *specs[3:]],
        out_specs=[near(full_spec((3 * feats, width))), near(full_spec((4 * SUM_ROWS, width)))],
        out_shape=[jax.ShapeDtypeStruct((count, width), BF16) for count in (3 * feats, 4 * SUM_ROWS)],
        name="tail_grads",
    )(*ins)


def pack_kernel(core_ref, up_ref, down_ref, bias_ref, out_ref):
    count = up_ref.shape[0]
    out_ref[:count, :] = up_ref[...]
    out_ref[count : 2 * count, :] = down_ref[...]
    row = lax.broadcasted_iota(jnp.int32, (BIAS_ROWS, bias_ref.shape[1]), 0)
    block = jnp.zeros(row.shape, F32)
    for index, line in enumerate(three_parts(bias_ref[...])):
        block = jnp.where(row == index, line, block)
    out_ref[2 * count :, :] = block.astype(BF16)


def pack_weights(core, up, down, bias):
    hidden = up.shape[1]
    shape = (up.shape[0] + BIAS_ROWS, hidden)
    if up.shape != down.shape:
        cuts = [
            lax.dynamic_slice_in_dim(item, core * (item.shape[0] // 2), item.shape[0] // 2).reshape(-1, hidden)
            for item in (up, down)
        ]
        zeros = jnp.zeros((BIAS_ROWS - 3, hidden), F32)
        return jnp.concatenate([*cuts, jnp.concatenate([*three_parts(bias), zeros]).astype(BF16)])
    return call(
        pack_kernel,
        grid=(1,),
        in_specs=[SMALL_SPEC]
        + [View((up.shape[0] // 2, hidden), lambda i, place: (place[0], 0))] * 2
        + [full_spec(bias.shape)],
        out_specs=full_spec(shape),
        out_shape=jax.ShapeDtypeStruct(shape, BF16),
        name="pack_weights",
    )(core.reshape(1), up, down, bias)


def column_sums(array):
    return jnp.sum(array, axis=0, keepdims=True)


def turn_kernel(received, place_ref, resid_ref, cot_ref, da_ref, w_out_ref, gain_ref, *refs):
    more_refs = refs[:received]
    dres_ref, low_ref, stats_ref, *grad_refs = refs[received:]
    feats = grad_refs[0].shape[1]
    total = da_ref[0]
    block = more_refs[0].shape[0]
    blocks = total.shape[0] // block
    more = [ref[...].astype(F32) for ref in more_refs]
    total = total + jnp.concatenate(
        [functools.reduce(jnp.add, more[index::blocks]) for index in range(blocks)], axis=0
    )
    cot = cot_ref[0].astype(F32)
    grad_n, gain_sum, shift_sum = norm_back(resid_ref[0], gain_ref[...], total)
    dres = cot + grad_n
    dres_ref[...] = dres
    low = dres.astype(BF16)
    low_ref[...] = low
    for index, ref in enumerate(grad_refs):
        here = pl.ds(pl.multiple_of((place_ref[HEADS_PLACE] ^ index) * feats, feats), feats)
        ref[...] = dot_nt(low, w_out_ref[here, :]).astype(BF16)
    stats_ref[0:1] = gain_sum
    stats_ref[1:2] = shift_sum
    stats_ref[2:3] = column_sums(dres)
    stats_ref[3:4] = column_sums(cot)
    stats_ref[4:8] = jnp.zeros_like(stats_ref[4:8])


def turn_back(places, resid, cot, gain, da, more, w_out, peers):
    _, part, width = resid.shape
    feats = width // peers
    ins = (resid, cot, da, w_out, gain)
    return call(
        functools.partial(turn_kernel, len(more)),
        grid=(1,),
        in_specs=[SMALL_SPEC]
        + [near(full_spec(item.shape)) for item in ins[:4]]
        + [full_spec(item.shape) for item in ins[4:]]
        + [near(full_spec(item.shape)) for item in more],
        out_specs=[near(full_spec((part, width))), near(full_spec((part, width))), near(full_spec((8, width)))]
        + [near(full_spec((part, feats)))] * peers,
        out_shape=[
            jax.ShapeDtypeStruct((part, width), F32),
            jax.ShapeDtypeStruct((part, width), BF16),
            jax.ShapeDtypeStruct((8, width), F32),
        ]
        + [jax.ShapeDtypeStruct((part, feats), BF16)] * peers,
        name="turn_back",
    )(places, *ins, *more)


def finish_kernel(place_ref, tok_ref, gain_ref, term_ref, dres_ref, grad_ref):
    grad_n, _, _ = norm_back(tok_ref[...].astype(F32), gain_ref[...], term_ref[...].astype(F32))
    grad_ref[...] = (dres_ref[...] + grad_n).astype(BF16)


def finish(places, tokens, gain, term, dres):
    part, width = term.shape
    return call(
        finish_kernel,
        grid=(1,),
        in_specs=[SMALL_SPEC, View((part, width), lambda i, place: (place[PART_PLACE] // part, 0))]
        + [full_spec(item.shape) for item in (gain, term, dres)],
        out_specs=full_spec((part, width)),
        out_shape=jax.ShapeDtypeStruct((part, width), BF16),
        name="finish",
    )(places, tokens, gain, term, dres)


def flipped(array, distance):
    return lax.ppermute(array, "seq", [(i, i ^ distance) for i in range(lax.axis_size("seq"))])


def crossed(array, distance):
    if distance == 0:
        return array
    return lax.ppermute(array, "heads", [(i, i ^ distance) for i in range(lax.axis_size("heads"))])


def added(left, right):
    return (left.astype(F32) + right.astype(F32)).astype(BF16)


def halved(array, axis, bit):
    side = (lax.axis_index("seq") >> bit) & 1
    count = array.shape[axis] // 2
    keep = lax.dynamic_slice_in_dim(array, side * count, count, axis)
    give = lax.dynamic_slice_in_dim(array, (1 - side) * count, count, axis)
    other = flipped(give, 1 << bit)
    return added(keep, other), other


def doubled(array, axis, bit):
    side = (lax.axis_index("seq") >> bit) & 1
    other = flipped(array, 1 << bit)
    whole = jnp.where(side == 0, jnp.concatenate([array, other], axis), jnp.concatenate([other, array], axis))
    return whole, other


def after(value, earlier):
    return lax.optimization_barrier((value, earlier))[0]


def shards(tokens, docs, ln_gain, ln_bias, w_qkv, b_qv, w_out, b_out, w_up, b_up, w_down, b_down, cotangent):
    rows, width = tokens.shape
    feats = w_qkv.shape[3]
    heads = feats // HEAD_DIM
    seq_count = lax.axis_size("seq")
    head_count = lax.axis_size("heads")
    seq_pos = lax.axis_index("seq")
    head_pos = lax.axis_index("heads")
    seq_bits = seq_count.bit_length() - 1
    gains, shifts = ln_gain[0], ln_bias[0]
    half = rows // 2
    part = rows // head_count
    peers = [head_pos ^ distance for distance in range(head_count)]
    part_starts = [(peer & 1) * half + (peer >> 1) * part for peer in peers]
    edges = [jnp.sum((docs <= item).astype(jnp.int32)) - seq_pos * rows for item in range(DOCS - 1)]
    places = jnp.stack(
        [item.astype(jnp.int32) for item in (head_pos * heads, *edges, head_pos, seq_pos, *part_starts)]
    )

    core = seq_pos & 1
    hidden = w_up.shape[2]
    w_out_all = lax.all_gather(w_out[0], "heads", axis=0, tiled=True)
    fetched_one = crossed(pack_weights(core.astype(jnp.int32), w_up[0], w_down[0], b_up), 1)

    w_three = jnp.transpose(w_qkv[0], (1, 2, 0))
    bits = min(seq_bits, TOP)
    normed, queries, pairs, *messages = project(places, tokens, gains[0:1], shifts[0:1], w_three, b_qv[0], bits)
    layout = message_layout(rows, bits)
    counts = count_columns(rows, bits + 1)
    own_counts, far_counts = counts[:1], counts[1:, : rows // 2]
    direct = layout[:-1] if bits > 1 else layout
    far = [flipped(messages[group_of(entries[0][0]) - 1], entries[0][0]) for entries in direct]
    own_outs = attend_own(queries, pairs, own_counts)
    if bits > 1:
        far.append(flipped(after(jnp.concatenate(far[1:], axis=1), own_outs), 1))
    outs, attn_mine, attn_theirs = attend_far(places, queries, own_outs, far, layout, far_counts)
    fetched = [fetched_one, flipped(after(fetched_one, outs), 1)]
    attns = [attn_mine] + [
        crossed(attn_theirs if distance & 1 else attn_mine, distance) for distance in range(1, head_count)
    ]

    def in_rows(array):
        return jnp.concatenate([array[2 * inner + side] for side in range(2) for inner in range(head_count // 2)])

    steps = head_count // 2
    w_out_all, up_here, down_here, *fetched = bring([w_out_all, w_up[0], w_down[0], *fetched])
    shared = (
        tokens, cotangent, w_out_all, b_out, gains[1:2], shifts[1:2], up_here, down_here, b_up, fetched, attns,
    )
    cuts = 2
    sent = [feed(places, part // cuts, (index, cuts), range(1, steps), BF16, *shared) for index in range(cuts)]
    da_more = [crossed(item[7][step - 1], 2 * step) for step in range(1, steps) for item in sent]
    own = feed(places, part, (0, 1), range(0, 1), F32, *shared)
    resid, normed_two, cots, h0, h1, p0, p1, da_two, out_term, up_sums = zip(own, *sent)
    dres, dres_low, stats_two, *grad_attns = turn_back(
        places, resid[0], cots[0], gains[1:2], da_two[0], da_more, w_out_all, head_count
    )
    grad_attns = [crossed(item, distance) for distance, item in enumerate(grad_attns)]
    later = after(places, dres)
    out_keep, out_give = out_grads(later, dres_low, attns)
    later = after(later, out_keep)
    products = [(normed_two, p0), (h0, cots), (normed_two, p1), (h1, cots)]
    if hidden == width:
        packs = [outer_sums(later, products)]
    else:
        packs = [outer_sums(later, products[0::2]), outer_sums(later, products[1::2])]
    packs = after(packs, grad_attns)
    out_core = flipped(after(out_give, (grad_attns, packs)), 1)
    out_grad = added(out_keep, out_core)

    out_terms = after(jnp.concatenate(out_term[1:], axis=1), (grad_attns, packs))
    out_more = [crossed(out_terms[step - 1], 2 * step) for step in range(1, steps)]
    queries_b, grads_b, dq_far, *dfar = back_far(
        after(places, packs), grad_attns, queries, outs, far, layout, far_counts
    )
    out_sum = functools.reduce(jnp.add, [item.astype(F32) for item in after(out_more, dq_far)], out_term[0][0])
    out_part = (resid[0][0] + out_sum + b_down[0]).astype(BF16)
    back = []
    if bits:
        arrived = flipped(after(dfar[0], (out_more, out_core)), 1)
        arrived = after(arrived, out_part)
        offset = rows // 2
        onward = []
        for item in dfar[1:]:
            count = item.shape[1]
            onward.append(added(item, arrived[:, offset : offset + count]))
            offset += count
        queries_b = after(queries_b, onward)
        back = [(arrived, rows // 2)] + [
            (flipped(item, entries[0][0]), item.shape[1]) for entries, item in zip(direct[1:], onward)
        ]
    out_other = crossed(after(out_grad, out_part)[steps:], 1)
    out_grad = added(out_grad[:steps], out_other)
    arrived = [flipped(give, 1) for _, give in after(packs, out_part)]
    packs = [(keep, item) for (keep, _), item in zip(packs, arrived)]
    queries_b, out_part = lax.optimization_barrier((queries_b, out_part))
    gathered = lax.all_gather(out_part, "heads", axis=0)
    dq, dkv = back_own(queries_b, grads_b, pairs, own_counts, dq_far)
    ups = functools.reduce(jnp.add, [jnp.sum(item[:, :, 0], axis=0) for item in up_sums])
    *grads_three, terms = collect(after(places, (ups, arrived, out_other)), dq, dkv, back, w_three, head_count)
    term = lax.psum_scatter(terms, "heads", scatter_dimension=0, tiled=True)
    orders = [list(range(1, seq_bits))] * 2
    if seq_bits > 2:
        orders[1] = [2, 1] + orders[0][2:]
    packs = [added(*item) for item in after(packs, terms)]
    count = packs[0].shape[1] // 2
    packs = [[item[:, :count], item[:, count:]] for item in packs]
    arrived = []
    for step in range(seq_bits - 1):
        for pack in packs:
            for side, order in enumerate(orders):
                pack[side], other = halved(pack[side], 1, order[step])
                if not step:
                    arrived.append(other)
    packs = [jnp.concatenate(pack, axis=1) for pack in packs]
    distance = 2
    while distance < head_count:
        count = out_grad.shape[0] // 2
        out_grad = added(out_grad[:count], crossed(out_grad[count:], distance))
        distance = 2 * distance
    grad_w_out = out_grad[0]

    rest, sums = tail_grads(normed, tokens, w_three, gathered, stats_two, ups, grads_three)
    count = rest.shape[0] // 2
    keep, give = (lax.dynamic_slice_in_dim(rest, side * count, count) for side in (core, 1 - core))
    rest = added(jnp.concatenate([keep, sums]), flipped(jnp.concatenate([give, sums]), 1))
    rest = jnp.concatenate([rest, grad_w_out])
    cut = rest.shape[0] // 2
    rest = [rest[:cut], rest[cut:]]

    def swap(step):
        others = [flipped(item, 1 << order[step]) for item, order in zip(rest, orders)]
        return [added(item, other) for item, other in zip(rest, others)], others

    others = []
    if seq_bits > 1:
        rest, others = swap(0)
    output = in_rows(gathered)
    arrived = (packs, others, output)
    grad_part = finish(after(places, arrived), tokens, gains[0:1], term, dres)
    grad_tokens = in_rows(lax.all_gather(grad_part, "heads", axis=0)).astype(F32)
    packs, rest = after((packs, rest), grad_part)
    passed = [crossed(item[item.shape[0] // 2 :], 1) for item in packs]
    packs = [added(item[: item.shape[0] // 2], other) for item, other in zip(packs, passed)]
    for step in range(1, seq_bits - 1):
        rest, _ = swap(step)
    rest = jnp.concatenate(rest)
    half_rows = packs[0].shape[1] // 2
    packs = [[item[:, :half_rows], item[:, half_rows:]] for item in packs]
    for step in reversed(range(seq_bits - 1)):
        for pack in packs:
            for side, order in enumerate(orders):
                pack[side], _ = doubled(pack[side], 1, order[step])
    packs = [doubled(jnp.concatenate(pack, axis=1), 1, 0)[0] for pack in packs]
    sums = rest[count : count + 4 * SUM_ROWS]
    rest = jnp.concatenate([rest[:count], rest[count + 4 * SUM_ROWS :]])
    rest = doubled(rest, 0, 0)[0].astype(F32).reshape(2, -1, width)
    grad_w_out = rest[:, count:].reshape(feats, width)
    rest = rest[:, :count]
    more = [crossed(sums[:SUM_ROWS], distance).astype(F32) for distance in range(1, head_count)]
    sums = sums.astype(F32)
    wide = functools.reduce(jnp.add, more, sums[:SUM_ROWS])[:6]
    grad_b_up = sums[SUM_ROWS, :hidden] + more[0][6, :hidden]
    grad_b_qv = jnp.stack([sums[(index + 2) * SUM_ROWS, :feats] for index in range(2)])
    packs = [packs[0][0], packs[0][1]] if hidden == width else [packs[0][0], packs[1][0]]
    grad_w_up, grad_w_down = (item.astype(F32) for item in packs)
    grad_w_qkv = jnp.transpose(rest.reshape(3, feats, width), (2, 0, 1))
    return (
        output, grad_tokens, wide[None, 0:2], wide[None, 2:4], grad_w_qkv[None], grad_b_qv[None],
        grad_w_out[None], wide[4:5], grad_w_up[None], grad_b_up[None], grad_w_down[None], wide[5:6],
    )


def solution(mesh):
    in_specs = (
        P("seq", None), P(), P(), P(), P(None, None, None, "heads"), P(None, None, "heads"),
        P(None, "heads", None), P(), P(None, None, "heads"), P(None, "heads"), P(None, "heads", None), P(),
        P("seq", None),
    )
    out_specs = (
        P("seq", None), P("seq", None), P(), P(), P(None, None, None, "heads"), P(None, None, "heads"),
        P(None, "heads", None), P(), P(None, None, "heads"), P(None, "heads"), P(None, "heads", None), P(),
    )
    return jax.shard_map(shards, mesh=mesh, in_specs=in_specs, out_specs=out_specs, check_vma=False)
```
